512 devices in a mesh: row: 16 (over z_lo, y), col: 32 (over x, z_hi, core).
Axes of the slice: x: 4, y: 4, z: 16 (z_hi: 4, z_lo: 4; z = z_hi * 4 + z_lo), core: 2. Of those that a mesh axis runs over, the one named last changes fastest.
Arguments:
- tiles: bfloat16 [16, 32, 32, 128, 128], P('row', 'col'), may hold values from -0.5 to 0.5
- tile_slots: int32 [16, 32, 32], P('row', 'col'), may hold values from 0 to 191, as said below
- tile_counts: int32 [16, 32], P('row', 'col'), may hold values from 8 to 32, as said below
- user_degree: int32 [32768], P('row'), may hold values from 1 to 64
- item_degree: int32 [49152], P('col'), may hold values from 1 to 64
- start_panel: float32 [64, 49152], P(None, ('col', 'row')), may hold values from -6 to 6
Outputs:
- left_panel: float32 [64, 32768], P(None, ('row', 'col'))
- right_panel: float32 [64, 49152], P(None, ('col', 'row'))
- left_factors: float32 [3, 64, 64], replicated
- right_factors: float32 [3, 64, 64], replicated
The draws below stay inside these ranges and needn't reach their ends.
Inputs may be any that keep to these rules, and one draw needn't show every extreme that they name: `tile_slots`: within one grid cell the 32 slot numbers are distinct; slot s is local tile row s // 12 and local tile column s % 12; entries from position tile_counts on are padding. `tile_counts`: some grid cell holds 32 live tiles.
All inputs are finite; a program needn't handle non-finite values.
Results may differ from the reference program's by a relative error of at most 0.0005.
Values sent between devices are 32-bit elements; how exact they have to be, the bound alone decides.
No kernel may reach another device: no remote copies, remote signals or barrier semaphores. Data moves between devices by JAX's collectives and lax.ppermute only.
A program may use at most 64 MiB of HBM per device.

```python
import math
import jax
import jax.numpy as jnp
from jax import lax

BLOCK = 64
TILE = 128
STEPS = 3
RB_DEV = 16
CB_DEV = 12
MAXT = 32
GRID_R = 16
GRID_C = 32
USERS = 32768
ITEMS = 49152


def draw_tile_slots(key, part):
    cell_keys = jax.random.split(jax.random.fold_in(key, 3), GRID_R * GRID_C)

    def one_cell(cell_key):
        return jax.random.permutation(cell_key, RB_DEV * CB_DEV)[:MAXT]
    slot_table = jax.vmap(one_cell)(cell_keys).astype(jnp.int32)
    return slot_table.reshape(GRID_R, GRID_C, MAXT)


def draw_tile_counts(key, part):
    base_key = jax.random.fold_in(key, 5)
    counts = jax.random.randint(base_key, (GRID_R * GRID_C,), MAXT // 4, MAXT // 2 + 1)
    chosen_cell = jax.random.randint(jax.random.fold_in(key, 7), (), 0, GRID_R * GRID_C)
    counts = jnp.where(jnp.arange(GRID_R * GRID_C) == chosen_cell, MAXT, counts)
    return counts.astype(jnp.int32).reshape(GRID_R, GRID_C)


def degree_law(key, length):
    positions = jnp.arange(length, dtype=jnp.int32)
    limits = 8 + 57 * positions // length
    return (jax.random.randint(key, (length,), 0, limits) + 1).astype(jnp.int32)


def draw_user_degree(key, part):
    return degree_law(jax.random.fold_in(key, 11), USERS)


def draw_item_degree(key, part):
    return degree_law(jax.random.fold_in(key, 13), ITEMS)


def block_scale(key, dims, shards, least, largest):
    factor_of = 1.0
    for axis_at, blocks in shards:
        heights = jax.random.uniform(jax.random.fold_in(jax.random.fold_in(key, 6), axis_at), (blocks,), jnp.float32, least / len(shards), largest / len(shards))
        factor_of = factor_of * jnp.repeat(jnp.exp(heights), dims[axis_at] // blocks).reshape((-1,) + (1,) * (len(dims) - 1 - axis_at))
    return factor_of


def gaussian(rng, dims, scale, most, shards=(), kind=jnp.bfloat16):
    loudness = block_scale(rng, dims, shards, -0.22, 0.18) if shards else 1.0
    drawn = jax.random.normal(rng, dims, jnp.float32) * scale * loudness
    return jnp.minimum(jnp.maximum(drawn, -most), most).astype(kind)


def setup_inputs(seed: int = 0) -> dict:
    keys = jax.random.split(jax.random.key(seed), 7)
    tiles = gaussian(keys[0], (GRID_R, GRID_C, MAXT, TILE, TILE), 0.08, 0.5, ((0, 16), (1, 32)))
    tile_slots = draw_tile_slots(jax.random.fold_in(keys[6], 71), 0)
    tile_counts = draw_tile_counts(jax.random.fold_in(keys[6], 71), 0)
    user_degree = draw_user_degree(jax.random.fold_in(keys[6], 71), 0)
    item_degree = draw_item_degree(jax.random.fold_in(keys[6], 71), 0)
    start_panel = gaussian(keys[5], (BLOCK, ITEMS), 1.0, 6.0, ((1, 512),), jnp.float32)
    return {"tiles": tiles, "tile_slots": tile_slots, "tile_counts": tile_counts, "user_degree": user_degree, "item_degree": item_degree, "start_panel": start_panel}


HIGH = lax.Precision.HIGHEST

def orthonormal(vectors):
    gram_matrix = jnp.einsum('bn,cn->bc', vectors, vectors, precision=HIGH)
    factor = jnp.linalg.cholesky(gram_matrix)
    return (factor, lax.linalg.triangular_solve(factor, vectors, left_side=True, lower=True))

def grid_tables(tiles, tile_slots, tile_counts):
    grid_tiles = tiles.reshape(GRID_R, GRID_C * MAXT, TILE, TILE)
    grid_slots = tile_slots.reshape(GRID_R, GRID_C * MAXT).astype(jnp.int32)
    counts_rows = jnp.repeat(tile_counts.astype(jnp.int32), MAXT, axis=1)
    positions = jnp.arange(GRID_C * MAXT, dtype=jnp.int32)
    return (grid_tiles, grid_slots, counts_rows, positions)

def forward_product(tiles, tile_slots, tile_counts, vectors):
    grid_tiles, grid_slots, counts_rows, positions = grid_tables(tiles, tile_slots, tile_counts)
    column_owner = positions // MAXT
    panel_blocks = vectors.reshape(BLOCK, GRID_C * CB_DEV, TILE)

    def visit(grid_row, summed):
        grid_row = jnp.asarray(grid_row).astype(jnp.int32)
        tile_rows = lax.dynamic_index_in_dim(grid_tiles, grid_row, 0, keepdims=False).astype(jnp.float32)
        slot_row = lax.dynamic_index_in_dim(grid_slots, grid_row, 0, keepdims=False)
        count_row = lax.dynamic_index_in_dim(counts_rows, grid_row, 0, keepdims=False)
        live_mask = (positions % MAXT < count_row).astype(jnp.float32)
        item_index = (column_owner * CB_DEV + slot_row % CB_DEV).astype(jnp.int32)
        user_index = (grid_row * RB_DEV + slot_row // CB_DEV).astype(jnp.int32)
        chosen = panel_blocks[:, item_index, :].astype(jnp.float32)
        partial_value = jnp.einsum('mrc,bmc->bmr', tile_rows, chosen, precision=HIGH) * live_mask[None, :, None]
        return summed.at[:, user_index, :].add(partial_value)
    summed = lax.fori_loop(0, GRID_R, visit, jnp.zeros((BLOCK, GRID_R * RB_DEV, TILE), jnp.float32))
    return summed.reshape(BLOCK, USERS)

def backward_product(tiles, tile_slots, tile_counts, vectors):
    grid_tiles, grid_slots, counts_rows, positions = grid_tables(tiles, tile_slots, tile_counts)
    column_owner = positions // MAXT
    panel_blocks = vectors.reshape(BLOCK, GRID_R * RB_DEV, TILE)

    def visit(grid_row, summed):
        grid_row = jnp.asarray(grid_row).astype(jnp.int32)
        tile_rows = lax.dynamic_index_in_dim(grid_tiles, grid_row, 0, keepdims=False).astype(jnp.float32)
        slot_row = lax.dynamic_index_in_dim(grid_slots, grid_row, 0, keepdims=False)
        count_row = lax.dynamic_index_in_dim(counts_rows, grid_row, 0, keepdims=False)
        live_mask = (positions % MAXT < count_row).astype(jnp.float32)
        item_index = (column_owner * CB_DEV + slot_row % CB_DEV).astype(jnp.int32)
        user_index = (grid_row * RB_DEV + slot_row // CB_DEV).astype(jnp.int32)
        chosen = panel_blocks[:, user_index, :].astype(jnp.float32)
        partial_value = jnp.einsum('mrc,bmr->bmc', tile_rows, chosen, precision=HIGH) * live_mask[None, :, None]
        return summed.at[:, item_index, :].add(partial_value)
    summed = lax.fori_loop(0, GRID_R, visit, jnp.zeros((BLOCK, GRID_C * CB_DEV, TILE), jnp.float32))
    return summed.reshape(BLOCK, ITEMS)

def reference(tiles, tile_slots, tile_counts, user_degree, item_degree, start_panel):
    user_scale = lax.rsqrt(user_degree.astype(jnp.float32))
    item_scale = lax.rsqrt(item_degree.astype(jnp.float32))
    start_factor, item_basis = orthonormal(start_panel)
    user_basis = start_panel[:, :0]
    item_factor = start_factor
    user_list = []
    item_list = []
    for iteration in range(STEPS):
        scaled = item_basis * item_scale[None, :]
        forward = forward_product(tiles, tile_slots, tile_counts, scaled) * user_scale[None, :]
        if iteration > 0:
            forward = forward - jnp.dot(item_factor.T, user_basis, precision=HIGH)
        user_factor, user_basis = orthonormal(forward)
        scaled = user_basis * user_scale[None, :]
        backward = backward_product(tiles, tile_slots, tile_counts, scaled) * item_scale[None, :]
        backward = backward - jnp.dot(user_factor.T, item_basis, precision=HIGH)
        item_factor, item_basis = orthonormal(backward)
        user_list.append(user_factor)
        item_list.append(item_factor)
    return (math.sqrt(USERS) * user_basis, math.sqrt(ITEMS) * item_basis, jnp.stack(user_list), jnp.stack(item_list))
```

```python
import functools
import math

import jax
import jax.numpy as jnp
from jax import lax
from jax.experimental import pallas as pl
from jax.experimental.pallas import tpu as pltpu
from jax.sharding import Mesh
from jax.sharding import PartitionSpec as P

STEPS = 3
TILE = 128
BLOCK = 64
HIGH = lax.Precision.HIGHEST

ROW = ("zl", "y")
COL = ("x", "zh", "core")
NEAR = ("x", "core")


def factor_rows(gram_ref, out_ref):
    gram = gram_ref[:, :BLOCK]
    eye = (
        lax.broadcasted_iota(jnp.int32, (BLOCK, BLOCK), 0)
        == lax.broadcasted_iota(jnp.int32, (BLOCK, BLOCK), 1)
    ).astype(jnp.float32)
    whole = jnp.concatenate([gram, eye], axis=1)
    groups = [whole[8 * i : 8 * i + 8] for i in range(BLOCK // 8)]
    for j in range(BLOCK):
        first = j // 8
        k = j % 8
        row = groups[first][k : k + 1]
        root = lax.rsqrt(row[:, j : j + 1])
        scaled = row * root
        out_ref[j : j + 1, :] = scaled
        for i in range(first, BLOCK // 8):
            groups[i] = groups[i] - (groups[i][:, j : j + 1] * root) * scaled


def split_three(value):
    high = value.astype(jnp.bfloat16)
    rest = value - high.astype(jnp.float32)
    middle = rest.astype(jnp.bfloat16)
    low = (rest - middle.astype(jnp.float32)).astype(jnp.bfloat16)
    return jnp.concatenate([high, middle, low], axis=0)


def product(slots_ref, count_ref, tiles_ref, parts_ref, sent_ref, forward, cb):
    count = count_ref[0]
    group = 4

    def visit(step, carry):
        added = []
        for g in range(group):
            t = step * group + g
            slot = slots_ref[t]
            local_row = slot // cb
            local_col = slot - local_row * cb
            source, target = (
                (local_col, local_row) if forward else (local_row, local_col)
            )
            tile = tiles_ref[t]
            tile = jnp.where(t < count, tile, jnp.zeros_like(tile))
            parts = parts_ref[pl.ds(pl.multiple_of(source * 192, 64), 192), :]
            dims = (((1,), (1 if forward else 0,)), ((), ()))
            value = lax.dot_general(
                parts, tile, dims, preferred_element_type=jnp.float32
            )
            added.append((target, value[:64] + value[64:128] + value[128:]))
        for target, value in added:
            where = pl.ds(pl.multiple_of(target * 64, 64), 64)
            sent_ref[where, :] += value
        return carry

    lax.fori_loop(0, (count + group - 1) // group, visit, 0)


def send_panel(
    slots_ref, count_ref, tiles_ref, panel_ref, scale_ref, parts_ref, sent_ref, *,
    forward, cb, blocks, targets,
):
    sent_ref[...] = jnp.zeros_like(sent_ref)
    gram = jnp.zeros((BLOCK, BLOCK), jnp.float32)
    for b in range(blocks):
        value = panel_ref[64 * b : 64 * b + 64, :]
        gram += lax.dot_general(
            value, value, (((1,), (1,)), ((), ())), precision=HIGH,
            preferred_element_type=jnp.float32,
        )
        parts_ref[192 * b : 192 * b + 192, :] = split_three(
            value * scale_ref[b : b + 1, :]
        )
    product(slots_ref, count_ref, tiles_ref, parts_ref, sent_ref, forward, cb)
    sent_ref[64 * targets : 64 * targets + 64, :BLOCK] = gram


def start_kernel(
    slots_ref, count_ref, tiles_ref, panel_ref, scale_ref, sent_ref, parts_ref, *, blocks, targets, cb
):
    send_panel(
        slots_ref, count_ref, tiles_ref, panel_ref, scale_ref, parts_ref, sent_ref,
        forward=True, cb=cb, blocks=blocks, targets=targets,
    )


def mix(got_ref, old_ref, old_factor_ref, scale_ref, panel_ref, factor_ref, blocks):
    factor_rows(got_ref.at[64 * blocks : 64 * blocks + 64, :], factor_ref)
    inverse = factor_ref[:, BLOCK:]
    if old_ref is not None:
        upper_mask = lax.broadcasted_iota(
            jnp.int32, (BLOCK, BLOCK), 0
        ) <= lax.broadcasted_iota(jnp.int32, (BLOCK, BLOCK), 1)
        upper = jnp.where(upper_mask, factor_ref[:, :BLOCK], 0.0)
        back = jnp.dot(
            upper, old_factor_ref[:, BLOCK:], precision=HIGH,
            preferred_element_type=jnp.float32,
        )
        weights = jnp.concatenate([inverse, -back], axis=1)
    else:
        weights = inverse
    for b in range(blocks):
        value = got_ref[64 * b : 64 * b + 64, :] * scale_ref[b : b + 1, :]
        if old_ref is not None:
            value = jnp.concatenate([value, old_ref[64 * b : 64 * b + 64, :]], axis=0)
        panel_ref[64 * b : 64 * b + 64, :] = jnp.dot(
            weights, value, precision=HIGH, preferred_element_type=jnp.float32
        )


def step_kernel(*refs, forward, cb, blocks, targets, with_old, last):
    refs = list(refs)
    if not last:
        slots_ref, count_ref, tiles_ref = refs[:3]
        refs = refs[3:]
    got_ref, scale_ref = refs[:2]
    refs = refs[2:]
    old_ref = old_factor_ref = None
    if with_old:
        old_ref, old_factor_ref = refs[:2]
        refs = refs[2:]
    panel_ref, factor_ref, sent_ref = refs[:3]
    mix(got_ref, old_ref, old_factor_ref, scale_ref, panel_ref, factor_ref, blocks)
    if last:
        gram = jnp.zeros((BLOCK, BLOCK), jnp.float32)
        for b in range(blocks):
            value = panel_ref[64 * b : 64 * b + 64, :]
            gram += lax.dot_general(
                value, value, (((1,), (1,)), ((), ())), precision=HIGH,
                preferred_element_type=jnp.float32,
            )
        sent_ref[...] = jnp.concatenate([gram, jnp.zeros_like(gram)], axis=1)
    else:
        send_panel(
            slots_ref, count_ref, tiles_ref, panel_ref, scale_ref, refs[3], sent_ref,
            forward=forward, cb=cb, blocks=blocks, targets=targets,
        )


def end_kernel(gram_ref, right_ref, left_ref, left_factor_ref, out_right_ref, out_left_ref, factor_ref, *, left_size, right_size):
    factor_rows(gram_ref, factor_ref)
    out_right_ref[...] = math.sqrt(right_size) * jnp.dot(
        factor_ref[:, BLOCK:], right_ref[...], precision=HIGH,
        preferred_element_type=jnp.float32,
    )
    out_left_ref[...] = math.sqrt(left_size) * jnp.dot(
        left_factor_ref[:, BLOCK:], left_ref[...], precision=HIGH,
        preferred_element_type=jnp.float32,
    )


SMEM = pl.BlockSpec(memory_space=pltpu.SMEM)
VMEM = pl.BlockSpec(memory_space=pltpu.VMEM)
PARAMS = pltpu.CompilerParams(vmem_limit_bytes=32 * 1024 * 1024)


def f32(*shape):
    return jax.ShapeDtypeStruct(shape, jnp.float32)


def gather_whole(value, axes, count):
    copies = jnp.broadcast_to(value[None], (count,) + value.shape)
    return lax.all_to_all(copies, axes, 0, 0, tiled=True)


def sum_col(sent):
    near = lax.axis_size(NEAR)
    rows = sent.shape[0] // near
    own = jnp.sum(
        lax.all_to_all(sent.reshape(near, rows, TILE), NEAR, 0, 0, tiled=True), axis=0
    )
    own = jnp.sum(lax.all_gather(own, "zh", axis=0, tiled=False), axis=0)
    return gather_whole(own, NEAR, near).reshape(sent.shape)


def sum_row(sent):
    count = lax.axis_size(ROW)
    rows = sent.shape[0] // count
    own = jnp.sum(
        lax.all_to_all(sent.reshape(count, rows, TILE), ROW, 0, 0, tiled=True), axis=0
    )
    return gather_whole(own, ROW, count).reshape(sent.shape)


def per_device(tiles, tile_slots, tile_counts, user_degree, item_degree, start_panel):
    tile_stack = tiles[0, 0]
    slots = tile_slots[0, 0]
    count = tile_counts[0]
    rb = user_degree.shape[0] // TILE
    cb = item_degree.shape[0] // TILE
    rows = lax.axis_size(ROW)
    cols = lax.axis_size(COL)
    user_rows = BLOCK * (rb + 1)
    item_rows = -(-BLOCK * (cb + 1) // (8 * rows)) * (8 * rows)
    user_scale = lax.rsqrt(user_degree.astype(jnp.float32)).reshape(rb, TILE)
    item_scale = lax.rsqrt(item_degree.astype(jnp.float32)).reshape(cb, TILE)

    start = gather_whole(start_panel, ROW, rows)
    start = jnp.transpose(start, (1, 0, 2)).reshape(BLOCK, cb, TILE)
    start = jnp.transpose(start, (1, 0, 2)).reshape(cb * BLOCK, TILE)

    sent = pl.pallas_call(
        functools.partial(start_kernel, blocks=cb, targets=rb, cb=cb),
        out_shape=f32(user_rows, TILE),
        in_specs=[SMEM, SMEM, VMEM, VMEM, VMEM],
        out_specs=VMEM,
        scratch_shapes=[pltpu.VMEM((cb * 192, TILE), jnp.bfloat16)],
        compiler_params=PARAMS,
        name="start",
    )(slots, count, tile_stack, start, item_scale)

    panels = [start]
    factors = []
    for half in range(1, 2 * STEPS + 1):
        users = half % 2 == 1
        last = half == 2 * STEPS
        got = sum_col(sent) if users else sum_row(sent)
        blocks, targets = (rb, cb) if users else (cb, rb)
        sent_rows = item_rows if users else user_rows
        with_old = half > 1
        operands = [] if last else [slots, count, tile_stack]
        specs = [] if last else [SMEM, SMEM, VMEM]
        operands += [got, user_scale if users else item_scale]
        specs += [VMEM, VMEM]
        if with_old:
            operands += [panels[half - 2], factors[half - 2]]
            specs += [VMEM, VMEM]
        panel, factor, sent = pl.pallas_call(
            functools.partial(
                step_kernel, forward=not users, cb=cb, blocks=blocks, targets=targets,
                with_old=with_old, last=last,
            ),
            out_shape=[
                f32(blocks * BLOCK, TILE),
                f32(BLOCK, 2 * BLOCK),
                f32(BLOCK, TILE) if last else f32(sent_rows, TILE),
            ],
            in_specs=specs,
            out_specs=[VMEM, VMEM, VMEM],
            scratch_shapes=[]
            if last
            else [pltpu.VMEM((blocks * 192, TILE), jnp.bfloat16)],
            compiler_params=PARAMS,
            name=f"half{half}",
        )(*operands)
        panels.append(panel)
        factors.append(factor)

    gram = jnp.sum(gather_whole(sent, NEAR, lax.axis_size(NEAR)), axis=0)
    gram = jnp.sum(lax.all_gather(gram, "zh", axis=0, tiled=False), axis=0)

    user_group = rb * TILE // cols
    item_group = cb * TILE // rows
    left = jnp.transpose(panels[-2].reshape(rb, BLOCK, TILE), (1, 0, 2))
    left = lax.dynamic_slice_in_dim(
        left.reshape(BLOCK, rb * TILE), lax.axis_index(COL) * user_group, user_group, 1
    )
    right = jnp.transpose(panels[-1].reshape(cb, BLOCK, TILE), (1, 0, 2))
    right = lax.dynamic_slice_in_dim(
        right.reshape(BLOCK, cb * TILE), lax.axis_index(ROW) * item_group, item_group, 1
    )
    right_panel, left_panel, factor = pl.pallas_call(
        functools.partial(
            end_kernel, left_size=rb * TILE * rows, right_size=cb * TILE * cols
        ),
        out_shape=[
            f32(BLOCK, item_group),
            f32(BLOCK, user_group),
            f32(BLOCK, 2 * BLOCK),
        ],
        in_specs=[VMEM] * 4,
        out_specs=[VMEM] * 3,
        compiler_params=PARAMS,
        name="end",
    )(gram, right, left, factors[-1])
    factors.append(factor)
    lower = [jnp.tril(jnp.transpose(f[:, :BLOCK])) for f in factors]
    return (
        left_panel,
        right_panel,
        jnp.stack(lower[1::2]),
        jnp.stack(lower[2::2]),
    )


def solution(mesh):
    split = Mesh(mesh.devices.reshape(4, 4, 4, 4, 2), ROW + COL)
    in_specs = (
        P(ROW, COL, None, None, None),
        P(ROW, COL, None),
        P(ROW, COL),
        P(ROW),
        P(COL),
        P(None, COL + ROW),
    )
    out_specs = (P(None, ROW + COL), P(None, COL + ROW), P(), P())
    return jax.shard_map(
        per_device, mesh=split, in_specs=in_specs, out_specs=out_specs, check_vma=False
    )
```

```python
import functools
import math

import jax
import jax.numpy as jnp
from jax import lax
from jax.experimental import pallas as pl
from jax.experimental.pallas import tpu as pltpu
from jax.sharding import Mesh
from jax.sharding import PartitionSpec as P

STEPS = 3
TILE = 128
BLOCK = 64
GRAM_ROWS = 24
HIGH = lax.Precision.HIGHEST

ROW = ("zl", "y")
COL = ("x", "zh", "core")
NEAR = ("x", "core")


def pack_gram(gram):
    half = BLOCK // 2

    def rows(block):
        return jnp.concatenate([block[8 * i : 8 * i + 8] for i in range(4)], axis=1)

    return jnp.concatenate(
        [
            rows(gram[:half, :half]),
            rows(gram[half:, half:]),
            rows(gram[half:, :half]),
        ],
        axis=0,
    )


def unpack_gram(packed):
    half = BLOCK // 2

    def block(rows):
        return jnp.concatenate(
            [rows[:, half * i : half * i + half] for i in range(4)], axis=0
        )

    upper, lower, cross = (block(packed[8 * i : 8 * i + 8]) for i in range(3))
    return jnp.concatenate(
        [
            jnp.concatenate([upper, jnp.transpose(cross)], axis=1),
            jnp.concatenate([cross, lower], axis=1),
        ],
        axis=0,
    )


def factor_rows(gram, out_ref):
    eye = (
        lax.broadcasted_iota(jnp.int32, (BLOCK, BLOCK), 0)
        == lax.broadcasted_iota(jnp.int32, (BLOCK, BLOCK), 1)
    ).astype(jnp.float32)
    whole = jnp.concatenate([gram, eye], axis=1)
    groups = [whole[8 * i : 8 * i + 8] for i in range(BLOCK // 8)]
    for j in range(BLOCK):
        first = j // 8
        k = j % 8
        row = groups[first][k : k + 1]
        root = lax.rsqrt(row[:, j : j + 1])
        scaled = row * root
        out_ref[j : j + 1, :] = scaled
        for i in range(first, BLOCK // 8):
            groups[i] = groups[i] - (groups[i][:, j : j + 1] * root) * scaled


def split_three(value):
    high = value.astype(jnp.bfloat16)
    rest = value - high.astype(jnp.float32)
    middle = rest.astype(jnp.bfloat16)
    low = (rest - middle.astype(jnp.float32)).astype(jnp.bfloat16)
    return jnp.concatenate([high, middle, low], axis=0)


def product(slots_ref, count_ref, tiles_ref, parts_ref, sums_ref, forward, cb):
    count = count_ref[0]
    group = 4

    def visit(step, carry):
        added = []
        for g in range(group):
            t = step * group + g
            slot = slots_ref[t]
            local_row = slot // cb
            local_col = slot - local_row * cb
            source, target = (
                (local_col, local_row) if forward else (local_row, local_col)
            )
            tile = tiles_ref[t]
            tile = jnp.where(t < count, tile, jnp.zeros_like(tile))
            parts = parts_ref[pl.ds(pl.multiple_of(source * 192, 64), 192), :]
            dims = (((1,), (1 if forward else 0,)), ((), ()))
            value = lax.dot_general(
                parts, tile, dims, preferred_element_type=jnp.float32
            )
            added.append((target, value[:64] + value[64:128] + value[128:]))
        for target, value in added:
            where = pl.ds(pl.multiple_of(target * 64, 64), 64)
            sums_ref[where, :] += value
        return carry

    lax.fori_loop(0, (count + group - 1) // group, visit, 0)


def add_gram(gram, value):
    return gram + lax.dot_general(
        value, value, (((1,), (1,)), ((), ())), precision=HIGH,
        preferred_element_type=jnp.float32,
    )


def send_panel(
    slots_ref, count_ref, tiles_ref, panel_ref, scale_ref, sent_ref, parts_ref, sums_ref, *, forward, cb
):
    sums_ref[...] = jnp.zeros_like(sums_ref)
    gram = jnp.zeros((BLOCK, BLOCK), jnp.float32)
    for b in range(panel_ref.shape[0] // BLOCK):
        value = panel_ref[64 * b : 64 * b + 64, :]
        gram = add_gram(gram, value)
        parts_ref[192 * b : 192 * b + 192, :] = split_three(
            value * scale_ref[b : b + 1, :]
        )
    product(slots_ref, count_ref, tiles_ref, parts_ref, sums_ref, forward, cb)
    packed = pack_gram(gram)
    count = sent_ref.shape[0]
    rows = sums_ref.shape[0] // count
    for k in range(count):
        sent_ref[k, :rows, :] = sums_ref[rows * k : rows * k + rows, :]
        sent_ref[k, rows:, :] = packed


def start_kernel(slots_ref, count_ref, tiles_ref, panel_ref, scale_ref, sent_ref, parts_ref, sums_ref, *, cb):
    send_panel(
        slots_ref, count_ref, tiles_ref, panel_ref, scale_ref, sent_ref, parts_ref, sums_ref,
        forward=True, cb=cb,
    )


def fold_kernel(got_ref, out_ref):
    rows = out_ref.shape[-2]
    total = got_ref[0, :rows, :]
    for k in range(1, got_ref.shape[0]):
        total += got_ref[k, :rows, :]
    for k in range(out_ref.shape[0]):
        out_ref[k] = total


def sum_gram(got_ref):
    packed = got_ref[0, -GRAM_ROWS:, :]
    for k in range(1, got_ref.shape[0]):
        packed += got_ref[k, -GRAM_ROWS:, :]
    return unpack_gram(packed)


def factor_kernel(*refs, with_old):
    if not with_old:
        got_ref, factor_ref = refs
        factor_rows(sum_gram(got_ref), factor_ref)
        return
    got_ref, old_ref, old_factor_ref, factor_ref, part_ref = refs
    factor_rows(sum_gram(got_ref), factor_ref)
    upper_mask = lax.broadcasted_iota(
        jnp.int32, (BLOCK, BLOCK), 0
    ) <= lax.broadcasted_iota(jnp.int32, (BLOCK, BLOCK), 1)
    upper = jnp.where(upper_mask, factor_ref[:, :BLOCK], 0.0)
    back = jnp.dot(
        upper, -old_factor_ref[:, BLOCK:], precision=HIGH,
        preferred_element_type=jnp.float32,
    )
    for b in range(old_ref.shape[0] // BLOCK):
        part_ref[64 * b : 64 * b + 64, :] = jnp.dot(
            back, old_ref[64 * b : 64 * b + 64, :], precision=HIGH,
            preferred_element_type=jnp.float32,
        )


def step_kernel(*refs, forward, cb, with_old, last):
    refs = list(refs)
    tables = []
    if not last:
        tables, refs = refs[:3], refs[3:]
    got_ref, scale_ref, factor_ref = refs[:3]
    refs = refs[3:]
    if with_old:
        part_ref, refs = refs[0], refs[1:]
    panel_ref, sent_ref = refs[:2]
    inverse = factor_ref[:, BLOCK:]
    gram = jnp.zeros((BLOCK, BLOCK), jnp.float32)
    for b in range(panel_ref.shape[0] // BLOCK):
        where = slice(64 * b, 64 * b + 64)
        value = jnp.dot(
            inverse, got_ref[where, :] * scale_ref[b : b + 1, :], precision=HIGH,
            preferred_element_type=jnp.float32,
        )
        if with_old:
            value += part_ref[where, :]
        panel_ref[where, :] = value
        if last:
            gram = add_gram(gram, value)
    if last:
        sent_ref[...] = pack_gram(gram)
    else:
        send_panel(
            *tables, panel_ref, scale_ref, sent_ref, refs[2], refs[3],
            forward=forward, cb=cb,
        )


def end_kernel(
    got_ref, right_ref, left_ref, left_factor_ref, out_right_ref, out_left_ref, factor_ref, *,
    left_size, right_size,
):
    factor_rows(sum_gram(got_ref), factor_ref)
    out_right_ref[...] = math.sqrt(right_size) * jnp.dot(
        factor_ref[:, BLOCK:], right_ref[...], precision=HIGH,
        preferred_element_type=jnp.float32,
    )
    out_left_ref[...] = math.sqrt(left_size) * jnp.dot(
        left_factor_ref[:, BLOCK:], left_ref[...], precision=HIGH,
        preferred_element_type=jnp.float32,
    )


SMEM = pl.BlockSpec(memory_space=pltpu.SMEM)
VMEM = pl.BlockSpec(memory_space=pltpu.VMEM)
PARAMS = pltpu.CompilerParams(vmem_limit_bytes=8 * 1024 * 1024)


def f32(*shape):
    return jax.ShapeDtypeStruct(shape, jnp.float32)


def gather_whole(value, axes, count):
    copies = jnp.broadcast_to(value[None], (count,) + value.shape)
    return lax.all_to_all(copies, axes, 0, 0, tiled=True)


def fold(got, copies, rows):
    return pl.pallas_call(
        fold_kernel,
        out_shape=f32(copies, rows, TILE),
        in_specs=[VMEM],
        out_specs=VMEM,
        compiler_params=PARAMS,
        name="fold",
    )(got)


def exchange(messages, axes):
    return lax.all_to_all(messages, axes, 0, 0, tiled=True)


def sum_col(sent):
    near = lax.axis_size(NEAR)
    own = fold(exchange(sent, NEAR), 1, sent.shape[1])[0]
    got = lax.all_gather(own, "zh", axis=0, tiled=False)
    rows = sent.shape[1] - GRAM_ROWS
    return got, exchange(fold(got, near, rows), NEAR).reshape(near * rows, TILE)


def sum_row(sent):
    count = lax.axis_size(ROW)
    got = exchange(sent, ROW)
    rows = sent.shape[1] - GRAM_ROWS
    return got, exchange(fold(got, count, rows), ROW).reshape(count * rows, TILE)


def per_device(tiles, tile_slots, tile_counts, user_degree, item_degree, start_panel):
    tile_stack = tiles[0, 0]
    slots = tile_slots[0, 0]
    count = tile_counts[0]
    rb = user_degree.shape[0] // TILE
    cb = item_degree.shape[0] // TILE
    rows = lax.axis_size(ROW)
    cols = lax.axis_size(COL)
    near = lax.axis_size(NEAR)
    user_scale = lax.rsqrt(user_degree.astype(jnp.float32)).reshape(rb, TILE)
    item_scale = lax.rsqrt(item_degree.astype(jnp.float32)).reshape(cb, TILE)

    start = gather_whole(start_panel, ROW, rows)
    start = jnp.transpose(start, (1, 0, 2)).reshape(BLOCK, cb, TILE)
    start = jnp.transpose(start, (1, 0, 2)).reshape(cb * BLOCK, TILE)

    user_messages = f32(near, rb * BLOCK // near + GRAM_ROWS, TILE)
    item_messages = f32(rows, cb * BLOCK // rows + GRAM_ROWS, TILE)
    user_sums = pltpu.VMEM((rb * BLOCK, TILE), jnp.float32)
    item_sums = pltpu.VMEM((cb * BLOCK, TILE), jnp.float32)
    user_parts = pltpu.VMEM((rb * 192, TILE), jnp.bfloat16)
    item_parts = pltpu.VMEM((cb * 192, TILE), jnp.bfloat16)
    sent = pl.pallas_call(
        functools.partial(start_kernel, cb=cb),
        out_shape=user_messages,
        in_specs=[SMEM, SMEM, VMEM, VMEM, VMEM],
        out_specs=VMEM,
        scratch_shapes=[item_parts, user_sums],
        compiler_params=PARAMS,
        name="start",
    )(slots, count, tile_stack, start, item_scale)

    panels = [start]
    factors = []
    for half in range(1, 2 * STEPS + 1):
        users = half % 2 == 1
        last = half == 2 * STEPS
        with_old = half > 1
        got, whole = sum_col(sent) if users else sum_row(sent)
        panel_shape = f32((rb if users else cb) * BLOCK, TILE)
        old = [panels[half - 2], factors[half - 2]] if with_old else []
        factored = pl.pallas_call(
            functools.partial(factor_kernel, with_old=with_old),
            out_shape=[f32(BLOCK, 2 * BLOCK)] + ([panel_shape] if with_old else []),
            in_specs=[VMEM] * (1 + len(old)),
            out_specs=[VMEM] * (2 if with_old else 1),
            compiler_params=PARAMS,
            name=f"factor{half}",
        )(got, *old)
        factors.append(factored[0])
        tables = [] if last else [slots, count, tile_stack]
        operands = [whole, user_scale if users else item_scale, *factored]
        panel, sent = pl.pallas_call(
            functools.partial(
                step_kernel, forward=not users, cb=cb, with_old=with_old, last=last
            ),
            out_shape=[
                panel_shape,
                f32(GRAM_ROWS, TILE)
                if last
                else (item_messages if users else user_messages),
            ],
            in_specs=([] if last else [SMEM, SMEM, VMEM]) + [VMEM] * len(operands),
            out_specs=[VMEM, VMEM],
            scratch_shapes=[]
            if last
            else ([user_parts, item_sums] if users else [item_parts, user_sums]),
            compiler_params=PARAMS,
            name=f"half{half}",
        )(*tables, *operands)
        panels.append(panel)

    gram = fold(gather_whole(sent, NEAR, near), 1, GRAM_ROWS)[0]
    gram = lax.all_gather(gram, "zh", axis=0, tiled=False)

    user_group = rb * TILE // cols
    item_group = cb * TILE // rows
    left = jnp.transpose(panels[-2].reshape(rb, BLOCK, TILE), (1, 0, 2))
    left = lax.dynamic_slice_in_dim(
        left.reshape(BLOCK, rb * TILE), lax.axis_index(COL) * user_group, user_group, 1
    )
    right = jnp.transpose(panels[-1].reshape(cb, BLOCK, TILE), (1, 0, 2))
    right = lax.dynamic_slice_in_dim(
        right.reshape(BLOCK, cb * TILE), lax.axis_index(ROW) * item_group, item_group, 1
    )
    right_panel, left_panel, factor = pl.pallas_call(
        functools.partial(
            end_kernel, left_size=rb * TILE * rows, right_size=cb * TILE * cols
        ),
        out_shape=[
            f32(BLOCK, item_group),
            f32(BLOCK, user_group),
            f32(BLOCK, 2 * BLOCK),
        ],
        in_specs=[VMEM] * 4,
        out_specs=[VMEM] * 3,
        compiler_params=PARAMS,
        name="end",
    )(gram, right, left, factors[-1])
    factors.append(factor)
    lower = [jnp.tril(jnp.transpose(f[:, :BLOCK])) for f in factors]
    return (
        left_panel,
        right_panel,
        jnp.stack(lower[1::2]),
        jnp.stack(lower[2::2]),
    )


def solution(mesh):
    split = Mesh(mesh.devices.reshape(4, 4, 4, 4, 2), ROW + COL)
    in_specs = (
        P(ROW, COL, None, None, None),
        P(ROW, COL, None),
        P(ROW, COL),
        P(ROW),
        P(COL),
        P(None, COL + ROW),
    )
    out_specs = (P(None, ROW + COL), P(None, COL + ROW), P(), P())
    return jax.shard_map(
        per_device, mesh=split, in_specs=in_specs, out_specs=out_specs, check_vma=False
    )
```

```python
import functools
import math

import jax
import jax.numpy as jnp
from jax import lax
from jax.experimental import pallas as pl
from jax.experimental.pallas import tpu as pltpu
from jax.sharding import Mesh
from jax.sharding import PartitionSpec as P

STEPS = 3
TILE = 128
BLOCK = 64
GRAM_ROWS = 24
HALF_ROWS = 16
HIGH = lax.Precision.HIGHEST

ROW = ("zl", "y")
COL = ("x", "zh", "core")
NEAR = ("x", "core")


def pack_gram(gram):
    half = BLOCK // 2

    def rows(block):
        return jnp.concatenate([block[8 * i : 8 * i + 8] for i in range(4)], axis=1)

    return jnp.concatenate(
        [
            rows(gram[:half, :half]),
            rows(gram[half:, half:]),
            rows(gram[half:, :half]),
        ],
        axis=0,
    )


def unpack_gram(packed):
    half = BLOCK // 2

    def block(rows):
        return jnp.concatenate(
            [rows[:, half * i : half * i + half] for i in range(4)], axis=0
        )

    upper, lower, cross = (block(packed[8 * i : 8 * i + 8]) for i in range(3))
    return jnp.concatenate(
        [
            jnp.concatenate([upper, jnp.transpose(cross)], axis=1),
            jnp.concatenate([cross, lower], axis=1),
        ],
        axis=0,
    )


def factor_rows(gram, out_ref):
    eye = (
        lax.broadcasted_iota(jnp.int32, (BLOCK, BLOCK), 0)
        == lax.broadcasted_iota(jnp.int32, (BLOCK, BLOCK), 1)
    ).astype(jnp.float32)
    whole = jnp.concatenate([gram, eye], axis=1)
    groups = [whole[8 * i : 8 * i + 8] for i in range(BLOCK // 8)]
    for first in range(BLOCK // 8):
        base = 8 * first
        below = range(first, BLOCK // 8)
        spread = {
            i: [
                jnp.broadcast_to(groups[i][:, base + m : base + m + 1], groups[i].shape)
                for m in range(8)
            ]
            for i in below
        }
        for k in range(8):
            root = lax.rsqrt(spread[first][k][k : k + 1])
            scaled = groups[first][k : k + 1] * root
            out_ref[base + k : base + k + 1, :] = scaled
            across = {m: spread[first][m][k : k + 1] * root for m in range(k + 1, 8)}
            for i in below:
                times = spread[i][k] * root
                groups[i] = groups[i] - times * scaled
                for m in across:
                    spread[i][m] = spread[i][m] - times * across[m]


def split_three(value):
    high = value.astype(jnp.bfloat16)
    rest = value - high.astype(jnp.float32)
    middle = rest.astype(jnp.bfloat16)
    low = (rest - middle.astype(jnp.float32)).astype(jnp.bfloat16)
    return high, middle, low


def exact_dot(left, right):
    high, middle, low = left
    first = jnp.concatenate([high, high, middle, high, middle, low], axis=1)
    high, middle, low = right
    second = jnp.concatenate([high, middle, high, low, middle, high], axis=0)
    return jnp.dot(first, second, preferred_element_type=jnp.float32)


def product(slots_ref, count_ref, tiles_ref, parts_ref, sums_ref, forward, cb):
    count = count_ref[0]
    spare = sums_ref.shape[0] // BLOCK - 1
    group = 16

    def visit(step, carry):
        added = []
        for g in range(group):
            t = step * group + g
            slot = slots_ref[t]
            local_row = slot // cb
            local_col = slot - local_row * cb
            source, target = (
                (local_col, local_row) if forward else (local_row, local_col)
            )
            tile = tiles_ref[t]
            target = jnp.where(t < count, target, spare)
            parts = parts_ref[pl.ds(pl.multiple_of(source * 192, 64), 192), :]
            dims = (((1,), (1 if forward else 0,)), ((), ()))
            value = lax.dot_general(
                parts, tile, dims, preferred_element_type=jnp.float32
            )
            added.append((target, value[:64] + value[64:128] + value[128:]))
        for target, value in added:
            where = pl.ds(pl.multiple_of(target * 64, 64), 64)
            sums_ref[where, :] += value
        return carry

    lax.fori_loop(0, (count + group - 1) // group, visit, 0)


def add_gram(gram, value):
    same, cross = gram
    high, middle, low = split_three(value)
    dims = (((1,), (1,)), ((), ()))
    same += lax.dot_general(
        jnp.concatenate([high, middle], axis=1), jnp.concatenate([high, middle], axis=1), dims,
        preferred_element_type=jnp.float32,
    )
    cross += lax.dot_general(
        jnp.concatenate([high, high], axis=1), jnp.concatenate([middle, low], axis=1), dims,
        preferred_element_type=jnp.float32,
    )
    return same, cross


def no_gram():
    return (jnp.zeros((BLOCK, BLOCK), jnp.float32),) * 2


def whole_gram(gram):
    same, cross = gram
    return same + cross + jnp.transpose(cross)


def send_panel(
    slots_ref, count_ref, tiles_ref, panel_ref, scale_ref, sent_ref, parts_ref, sums_ref, *, forward, cb, core=None
):
    sums_ref[...] = jnp.zeros_like(sums_ref)
    gram = no_gram()
    for b in range(panel_ref.shape[0] // BLOCK):
        value = panel_ref[64 * b : 64 * b + 64, :]
        gram = add_gram(gram, value)
        parts_ref[192 * b : 192 * b + 192, :] = jnp.concatenate(
            split_three(value * scale_ref[b : b + 1, :]), axis=0
        )
    product(slots_ref, count_ref, tiles_ref, parts_ref, sums_ref, forward, cb)
    packed = pack_gram(whole_gram(gram))
    if core is not None:
        cross = packed[HALF_ROWS:]
        packed = jnp.where(
            core == 0, packed[:HALF_ROWS], jnp.concatenate([cross, cross], axis=0)
        )
    count = sent_ref.shape[0]
    rows = (sums_ref.shape[0] - BLOCK) // count
    for k in range(count):
        sent_ref[k, :rows, :] = sums_ref[rows * k : rows * k + rows, :]
        sent_ref[k, rows:, :] = packed


def start_kernel(slots_ref, count_ref, tiles_ref, panel_ref, scale_ref, sent_ref, parts_ref, sums_ref, *, cb):
    send_panel(
        slots_ref, count_ref, tiles_ref, panel_ref, scale_ref, sent_ref, parts_ref, sums_ref,
        forward=True, cb=cb,
    )


def fold_kernel(got_ref, out_ref, *rest):
    rows = out_ref.shape[-2]
    total = got_ref[0, :rows, :]
    for k in range(1, got_ref.shape[0]):
        total += got_ref[k, :rows, :]
    for k in range(out_ref.shape[0]):
        out_ref[k] = total
    if rest:
        other = got_ref[0, rows:, :]
        for k in range(1, got_ref.shape[0]):
            other += got_ref[k, rows:, :]
        rest[0][...] = other


def sum_gram(got_ref):
    packed = got_ref[0, -GRAM_ROWS:, :]
    for k in range(1, got_ref.shape[0]):
        packed += got_ref[k, -GRAM_ROWS:, :]
    return unpack_gram(packed)


def join_gram(core_ref, own_ref, other_ref):
    first = core_ref[0] == 0
    own, other = own_ref[...], other_ref[...]
    return unpack_gram(
        jnp.concatenate(
            [
                jnp.where(first, own, other),
                jnp.where(first, other, own)[: GRAM_ROWS - HALF_ROWS],
            ],
            axis=0,
        )
    )


def factor_kernel(*refs, with_old, halves):
    refs = list(refs)
    if halves:
        gram, refs = join_gram(*refs[:3]), refs[3:]
    else:
        gram, refs = sum_gram(refs[0]), refs[1:]
    if not with_old:
        factor_rows(gram, refs[0])
        return
    old_ref, old_factor_ref, factor_ref, part_ref = refs
    factor_rows(gram, factor_ref)
    upper_mask = lax.broadcasted_iota(
        jnp.int32, (BLOCK, BLOCK), 0
    ) <= lax.broadcasted_iota(jnp.int32, (BLOCK, BLOCK), 1)
    upper = jnp.where(upper_mask, factor_ref[:, :BLOCK], 0.0)
    back = jnp.dot(
        upper, -old_factor_ref[:, BLOCK:], precision=HIGH,
        preferred_element_type=jnp.float32,
    )
    for b in range(old_ref.shape[0] // BLOCK):
        part_ref[64 * b : 64 * b + 64, :] = jnp.dot(
            back, old_ref[64 * b : 64 * b + 64, :], precision=HIGH,
            preferred_element_type=jnp.float32,
        )


def step_kernel(*refs, forward, cb, with_old, last):
    refs = list(refs)
    tables = []
    if not last:
        tables, refs = refs[:3], refs[3:]
    core = None
    if not (forward or last):
        core, refs = refs[0][0], refs[1:]
    got_ref, scale_ref, factor_ref = refs[:3]
    refs = refs[3:]
    if with_old:
        part_ref, refs = refs[0], refs[1:]
    panel_ref, sent_ref = refs[:2]
    inverse = split_three(factor_ref[:, BLOCK:])
    gram = no_gram()
    for b in range(panel_ref.shape[0] // BLOCK):
        where = slice(64 * b, 64 * b + 64)
        value = exact_dot(
            inverse, split_three(got_ref[where, :] * scale_ref[b : b + 1, :])
        )
        if with_old:
            value += part_ref[where, :]
        panel_ref[where, :] = value
        if last:
            gram = add_gram(gram, value)
    if last:
        sent_ref[...] = pack_gram(whole_gram(gram))
    else:
        send_panel(
            *tables, panel_ref, scale_ref, sent_ref, refs[2], refs[3],
            forward=forward, cb=cb, core=core,
        )


def end_kernel(
    got_ref, right_ref, left_ref, left_factor_ref, out_right_ref, out_left_ref, factor_ref, *,
    left_size, right_size,
):
    factor_rows(sum_gram(got_ref), factor_ref)
    out_right_ref[...] = math.sqrt(right_size) * jnp.dot(
        factor_ref[:, BLOCK:], right_ref[...], precision=HIGH,
        preferred_element_type=jnp.float32,
    )
    out_left_ref[...] = math.sqrt(left_size) * jnp.dot(
        left_factor_ref[:, BLOCK:], left_ref[...], precision=HIGH,
        preferred_element_type=jnp.float32,
    )


SMEM = pl.BlockSpec(memory_space=pltpu.SMEM)
VMEM = pl.BlockSpec(memory_space=pltpu.VMEM)
PARAMS = pltpu.CompilerParams(vmem_limit_bytes=8 * 1024 * 1024)


def f32(*shape):
    return jax.ShapeDtypeStruct(shape, jnp.float32)


def gather_whole(value, axes, count):
    copies = jnp.broadcast_to(value[None], (count,) + value.shape)
    return lax.all_to_all(copies, axes, 0, 0, tiled=True)


def fold(got, copies, rows, rest=False):
    shapes = [f32(copies, rows, TILE)]
    if rest:
        shapes.append(f32(got.shape[1] - rows, TILE))
    return pl.pallas_call(
        fold_kernel,
        out_shape=shapes,
        in_specs=[VMEM],
        out_specs=[VMEM] * len(shapes),
        compiler_params=PARAMS,
        name="fold",
    )(got)


def exchange(messages, axes):
    return lax.all_to_all(messages, axes, 0, 0, tiled=True)


def sum_col(sent):
    near = lax.axis_size(NEAR)
    own = fold(exchange(sent, NEAR), 1, sent.shape[1])[0][0]
    got = lax.all_gather(own, "zh", axis=0, tiled=False)
    rows = sent.shape[1] - GRAM_ROWS
    return [got], exchange(fold(got, near, rows)[0], NEAR).reshape(near * rows, TILE)


def sum_row(sent, core):
    count = lax.axis_size(ROW)
    rows = sent.shape[1] - HALF_ROWS
    copies, own = fold(exchange(sent, ROW), count, rows, rest=True)
    whole = exchange(copies, ROW).reshape(count * rows, TILE)
    other = lax.ppermute(own, "core", [(0, 1), (1, 0)])
    return [core, own, other], whole


def per_device(tiles, tile_slots, tile_counts, user_degree, item_degree, start_panel):
    tile_stack = tiles[0, 0]
    slots = tile_slots[0, 0]
    count = tile_counts[0]
    rb = user_degree.shape[0] // TILE
    cb = item_degree.shape[0] // TILE
    rows = lax.axis_size(ROW)
    cols = lax.axis_size(COL)
    near = lax.axis_size(NEAR)
    core = lax.axis_index("core").astype(jnp.int32).reshape(1)
    user_scale = lax.rsqrt(user_degree.astype(jnp.float32)).reshape(rb, TILE)
    item_scale = lax.rsqrt(item_degree.astype(jnp.float32)).reshape(cb, TILE)

    start = gather_whole(start_panel, ROW, rows)
    start = jnp.transpose(start, (1, 0, 2)).reshape(BLOCK, cb, TILE)
    start = jnp.transpose(start, (1, 0, 2)).reshape(cb * BLOCK, TILE)

    user_messages = f32(near, rb * BLOCK // near + GRAM_ROWS, TILE)
    item_messages = f32(rows, cb * BLOCK // rows + HALF_ROWS, TILE)
    user_sums = pltpu.VMEM((rb * BLOCK + BLOCK, TILE), jnp.float32)
    item_sums = pltpu.VMEM((cb * BLOCK + BLOCK, TILE), jnp.float32)
    user_parts = pltpu.VMEM((rb * 192, TILE), jnp.bfloat16)
    item_parts = pltpu.VMEM((cb * 192, TILE), jnp.bfloat16)
    sent = pl.pallas_call(
        functools.partial(start_kernel, cb=cb),
        out_shape=user_messages,
        in_specs=[SMEM, SMEM, VMEM, VMEM, VMEM],
        out_specs=VMEM,
        scratch_shapes=[item_parts, user_sums],
        compiler_params=PARAMS,
        name="start",
    )(slots, count, tile_stack, start, item_scale)

    panels = [start]
    factors = []
    for half in range(1, 2 * STEPS + 1):
        users = half % 2 == 1
        last = half == 2 * STEPS
        with_old = half > 1
        gram, whole = sum_col(sent) if users else sum_row(sent, core)
        panel_shape = f32((rb if users else cb) * BLOCK, TILE)
        old = [panels[half - 2], factors[half - 2]] if with_old else []
        factored = pl.pallas_call(
            functools.partial(factor_kernel, with_old=with_old, halves=not users),
            out_shape=[f32(BLOCK, 2 * BLOCK)] + ([panel_shape] if with_old else []),
            in_specs=([VMEM] if users else [SMEM, VMEM, VMEM]) + [VMEM] * len(old),
            out_specs=[VMEM] * (2 if with_old else 1),
            compiler_params=PARAMS,
            name=f"factor{half}",
        )(*gram, *old)
        factors.append(factored[0])
        tables = [] if last else [slots, count, tile_stack]
        table_specs = [] if last else [SMEM, SMEM, VMEM]
        if users:
            tables.append(core)
            table_specs.append(SMEM)
        operands = [whole, user_scale if users else item_scale, *factored]
        panel, sent = pl.pallas_call(
            functools.partial(
                step_kernel, forward=not users, cb=cb, with_old=with_old, last=last
            ),
            out_shape=[
                panel_shape,
                f32(GRAM_ROWS, TILE)
                if last
                else (item_messages if users else user_messages),
            ],
            in_specs=table_specs + [VMEM] * len(operands),
            out_specs=[VMEM, VMEM],
            scratch_shapes=[]
            if last
            else ([user_parts, item_sums] if users else [item_parts, user_sums]),
            compiler_params=PARAMS,
            name=f"half{half}",
        )(*tables, *operands)
        panels.append(panel)

    gram = fold(gather_whole(sent, NEAR, near), 1, GRAM_ROWS)[0][0]
    gram = lax.all_gather(gram, "zh", axis=0, tiled=False)

    user_group = rb * TILE // cols
    item_group = cb * TILE // rows
    left = jnp.transpose(panels[-2].reshape(rb, BLOCK, TILE), (1, 0, 2))
    left = lax.dynamic_slice_in_dim(
        left.reshape(BLOCK, rb * TILE), lax.axis_index(COL) * user_group, user_group, 1
    )
    right = jnp.transpose(panels[-1].reshape(cb, BLOCK, TILE), (1, 0, 2))
    right = lax.dynamic_slice_in_dim(
        right.reshape(BLOCK, cb * TILE), lax.axis_index(ROW) * item_group, item_group, 1
    )
    right_panel, left_panel, factor = pl.pallas_call(
        functools.partial(
            end_kernel, left_size=rb * TILE * rows, right_size=cb * TILE * cols
        ),
        out_shape=[
            f32(BLOCK, item_group),
            f32(BLOCK, user_group),
            f32(BLOCK, 2 * BLOCK),
        ],
        in_specs=[VMEM] * 4,
        out_specs=[VMEM] * 3,
        compiler_params=PARAMS,
        name="end",
    )(gram, right, left, factors[-1])
    factors.append(factor)
    lower = [jnp.tril(jnp.transpose(f[:, :BLOCK])) for f in factors]
    return (
        left_panel,
        right_panel,
        jnp.stack(lower[1::2]),
        jnp.stack(lower[2::2]),
    )


def solution(mesh):
    split = Mesh(mesh.devices.reshape(4, 4, 4, 4, 2), ROW + COL)
    in_specs = (
        P(ROW, COL, None, None, None),
        P(ROW, COL, None),
        P(ROW, COL),
        P(ROW),
        P(COL),
        P(None, COL + ROW),
    )
    out_specs = (P(None, ROW + COL), P(None, COL + ROW), P(), P())
    return jax.shard_map(
        per_device, mesh=split, in_specs=in_specs, out_specs=out_specs, check_vma=False
    )
```

```python
import functools
import math

import jax
import jax.numpy as jnp
from jax import lax
from jax.experimental import pallas as pl
from jax.experimental.pallas import tpu as pltpu
from jax.sharding import Mesh
from jax.sharding import PartitionSpec as P

STEPS = 3
TILE = 128
BLOCK = 64
GRAM_ROWS = 24
HALF_ROWS = 16
UNIT = 32
HIGH = lax.Precision.HIGHEST

ROW = ("zl", "y")
COL = ("x", "zh", "core")
NEAR = ("core", "x")


def pack_gram(gram):
    half = BLOCK // 2

    def rows(block):
        return jnp.concatenate([block[8 * i : 8 * i + 8] for i in range(4)], axis=1)

    return jnp.concatenate(
        [
            rows(gram[:half, :half]),
            rows(gram[half:, half:]),
            rows(gram[half:, :half]),
        ],
        axis=0,
    )


def unpack_gram(packed):
    half = BLOCK // 2

    def block(rows):
        return jnp.concatenate(
            [rows[:, half * i : half * i + half] for i in range(4)], axis=0
        )

    upper, lower, cross = (block(packed[8 * i : 8 * i + 8]) for i in range(3))
    return jnp.concatenate(
        [
            jnp.concatenate([upper, jnp.transpose(cross)], axis=1),
            jnp.concatenate([cross, lower], axis=1),
        ],
        axis=0,
    )


def factor_rows(gram, out_ref):
    eye = (
        lax.broadcasted_iota(jnp.int32, (BLOCK, BLOCK), 0)
        == lax.broadcasted_iota(jnp.int32, (BLOCK, BLOCK), 1)
    ).astype(jnp.float32)
    whole = jnp.concatenate([gram, eye], axis=1)
    groups = [whole[8 * i : 8 * i + 8] for i in range(BLOCK // 8)]
    for first in range(BLOCK // 8):
        base = 8 * first
        below = range(first, BLOCK // 8)
        spread = {
            i: [
                jnp.broadcast_to(groups[i][:, base + m : base + m + 1], groups[i].shape)
                for m in range(8)
            ]
            for i in below
        }
        for k in range(8):
            root = lax.rsqrt(spread[first][k][k : k + 1])
            scaled = groups[first][k : k + 1] * root
            out_ref[base + k : base + k + 1, :] = scaled
            across = {m: spread[first][m][k : k + 1] * root for m in range(k + 1, 8)}
            for i in below:
                times = spread[i][k] * root
                groups[i] = groups[i] - times * scaled
                for m in across:
                    spread[i][m] = spread[i][m] - times * across[m]


def split_three(value):
    high = value.astype(jnp.bfloat16)
    rest = value - high.astype(jnp.float32)
    middle = rest.astype(jnp.bfloat16)
    low = (rest - middle.astype(jnp.float32)).astype(jnp.bfloat16)
    return high, middle, low


def exact_dot(left, right):
    high, middle, low = left
    first = jnp.concatenate([high, high, middle, high, middle, low], axis=1)
    high, middle, low = right
    second = jnp.concatenate([high, middle, high, low, middle, high], axis=0)
    return jnp.dot(first, second, preferred_element_type=jnp.float32)


def product(slots_ref, count_ref, tiles_ref, parts_ref, sums_ref, forward, cb):
    count = count_ref[0]
    spare = sums_ref.shape[0] // BLOCK - 1
    group = 16

    def visit(step, carry):
        added = []
        for g in range(group):
            t = step * group + g
            slot = slots_ref[t]
            local_row = slot // cb
            local_col = slot - local_row * cb
            source, target = (
                (local_col, local_row) if forward else (local_row, local_col)
            )
            tile = tiles_ref[t]
            target = jnp.where(t < count, target, spare)
            parts = parts_ref[pl.ds(pl.multiple_of(source * 192, 64), 192), :]
            dims = (((1,), (1 if forward else 0,)), ((), ()))
            value = lax.dot_general(
                parts, tile, dims, preferred_element_type=jnp.float32
            )
            added.append((target, value[:64] + value[64:128] + value[128:]))
        for target, value in added:
            where = pl.ds(pl.multiple_of(target * 64, 64), 64)
            sums_ref[where, :] += value
        return carry

    lax.fori_loop(0, (count + group - 1) // group, visit, 0)


def add_gram(gram, value):
    same, cross = gram
    high, middle, low = split_three(value)
    dims = (((1,), (1,)), ((), ()))
    same += lax.dot_general(
        jnp.concatenate([high, middle], axis=1), jnp.concatenate([high, middle], axis=1), dims,
        preferred_element_type=jnp.float32,
    )
    cross += lax.dot_general(
        jnp.concatenate([high, high], axis=1), jnp.concatenate([middle, low], axis=1), dims,
        preferred_element_type=jnp.float32,
    )
    return same, cross


def no_gram():
    return (jnp.zeros((BLOCK, BLOCK), jnp.float32),) * 2


def whole_gram(gram):
    same, cross = gram
    return same + cross + jnp.transpose(cross)


def send_panel(
    slots_ref, count_ref, tiles_ref, panel_ref, scale_ref, sent_ref, parts_ref, sums_ref, *, forward, cb, core=None,
    ready=None,
):
    sums_ref[...] = jnp.zeros_like(sums_ref)
    gram = no_gram()
    for b in range(panel_ref.shape[0] // BLOCK):
        value = panel_ref[64 * b : 64 * b + 64, :]
        gram = add_gram(gram, value)
        parts_ref[192 * b : 192 * b + 192, :] = jnp.concatenate(
            split_three(value * scale_ref[b : b + 1, :]), axis=0
        )
    if ready is not None:
        ready.wait()
    product(slots_ref, count_ref, tiles_ref, parts_ref, sums_ref, forward, cb)
    packed = pack_gram(whole_gram(gram))
    if core is not None:
        cross = packed[HALF_ROWS:]
        packed = jnp.where(
            core == 0, packed[:HALF_ROWS], jnp.concatenate([cross, cross], axis=0)
        )
    count = sent_ref.shape[0]
    rows = (sums_ref.shape[0] - BLOCK) // count
    for k in range(count):
        sent_ref[k, :rows, :] = sums_ref[rows * k : rows * k + rows, :]
        sent_ref[k, rows:, :] = packed


def unit_rows(unit, rows):
    for piece in range(BLOCK // 16):
        at = BLOCK * unit + 16 * piece
        yield at % rows, UNIT * (at // rows)


def pack_kernel(panel_ref, out_ref):
    rows = out_ref.shape[1]
    columns = [[] for _ in range(TILE // UNIT)]
    for unit in range(panel_ref.shape[1] // UNIT):
        value = panel_ref[:, UNIT * unit : UNIT * unit + UNIT]
        for piece, (_, lane) in enumerate(unit_rows(unit, rows)):
            columns[lane // UNIT].append(value[16 * piece : 16 * piece + 16])
    packed = jnp.concatenate(
        [jnp.concatenate(pieces, axis=0) for pieces in columns], axis=1
    )
    for k in range(out_ref.shape[0]):
        out_ref[k] = packed


def start_kernel(
    slots_ref, count_ref, tiles_ref, got_ref, scale_ref, panel_ref, sent_ref,
    parts_ref, sums_ref, near_tiles_ref, sem, *, cb, units,
):
    copy = pltpu.make_async_copy(tiles_ref, near_tiles_ref, sem)
    copy.start()
    rows = got_ref.shape[1]
    for b in range(cb):
        found = []
        for c in range(TILE // UNIT):
            device, unit = divmod(TILE // UNIT * b + c, units)
            found.append(
                [
                    got_ref[device, row : row + 16, lane : lane + UNIT]
                    for row, lane in unit_rows(unit, rows)
                ]
            )
        for piece in range(BLOCK // 16):
            panel_ref[64 * b + 16 * piece : 64 * b + 16 * piece + 16, :] = (
                jnp.concatenate([pieces[piece] for pieces in found], axis=1)
            )
    send_panel(
        slots_ref, count_ref, near_tiles_ref, panel_ref, scale_ref, sent_ref, parts_ref, sums_ref,
        forward=True, cb=cb, ready=copy,
    )


def fold_kernel(got_ref, out_ref, *rest):
    rows = out_ref.shape[-2]
    total = got_ref[0, :rows, :]
    for k in range(1, got_ref.shape[0]):
        total += got_ref[k, :rows, :]
    for k in range(out_ref.shape[0]):
        out_ref[k] = total
    if rest:
        other = got_ref[0, rows:, :]
        for k in range(1, got_ref.shape[0]):
            other += got_ref[k, rows:, :]
        rest[0][...] = other


def sum_gram(got_ref):
    packed = got_ref[0, -GRAM_ROWS:, :]
    for k in range(1, got_ref.shape[0]):
        packed += got_ref[k, -GRAM_ROWS:, :]
    return unpack_gram(packed)


def join_gram(core_ref, own_ref, other_ref):
    first = core_ref[0] == 0
    own, other = own_ref[...], other_ref[...]
    return unpack_gram(
        jnp.concatenate(
            [
                jnp.where(first, own, other),
                jnp.where(first, other, own)[: GRAM_ROWS - HALF_ROWS],
            ],
            axis=0,
        )
    )


def lower_factor(factor_ref):
    lower = jnp.transpose(factor_ref[:, :BLOCK])
    mask = lax.broadcasted_iota(
        jnp.int32, (BLOCK, BLOCK), 0
    ) >= lax.broadcasted_iota(jnp.int32, (BLOCK, BLOCK), 1)
    return jnp.where(mask, lower, 0.0)


def factor_kernel(*refs, with_old, halves):
    refs = list(refs)
    if halves:
        gram, refs = join_gram(*refs[:3]), refs[3:]
    else:
        gram, refs = sum_gram(refs[0]), refs[1:]
    if not with_old:
        factor_rows(gram, refs[0])
        return
    old_ref, old_factor_ref, factor_ref, part_ref, lower_ref = refs
    factor_rows(gram, factor_ref)
    lower_ref[...] = lower_factor(factor_ref)
    upper_mask = lax.broadcasted_iota(
        jnp.int32, (BLOCK, BLOCK), 0
    ) <= lax.broadcasted_iota(jnp.int32, (BLOCK, BLOCK), 1)
    upper = jnp.where(upper_mask, factor_ref[:, :BLOCK], 0.0)
    back = jnp.dot(
        upper, -old_factor_ref[:, BLOCK:], precision=HIGH,
        preferred_element_type=jnp.float32,
    )
    for b in range(old_ref.shape[0] // BLOCK):
        part_ref[64 * b : 64 * b + 64, :] = jnp.dot(
            back, old_ref[64 * b : 64 * b + 64, :], precision=HIGH,
            preferred_element_type=jnp.float32,
        )


def step_kernel(*refs, forward, cb, with_old, last):
    refs = list(refs)
    tables = []
    if not last:
        tables, refs = refs[:3], refs[3:]
    core = None
    if not (forward or last):
        core, refs = refs[0][0], refs[1:]
    got_ref, scale_ref, factor_ref = refs[:3]
    refs = refs[3:]
    if with_old:
        part_ref, refs = refs[0], refs[1:]
    panel_ref, sent_ref = refs[:2]
    inverse = split_three(factor_ref[:, BLOCK:])
    gram = no_gram()
    for b in range(panel_ref.shape[0] // BLOCK):
        where = slice(64 * b, 64 * b + 64)
        value = exact_dot(
            inverse, split_three(got_ref[where, :] * scale_ref[b : b + 1, :])
        )
        if with_old:
            value += part_ref[where, :]
        panel_ref[where, :] = value
        if last:
            gram = add_gram(gram, value)
    if last:
        packed = pack_gram(whole_gram(gram))
        for k in range(sent_ref.shape[0]):
            sent_ref[k] = packed
    else:
        send_panel(
            *tables, panel_ref, scale_ref, sent_ref, refs[2], refs[3],
            forward=forward, cb=cb, core=core,
        )


def end_kernel(
    got_ref, right_ref, left_ref, left_factor_ref, first_ref, second_ref,
    out_right_ref, out_left_ref, lower_ref, factor_ref, *, left_size, right_size,
):
    lower_ref[0] = first_ref[...]
    lower_ref[1] = second_ref[...]
    factor_rows(sum_gram(got_ref), factor_ref)
    lower_ref[2] = lower_factor(factor_ref)
    out_right_ref[...] = math.sqrt(right_size) * jnp.dot(
        factor_ref[:, BLOCK:], right_ref[...], precision=HIGH,
        preferred_element_type=jnp.float32,
    )
    out_left_ref[...] = math.sqrt(left_size) * jnp.dot(
        left_factor_ref[:, BLOCK:], left_ref[...], precision=HIGH,
        preferred_element_type=jnp.float32,
    )


SMEM = pl.BlockSpec(memory_space=pltpu.SMEM)
VMEM = pl.BlockSpec(memory_space=pltpu.VMEM)
PARAMS = pltpu.CompilerParams(vmem_limit_bytes=8 * 1024 * 1024)


def f32(*shape):
    return jax.ShapeDtypeStruct(shape, jnp.float32)


def fold(got, copies, rows, rest=False):
    shapes = [f32(copies, rows, TILE)]
    if rest:
        shapes.append(f32(got.shape[1] - rows, TILE))
    return pl.pallas_call(
        fold_kernel,
        out_shape=shapes,
        in_specs=[VMEM],
        out_specs=[VMEM] * len(shapes),
        compiler_params=PARAMS,
        name="fold",
    )(got)


def exchange(messages, axes):
    return lax.all_to_all(messages, axes, 0, 0, tiled=True)


def sum_col(sent):
    near = lax.axis_size(NEAR)
    own = fold(exchange(sent, NEAR), 1, sent.shape[1])[0][0]
    got = lax.all_gather(own, "zh", axis=0, tiled=False)
    rows = sent.shape[1] - GRAM_ROWS
    line = lax.axis_size("x")
    half = exchange(fold(got, line, rows)[0], "x").reshape(line * rows, TILE)
    return [got], lax.all_gather(half, "core", axis=0, tiled=True)


def sum_row(sent, core):
    count = lax.axis_size(ROW)
    rows = sent.shape[1] - HALF_ROWS
    copies, own = fold(exchange(sent, ROW), count, rows, rest=True)
    whole = exchange(copies, ROW).reshape(count * rows, TILE)
    other = lax.ppermute(own, "core", [(0, 1), (1, 0)])
    return [core, own, other], whole


def per_device(tiles, tile_slots, tile_counts, user_degree, item_degree, start_panel):
    tile_stack = tiles[0, 0]
    slots = tile_slots[0, 0]
    count = tile_counts[0]
    rb = user_degree.shape[0] // TILE
    cb = item_degree.shape[0] // TILE
    rows = lax.axis_size(ROW)
    cols = lax.axis_size(COL)
    near = lax.axis_size(NEAR)
    core = lax.axis_index("core").astype(jnp.int32).reshape(1)
    user_scale = lax.rsqrt(user_degree.astype(jnp.float32)).reshape(rb, TILE)
    item_scale = lax.rsqrt(item_degree.astype(jnp.float32)).reshape(cb, TILE)

    units = start_panel.shape[1] // UNIT
    start = pl.pallas_call(
        pack_kernel,
        out_shape=f32(rows, BLOCK * units * UNIT // TILE, TILE),
        in_specs=[VMEM],
        out_specs=VMEM,
        compiler_params=PARAMS,
        name="pack",
    )(start_panel)
    start = exchange(start, ROW)

    user_messages = f32(near, rb * BLOCK // near + GRAM_ROWS, TILE)
    item_messages = f32(rows, cb * BLOCK // rows + HALF_ROWS, TILE)
    user_sums = pltpu.VMEM((rb * BLOCK + BLOCK, TILE), jnp.float32)
    item_sums = pltpu.VMEM((cb * BLOCK + BLOCK, TILE), jnp.float32)
    user_parts = pltpu.VMEM((rb * 192, TILE), jnp.bfloat16)
    item_parts = pltpu.VMEM((cb * 192, TILE), jnp.bfloat16)
    start, sent = pl.pallas_call(
        functools.partial(start_kernel, cb=cb, units=units),
        out_shape=[f32(cb * BLOCK, TILE), user_messages],
        in_specs=[SMEM, SMEM, pl.BlockSpec(memory_space=pl.ANY), VMEM, VMEM],
        out_specs=[VMEM, VMEM],
        scratch_shapes=[
            item_parts,
            user_sums,
            pltpu.VMEM(tile_stack.shape, tile_stack.dtype),
            pltpu.SemaphoreType.DMA,
        ],
        compiler_params=PARAMS,
        name="start",
    )(slots, count, tile_stack, start, item_scale)

    panels = [start]
    factors = []
    lower = []
    for half in range(1, 2 * STEPS + 1):
        users = half % 2 == 1
        last = half == 2 * STEPS
        with_old = half > 1
        gram, whole = sum_col(sent) if users else sum_row(sent, core)
        panel_shape = f32((rb if users else cb) * BLOCK, TILE)
        old = [panels[half - 2], factors[half - 2]] if with_old else []
        factored = pl.pallas_call(
            functools.partial(factor_kernel, with_old=with_old, halves=not users),
            out_shape=[f32(BLOCK, 2 * BLOCK)]
            + ([panel_shape, f32(BLOCK, BLOCK)] if with_old else []),
            in_specs=([VMEM] if users else [SMEM, VMEM, VMEM]) + [VMEM] * len(old),
            out_specs=[VMEM] * (3 if with_old else 1),
            compiler_params=PARAMS,
            name=f"factor{half}",
        )(*gram, *old)
        factors.append(factored[0])
        lower += factored[2:]
        tables = [] if last else [slots, count, tile_stack]
        table_specs = [] if last else [SMEM, SMEM, VMEM]
        if users:
            tables.append(core)
            table_specs.append(SMEM)
        operands = [whole, user_scale if users else item_scale, *factored[:2]]
        panel, sent = pl.pallas_call(
            functools.partial(
                step_kernel, forward=not users, cb=cb, with_old=with_old, last=last
            ),
            out_shape=[
                panel_shape,
                f32(near, GRAM_ROWS, TILE)
                if last
                else (item_messages if users else user_messages),
            ],
            in_specs=table_specs + [VMEM] * len(operands),
            out_specs=[VMEM, VMEM],
            scratch_shapes=[]
            if last
            else ([user_parts, item_sums] if users else [item_parts, user_sums]),
            compiler_params=PARAMS,
            name=f"half{half}",
        )(*tables, *operands)
        panels.append(panel)

    gram = fold(exchange(sent, NEAR), 1, GRAM_ROWS)[0][0]
    gram = lax.all_gather(gram, "zh", axis=0, tiled=False)

    user_group = rb * TILE // cols
    item_group = cb * TILE // rows
    left = jnp.transpose(panels[-2].reshape(rb, BLOCK, TILE), (1, 0, 2))
    left = lax.dynamic_slice_in_dim(
        left.reshape(BLOCK, rb * TILE), lax.axis_index(COL) * user_group, user_group, 1
    )
    right = jnp.transpose(panels[-1].reshape(cb, BLOCK, TILE), (1, 0, 2))
    right = lax.dynamic_slice_in_dim(
        right.reshape(BLOCK, cb * TILE), lax.axis_index(ROW) * item_group, item_group, 1
    )
    right_panel, left_panel, right_factors = pl.pallas_call(
        functools.partial(
            end_kernel, left_size=rb * TILE * rows, right_size=cb * TILE * cols
        ),
        out_shape=[
            f32(BLOCK, item_group),
            f32(BLOCK, user_group),
            f32(STEPS, BLOCK, BLOCK),
        ],
        in_specs=[VMEM] * 6,
        out_specs=[VMEM] * 3,
        scratch_shapes=[pltpu.VMEM((BLOCK, 2 * BLOCK), jnp.float32)],
        compiler_params=PARAMS,
        name="end",
    )(gram, right, left, factors[-1], lower[1], lower[3])
    return left_panel, right_panel, jnp.stack(lower[::2]), right_factors


def solution(mesh):
    split = Mesh(mesh.devices.reshape(4, 4, 4, 4, 2), ROW + COL)
    in_specs = (
        P(ROW, COL, None, None, None),
        P(ROW, COL, None),
        P(ROW, COL),
        P(ROW),
        P(COL),
        P(None, COL + ROW),
    )
    out_specs = (P(None, ROW + COL), P(None, COL + ROW), P(), P())
    return jax.shard_map(
        per_device, mesh=split, in_specs=in_specs, out_specs=out_specs, check_vma=False
    )
```

```python
import functools
import math

import jax
import jax.numpy as jnp
from jax import lax
from jax.experimental import pallas as pl
from jax.experimental.pallas import tpu as pltpu
from jax.sharding import Mesh
from jax.sharding import PartitionSpec as P

STEPS = 3
TILE = 128
BLOCK = 64
GRAM_ROWS = 24
HALF_ROWS = 16
UNIT = 32
HIGH = lax.Precision.HIGHEST

ROW = ("zl", "y")
COL = ("x", "zh", "core")
NEAR = ("core", "x")


def pack_gram(gram):
    half = BLOCK // 2

    def rows(block):
        return jnp.concatenate([block[8 * i : 8 * i + 8] for i in range(4)], axis=1)

    return jnp.concatenate(
        [
            rows(gram[:half, :half]),
            rows(gram[half:, half:]),
            rows(gram[half:, :half]),
        ],
        axis=0,
    )


def unpack_gram(packed):
    half = BLOCK // 2

    def block(rows):
        return jnp.concatenate(
            [rows[:, half * i : half * i + half] for i in range(4)], axis=0
        )

    upper, lower, cross = (block(packed[8 * i : 8 * i + 8]) for i in range(3))
    return jnp.concatenate(
        [
            jnp.concatenate([upper, jnp.transpose(cross)], axis=1),
            jnp.concatenate([cross, lower], axis=1),
        ],
        axis=0,
    )


def factor_rows(gram, out_ref):
    eye = (
        lax.broadcasted_iota(jnp.int32, (BLOCK, BLOCK), 0)
        == lax.broadcasted_iota(jnp.int32, (BLOCK, BLOCK), 1)
    ).astype(jnp.float32)
    whole = jnp.concatenate([gram, eye], axis=1)
    groups = [whole[8 * i : 8 * i + 8] for i in range(BLOCK // 8)]
    for first in range(BLOCK // 8):
        base = 8 * first
        below = range(first, BLOCK // 8)
        spread = {
            i: [
                jnp.broadcast_to(groups[i][:, base + m : base + m + 1], groups[i].shape)
                for m in range(8)
            ]
            for i in below
        }
        for k in range(8):
            root = lax.rsqrt(spread[first][k][k : k + 1])
            scaled = groups[first][k : k + 1] * root
            out_ref[base + k : base + k + 1, :] = scaled
            across = {m: spread[first][m][k : k + 1] * root for m in range(k + 1, 8)}
            for i in below:
                times = spread[i][k] * root
                groups[i] = groups[i] - times * scaled
                for m in across:
                    spread[i][m] = spread[i][m] - times * across[m]


def split_three(value):
    high = value.astype(jnp.bfloat16)
    rest = value - high.astype(jnp.float32)
    middle = rest.astype(jnp.bfloat16)
    low = (rest - middle.astype(jnp.float32)).astype(jnp.bfloat16)
    return high, middle, low


def exact_dot(left, right):
    high, middle, low = left
    first = jnp.concatenate([high, high, middle, high, middle, low], axis=1)
    high, middle, low = right
    second = jnp.concatenate([high, middle, high, low, middle, high], axis=0)
    return jnp.dot(first, second, preferred_element_type=jnp.float32)


def product(table_ref, tiles_ref, parts_ref, sums_ref, forward, cb):
    slot_count = tiles_ref.shape[0]
    count = table_ref[slot_count]
    spare = sums_ref.shape[0] // BLOCK - 1
    group = 16

    def visit(step, carry):
        added = []
        for g in range(group):
            t = step * group + g
            slot = table_ref[t]
            local_row = slot // cb
            local_col = slot - local_row * cb
            source, target = (
                (local_col, local_row) if forward else (local_row, local_col)
            )
            tile = tiles_ref[t]
            target = jnp.where(t < count, target, spare)
            parts = parts_ref[pl.ds(pl.multiple_of(source * 192, 64), 192), :]
            dims = (((1,), (1 if forward else 0,)), ((), ()))
            value = lax.dot_general(
                parts, tile, dims, preferred_element_type=jnp.float32
            )
            added.append((target, value[:64] + value[64:128] + value[128:]))
        for target, value in added:
            where = pl.ds(pl.multiple_of(target * 64, 64), 64)
            sums_ref[where, :] += value
        return carry

    lax.fori_loop(0, (count + group - 1) // group, visit, 0)


def add_gram(gram, value):
    same, cross = gram
    high, middle, low = split_three(value)
    dims = (((1,), (1,)), ((), ()))
    same += lax.dot_general(
        jnp.concatenate([high, middle], axis=1), jnp.concatenate([high, middle], axis=1), dims,
        preferred_element_type=jnp.float32,
    )
    cross += lax.dot_general(
        jnp.concatenate([high, high], axis=1), jnp.concatenate([middle, low], axis=1), dims,
        preferred_element_type=jnp.float32,
    )
    return same, cross


def no_gram():
    return (jnp.zeros((BLOCK, BLOCK), jnp.float32),) * 2


def whole_gram(gram):
    same, cross = gram
    return same + cross + jnp.transpose(cross)


def send_panel(
    table_ref, tiles_ref, panel_ref, scale_ref, sent_ref, parts_ref, sums_ref, *, forward, cb, ready=None
):
    sums_ref[...] = jnp.zeros_like(sums_ref)
    gram = no_gram()
    for b in range(panel_ref.shape[0] // BLOCK):
        value = panel_ref[64 * b : 64 * b + 64, :]
        gram = add_gram(gram, value)
        parts_ref[192 * b : 192 * b + 192, :] = jnp.concatenate(
            split_three(value * scale_ref[b : b + 1, :]), axis=0
        )
    if ready is not None:
        ready.wait()
    product(table_ref, tiles_ref, parts_ref, sums_ref, forward, cb)
    packed = pack_gram(whole_gram(gram))
    if not forward:
        cross = packed[HALF_ROWS:]
        packed = jnp.where(
            table_ref[tiles_ref.shape[0] + 1] == 0, packed[:HALF_ROWS], jnp.concatenate([cross, cross], axis=0)
        )
    count = sent_ref.shape[0]
    rows = (sums_ref.shape[0] - BLOCK) // count
    for k in range(count):
        sent_ref[k, :rows, :] = sums_ref[rows * k : rows * k + rows, :]
        sent_ref[k, rows:, :] = packed


def unit_rows(unit, rows):
    for piece in range(BLOCK // 16):
        at = BLOCK * unit + 16 * piece
        yield at % rows, UNIT * (at // rows)


def pack_kernel(panel_ref, out_ref):
    rows = out_ref.shape[1]
    columns = [[] for _ in range(TILE // UNIT)]
    for unit in range(panel_ref.shape[1] // UNIT):
        value = panel_ref[:, UNIT * unit : UNIT * unit + UNIT]
        for piece, (_, lane) in enumerate(unit_rows(unit, rows)):
            columns[lane // UNIT].append(value[16 * piece : 16 * piece + 16])
    packed = jnp.concatenate(
        [jnp.concatenate(pieces, axis=0) for pieces in columns], axis=1
    )
    for k in range(out_ref.shape[0]):
        out_ref[k] = packed


def start_kernel(
    table_ref, tiles_ref, got_ref, scale_ref, panel_ref, sent_ref,
    parts_ref, sums_ref, near_tiles_ref, sem, *, cb, units,
):
    copy = pltpu.make_async_copy(tiles_ref, near_tiles_ref, sem)
    copy.start()
    rows = got_ref.shape[1]
    for b in range(cb):
        found = []
        for c in range(TILE // UNIT):
            device, unit = divmod(TILE // UNIT * b + c, units)
            found.append(
                [
                    got_ref[device, row : row + 16, lane : lane + UNIT]
                    for row, lane in unit_rows(unit, rows)
                ]
            )
        for piece in range(BLOCK // 16):
            panel_ref[64 * b + 16 * piece : 64 * b + 16 * piece + 16, :] = (
                jnp.concatenate([pieces[piece] for pieces in found], axis=1)
            )
    send_panel(
        table_ref, near_tiles_ref, panel_ref, scale_ref, sent_ref, parts_ref, sums_ref,
        forward=True, cb=cb, ready=copy,
    )


def fold_kernel(got_ref, out_ref, *rest):
    rows = out_ref.shape[-2]
    total = got_ref[0, :rows, :]
    for k in range(1, got_ref.shape[0]):
        total += got_ref[k, :rows, :]
    for k in range(out_ref.shape[0]):
        out_ref[k] = total
    if rest:
        other = got_ref[0, rows:, :]
        for k in range(1, got_ref.shape[0]):
            other += got_ref[k, rows:, :]
        rest[0][...] = other


def sum_gram(got_ref):
    packed = got_ref[0, -GRAM_ROWS:, :]
    for k in range(1, got_ref.shape[0]):
        packed += got_ref[k, -GRAM_ROWS:, :]
    return unpack_gram(packed)


def join_gram(table_ref, own_ref, other_ref):
    first = table_ref[table_ref.shape[0] - 1] == 0
    own, other = own_ref[...], other_ref[...]
    return unpack_gram(
        jnp.concatenate(
            [
                jnp.where(first, own, other),
                jnp.where(first, other, own)[: GRAM_ROWS - HALF_ROWS],
            ],
            axis=0,
        )
    )


def lower_factor(factor_ref):
    lower = jnp.transpose(factor_ref[:, :BLOCK])
    mask = lax.broadcasted_iota(
        jnp.int32, (BLOCK, BLOCK), 0
    ) >= lax.broadcasted_iota(jnp.int32, (BLOCK, BLOCK), 1)
    return jnp.where(mask, lower, 0.0)


def factor_kernel(*refs, with_old, halves):
    refs = list(refs)
    if halves:
        gram, refs = join_gram(*refs[:3]), refs[3:]
    else:
        gram, refs = sum_gram(refs[0]), refs[1:]
    if not with_old:
        factor_rows(gram, refs[0])
        return
    old_ref, old_factor_ref, factor_ref, part_ref, lower_ref = refs
    factor_rows(gram, factor_ref)
    lower_ref[...] = lower_factor(factor_ref)
    upper_mask = lax.broadcasted_iota(
        jnp.int32, (BLOCK, BLOCK), 0
    ) <= lax.broadcasted_iota(jnp.int32, (BLOCK, BLOCK), 1)
    upper = jnp.where(upper_mask, factor_ref[:, :BLOCK], 0.0)
    back = jnp.dot(
        upper, -old_factor_ref[:, BLOCK:], precision=HIGH,
        preferred_element_type=jnp.float32,
    )
    for b in range(old_ref.shape[0] // BLOCK):
        part_ref[64 * b : 64 * b + 64, :] = jnp.dot(
            back, old_ref[64 * b : 64 * b + 64, :], precision=HIGH,
            preferred_element_type=jnp.float32,
        )


def step_kernel(*refs, forward, cb, with_old, last):
    refs = list(refs)
    tables = []
    if not last:
        tables, refs = refs[:2], refs[2:]
    got_ref, scale_ref, factor_ref = refs[:3]
    refs = refs[3:]
    if with_old:
        part_ref, refs = refs[0], refs[1:]
    panel_ref, sent_ref = refs[:2]
    inverse = split_three(factor_ref[:, BLOCK:])
    gram = no_gram()
    for b in range(panel_ref.shape[0] // BLOCK):
        where = slice(64 * b, 64 * b + 64)
        value = exact_dot(
            inverse, split_three(got_ref[where, :] * scale_ref[b : b + 1, :])
        )
        if with_old:
            value += part_ref[where, :]
        panel_ref[where, :] = value
        if last:
            gram = add_gram(gram, value)
    if last:
        packed = pack_gram(whole_gram(gram))
        for k in range(sent_ref.shape[0]):
            sent_ref[k] = packed
    else:
        send_panel(
            *tables, panel_ref, scale_ref, sent_ref, refs[2], refs[3],
            forward=forward, cb=cb,
        )


def end_kernel(
    got_ref, right_ref, left_ref, left_factor_ref, first_ref, second_ref,
    out_right_ref, out_left_ref, lower_ref, factor_ref, *, left_size, right_size,
):
    lower_ref[0] = first_ref[...]
    lower_ref[1] = second_ref[...]
    factor_rows(sum_gram(got_ref), factor_ref)
    lower_ref[2] = lower_factor(factor_ref)
    out_right_ref[...] = math.sqrt(right_size) * jnp.dot(
        factor_ref[:, BLOCK:], right_ref[...], precision=HIGH,
        preferred_element_type=jnp.float32,
    )
    out_left_ref[...] = math.sqrt(left_size) * jnp.dot(
        left_factor_ref[:, BLOCK:], left_ref[...], precision=HIGH,
        preferred_element_type=jnp.float32,
    )


SMEM = pl.BlockSpec(memory_space=pltpu.SMEM)
VMEM = pl.BlockSpec(memory_space=pltpu.VMEM)
PARAMS = pltpu.CompilerParams(vmem_limit_bytes=8 * 1024 * 1024)


def f32(*shape):
    return jax.ShapeDtypeStruct(shape, jnp.float32)


def fold(got, copies, rows, rest=False):
    shapes = [f32(copies, rows, TILE)]
    if rest:
        shapes.append(f32(got.shape[1] - rows, TILE))
    return pl.pallas_call(
        fold_kernel,
        out_shape=shapes,
        in_specs=[VMEM],
        out_specs=[VMEM] * len(shapes),
        compiler_params=PARAMS,
        name="fold",
    )(got)


def exchange(messages, axes):
    return lax.all_to_all(messages, axes, 0, 0, tiled=True)


def sum_col(sent):
    near = lax.axis_size(NEAR)
    own = fold(exchange(sent, NEAR), 1, sent.shape[1])[0][0]
    got = lax.all_gather(own, "zh", axis=0, tiled=False)
    rows = sent.shape[1] - GRAM_ROWS
    line = lax.axis_size("x")
    half = exchange(fold(got, line, rows)[0], "x").reshape(line * rows, TILE)
    return [got], lax.all_gather(half, "core", axis=0, tiled=True)


def sum_row(sent, table):
    count = lax.axis_size(ROW)
    rows = sent.shape[1] - HALF_ROWS
    copies, own = fold(exchange(sent, ROW), count, rows, rest=True)
    whole = exchange(copies, ROW).reshape(count * rows, TILE)
    other = lax.ppermute(own, "core", [(0, 1), (1, 0)])
    return [table, own, other], whole


def per_device(tiles, tile_slots, tile_counts, user_degree, item_degree, start_panel):
    tile_stack = tiles[0, 0]
    rb = user_degree.shape[0] // TILE
    cb = item_degree.shape[0] // TILE
    rows = lax.axis_size(ROW)
    cols = lax.axis_size(COL)
    near = lax.axis_size(NEAR)
    core = lax.axis_index("core").astype(jnp.int32).reshape(1)
    table = jnp.concatenate([tile_slots[0, 0], tile_counts[0], core])
    user_scale = lax.rsqrt(user_degree.astype(jnp.float32)).reshape(rb, TILE)
    item_scale = lax.rsqrt(item_degree.astype(jnp.float32)).reshape(cb, TILE)

    units = start_panel.shape[1] // UNIT
    start = pl.pallas_call(
        pack_kernel,
        out_shape=f32(rows, BLOCK * units * UNIT // TILE, TILE),
        in_specs=[VMEM],
        out_specs=VMEM,
        compiler_params=PARAMS,
        name="pack",
    )(start_panel)
    start = exchange(start, ROW)

    user_messages = f32(near, rb * BLOCK // near + GRAM_ROWS, TILE)
    item_messages = f32(rows, cb * BLOCK // rows + HALF_ROWS, TILE)
    user_sums = pltpu.VMEM((rb * BLOCK + BLOCK, TILE), jnp.float32)
    item_sums = pltpu.VMEM((cb * BLOCK + BLOCK, TILE), jnp.float32)
    user_parts = pltpu.VMEM((rb * 192, TILE), jnp.bfloat16)
    item_parts = pltpu.VMEM((cb * 192, TILE), jnp.bfloat16)
    start, sent = pl.pallas_call(
        functools.partial(start_kernel, cb=cb, units=units),
        out_shape=[f32(cb * BLOCK, TILE), user_messages],
        in_specs=[SMEM, pl.BlockSpec(memory_space=pltpu.HBM), VMEM, VMEM],
        out_specs=[VMEM, VMEM],
        scratch_shapes=[
            item_parts,
            user_sums,
            pltpu.VMEM(tile_stack.shape, tile_stack.dtype),
            pltpu.SemaphoreType.DMA,
        ],
        compiler_params=PARAMS,
        name="start",
    )(table, tile_stack, start, item_scale)

    panels = [start]
    factors = []
    lower = []
    for half in range(1, 2 * STEPS + 1):
        users = half % 2 == 1
        last = half == 2 * STEPS
        with_old = half > 1
        gram, whole = sum_col(sent) if users else sum_row(sent, table)
        panel_shape = f32((rb if users else cb) * BLOCK, TILE)
        old = [panels[half - 2], factors[half - 2]] if with_old else []
        factored = pl.pallas_call(
            functools.partial(factor_kernel, with_old=with_old, halves=not users),
            out_shape=[f32(BLOCK, 2 * BLOCK)]
            + ([panel_shape, f32(BLOCK, BLOCK)] if with_old else []),
            in_specs=([VMEM] if users else [SMEM, VMEM, VMEM]) + [VMEM] * len(old),
            out_specs=[VMEM] * (3 if with_old else 1),
            compiler_params=PARAMS,
            name=f"factor{half}",
        )(*gram, *old)
        factors.append(factored[0])
        lower += factored[2:]
        tables = [] if last else [table, tile_stack]
        table_specs = [] if last else [SMEM, VMEM]
        operands = [whole, user_scale if users else item_scale, *factored[:2]]
        panel, sent = pl.pallas_call(
            functools.partial(
                step_kernel, forward=not users, cb=cb, with_old=with_old, last=last
            ),
            out_shape=[
                panel_shape,
                f32(near, GRAM_ROWS, TILE)
                if last
                else (item_messages if users else user_messages),
            ],
            in_specs=table_specs + [VMEM] * len(operands),
            out_specs=[VMEM, VMEM],
            scratch_shapes=[]
            if last
            else ([user_parts, item_sums] if users else [item_parts, user_sums]),
            compiler_params=PARAMS,
            name=f"half{half}",
        )(*tables, *operands)
        panels.append(panel)

    gram = fold(exchange(sent, NEAR), lax.axis_size("zh"), GRAM_ROWS)[0]
    gram = exchange(gram, "zh")

    user_group = rb * TILE // cols
    item_group = cb * TILE // rows
    left = jnp.transpose(panels[-2].reshape(rb, BLOCK, TILE), (1, 0, 2))
    left = lax.dynamic_slice_in_dim(
        left.reshape(BLOCK, rb * TILE), lax.axis_index(COL) * user_group, user_group, 1
    )
    right = jnp.transpose(panels[-1].reshape(cb, BLOCK, TILE), (1, 0, 2))
    right = lax.dynamic_slice_in_dim(
        right.reshape(BLOCK, cb * TILE), lax.axis_index(ROW) * item_group, item_group, 1
    )
    right_panel, left_panel, right_factors = pl.pallas_call(
        functools.partial(
            end_kernel, left_size=rb * TILE * rows, right_size=cb * TILE * cols
        ),
        out_shape=[
            f32(BLOCK, item_group),
            f32(BLOCK, user_group),
            f32(STEPS, BLOCK, BLOCK),
        ],
        in_specs=[VMEM] * 6,
        out_specs=[VMEM] * 3,
        scratch_shapes=[pltpu.VMEM((BLOCK, 2 * BLOCK), jnp.float32)],
        compiler_params=PARAMS,
        name="end",
    )(gram, right, left, factors[-1], lower[1], lower[3])
    return left_panel, right_panel, jnp.stack(lower[::2]), right_factors


def solution(mesh):
    split = Mesh(mesh.devices.reshape(4, 4, 4, 4, 2), ROW + COL)
    in_specs = (
        P(ROW, COL, None, None, None),
        P(ROW, COL, None),
        P(ROW, COL),
        P(ROW),
        P(COL),
        P(None, COL + ROW),
    )
    out_specs = (P(None, ROW + COL), P(None, COL + ROW), P(), P())
    return jax.shard_map(
        per_device, mesh=split, in_specs=in_specs, out_specs=out_specs, check_vma=False
    )
```

```python
import functools
import math

import jax
import jax.numpy as jnp
from jax import lax
from jax.experimental import pallas as pl
from jax.experimental.pallas import tpu as pltpu
from jax.sharding import Mesh
from jax.sharding import PartitionSpec as P

STEPS = 3
TILE = 128
BLOCK = 64
GRAM_ROWS = 24
HALF_ROWS = 16
UNIT = 32
HIGH = lax.Precision.HIGHEST

ROW = ("zl", "y")
COL = ("x", "zh", "core")
NEAR = ("core", "x")


def pack_gram(gram):
    half = BLOCK // 2

    def rows(block):
        return jnp.concatenate([block[8 * i : 8 * i + 8] for i in range(4)], axis=1)

    return jnp.concatenate(
        [
            rows(gram[:half, :half]),
            rows(gram[half:, half:]),
            rows(gram[half:, :half]),
        ],
        axis=0,
    )


def unpack_gram(packed):
    half = BLOCK // 2

    def block(rows):
        return jnp.concatenate(
            [rows[:, half * i : half * i + half] for i in range(4)], axis=0
        )

    upper, lower, cross = (block(packed[8 * i : 8 * i + 8]) for i in range(3))
    return jnp.concatenate(
        [
            jnp.concatenate([upper, jnp.transpose(cross)], axis=1),
            jnp.concatenate([cross, lower], axis=1),
        ],
        axis=0,
    )


def factor_rows(gram, out_ref):
    eye = (
        lax.broadcasted_iota(jnp.int32, (BLOCK, BLOCK), 0)
        == lax.broadcasted_iota(jnp.int32, (BLOCK, BLOCK), 1)
    ).astype(jnp.float32)
    whole = jnp.concatenate([gram, eye], axis=1)
    groups = [whole[8 * i : 8 * i + 8] for i in range(BLOCK // 8)]
    for first in range(BLOCK // 8):
        base = 8 * first
        below = range(first, BLOCK // 8)
        spread = {
            i: [
                jnp.broadcast_to(groups[i][:, base + m : base + m + 1], groups[i].shape)
                for m in range(8)
            ]
            for i in below
        }
        for k in range(8):
            root = lax.rsqrt(spread[first][k][k : k + 1])
            scaled = groups[first][k : k + 1] * root
            out_ref[base + k : base + k + 1, :] = scaled
            across = {m: spread[first][m][k : k + 1] * root for m in range(k + 1, 8)}
            for i in below:
                times = spread[i][k] * root
                groups[i] = groups[i] - times * scaled
                for m in across:
                    spread[i][m] = spread[i][m] - times * across[m]


def split_three(value):
    high = value.astype(jnp.bfloat16)
    rest = value - high.astype(jnp.float32)
    middle = rest.astype(jnp.bfloat16)
    low = (rest - middle.astype(jnp.float32)).astype(jnp.bfloat16)
    return high, middle, low


def exact_dot(left, right):
    high, middle, low = left
    first = jnp.concatenate([high, high, middle, high, middle, low], axis=1)
    high, middle, low = right
    second = jnp.concatenate([high, middle, high, low, middle, high], axis=0)
    return jnp.dot(first, second, preferred_element_type=jnp.float32)


def product(table_ref, tiles_ref, parts_ref, sums_ref, forward, cb):
    slot_count = tiles_ref.shape[0]
    count = table_ref[slot_count]
    spare = sums_ref.shape[0] // BLOCK - 1
    group = 16

    def visit(step, carry):
        added = []
        for g in range(group):
            t = step * group + g
            slot = table_ref[t]
            local_row = slot // cb
            local_col = slot - local_row * cb
            source, target = (
                (local_col, local_row) if forward else (local_row, local_col)
            )
            tile = tiles_ref[t]
            target = jnp.where(t < count, target, spare)
            parts = parts_ref[pl.ds(pl.multiple_of(source * 192, 64), 192), :]
            dims = (((1,), (1 if forward else 0,)), ((), ()))
            value = lax.dot_general(
                parts, tile, dims, preferred_element_type=jnp.float32
            )
            added.append((target, value[:64] + value[64:128] + value[128:]))
        for target, value in added:
            where = pl.ds(pl.multiple_of(target * 64, 64), 64)
            sums_ref[where, :] += value
        return carry

    lax.fori_loop(0, (count + group - 1) // group, visit, 0)


def add_gram(gram, value):
    same, cross = gram
    high, middle, low = split_three(value)
    dims = (((1,), (1,)), ((), ()))
    same += lax.dot_general(
        jnp.concatenate([high, middle], axis=1), jnp.concatenate([high, middle], axis=1), dims,
        preferred_element_type=jnp.float32,
    )
    cross += lax.dot_general(
        jnp.concatenate([high, high], axis=1), jnp.concatenate([middle, low], axis=1), dims,
        preferred_element_type=jnp.float32,
    )
    return same, cross


def no_gram():
    return (jnp.zeros((BLOCK, BLOCK), jnp.float32),) * 2


def whole_gram(gram):
    same, cross = gram
    return same + cross + jnp.transpose(cross)


def send_panel(
    table_ref, tiles_ref, panel_ref, scale_ref, sent_ref, parts_ref, sums_ref, *, forward, cb, ready=None
):
    sums_ref[...] = jnp.zeros_like(sums_ref)
    gram = no_gram()
    for b in range(panel_ref.shape[0] // BLOCK):
        value = panel_ref[64 * b : 64 * b + 64, :]
        gram = add_gram(gram, value)
        parts_ref[192 * b : 192 * b + 192, :] = jnp.concatenate(
            split_three(value * scale_ref[b : b + 1, :]), axis=0
        )
    if ready is not None:
        ready.wait()
    product(table_ref, tiles_ref, parts_ref, sums_ref, forward, cb)
    packed = pack_gram(whole_gram(gram))
    if not forward:
        cross = packed[HALF_ROWS:]
        packed = jnp.where(
            table_ref[tiles_ref.shape[0] + 1] == 0, packed[:HALF_ROWS], jnp.concatenate([cross, cross], axis=0)
        )
    count = sent_ref.shape[0]
    rows = (sums_ref.shape[0] - BLOCK) // count
    for k in range(count):
        sent_ref[k, :rows, :] = sums_ref[rows * k : rows * k + rows, :]
        sent_ref[k, rows:, :] = packed


def unit_rows(unit, rows):
    for piece in range(BLOCK // 16):
        at = BLOCK * unit + 16 * piece
        yield at % rows, UNIT * (at // rows)


def pack_kernel(panel_ref, out_ref):
    rows = out_ref.shape[1]
    columns = [[] for _ in range(TILE // UNIT)]
    for unit in range(panel_ref.shape[1] // UNIT):
        value = panel_ref[:, UNIT * unit : UNIT * unit + UNIT]
        for piece, (_, lane) in enumerate(unit_rows(unit, rows)):
            columns[lane // UNIT].append(value[16 * piece : 16 * piece + 16])
    packed = jnp.concatenate(
        [jnp.concatenate(pieces, axis=0) for pieces in columns], axis=1
    )
    for k in range(out_ref.shape[0]):
        out_ref[k] = packed


def start_kernel(
    table_ref, tiles_ref, got_ref, scale_ref, panel_ref, sent_ref,
    parts_ref, sums_ref, near_tiles_ref, sem, *, cb, units,
):
    copy = pltpu.make_async_copy(tiles_ref, near_tiles_ref, sem)
    copy.start()
    rows = got_ref.shape[1]
    for b in range(cb):
        found = []
        for c in range(TILE // UNIT):
            device, unit = divmod(TILE // UNIT * b + c, units)
            found.append(
                [
                    got_ref[device, row : row + 16, lane : lane + UNIT]
                    for row, lane in unit_rows(unit, rows)
                ]
            )
        for piece in range(BLOCK // 16):
            panel_ref[64 * b + 16 * piece : 64 * b + 16 * piece + 16, :] = (
                jnp.concatenate([pieces[piece] for pieces in found], axis=1)
            )
    send_panel(
        table_ref, near_tiles_ref, panel_ref, scale_ref, sent_ref, parts_ref, sums_ref,
        forward=True, cb=cb, ready=copy,
    )


def fold_kernel(got_ref, out_ref, *rest):
    rows = out_ref.shape[-2]
    total = got_ref[0, :rows, :]
    for k in range(1, got_ref.shape[0]):
        total += got_ref[k, :rows, :]
    for k in range(out_ref.shape[0]):
        out_ref[k] = total
    if rest:
        other = got_ref[0, rows:, :]
        for k in range(1, got_ref.shape[0]):
            other += got_ref[k, rows:, :]
        rest[0][...] = other


def sum_gram(got_ref):
    packed = got_ref[0, -GRAM_ROWS:, :]
    for k in range(1, got_ref.shape[0]):
        packed += got_ref[k, -GRAM_ROWS:, :]
    return unpack_gram(packed)


def join_gram(table_ref, own_ref, other_ref):
    first = table_ref[table_ref.shape[0] - 2] == 0
    own, other = own_ref[...], other_ref[...]
    return unpack_gram(
        jnp.concatenate(
            [
                jnp.where(first, own, other),
                jnp.where(first, other, own)[: GRAM_ROWS - HALF_ROWS],
            ],
            axis=0,
        )
    )


def lower_factor(factor_ref):
    lower = jnp.transpose(factor_ref[:, :BLOCK])
    mask = lax.broadcasted_iota(
        jnp.int32, (BLOCK, BLOCK), 0
    ) >= lax.broadcasted_iota(jnp.int32, (BLOCK, BLOCK), 1)
    return jnp.where(mask, lower, 0.0)


def factor_kernel(*refs, with_old, halves, left_size=None):
    refs = list(refs)
    if halves:
        gram, refs = join_gram(*refs[:3]), refs[3:]
    else:
        gram, refs = sum_gram(refs[0]), refs[1:]
    if not with_old:
        factor_rows(gram, refs[0])
        return
    old_ref, old_factor_ref = refs[:2]
    if left_size is None:
        factor_ref, part_ref, lower_ref = refs[2:]
        factor_rows(gram, factor_ref)
        lower_ref[...] = lower_factor(factor_ref)
    else:
        left_ref, first_ref, second_ref, factor_ref, part_ref, lower_ref, out_ref = refs[2:]
        factor_rows(gram, factor_ref)
        lower_ref[0] = first_ref[...]
        lower_ref[1] = second_ref[...]
        lower_ref[2] = lower_factor(factor_ref)
        out_ref[...] = math.sqrt(left_size) * jnp.dot(
            factor_ref[:, BLOCK:], left_ref[...], precision=HIGH,
            preferred_element_type=jnp.float32,
        )
    upper_mask = lax.broadcasted_iota(
        jnp.int32, (BLOCK, BLOCK), 0
    ) <= lax.broadcasted_iota(jnp.int32, (BLOCK, BLOCK), 1)
    upper = jnp.where(upper_mask, factor_ref[:, :BLOCK], 0.0)
    back = jnp.dot(
        upper, -old_factor_ref[:, BLOCK:], precision=HIGH,
        preferred_element_type=jnp.float32,
    )
    for b in range(old_ref.shape[0] // BLOCK):
        part_ref[64 * b : 64 * b + 64, :] = jnp.dot(
            back, old_ref[64 * b : 64 * b + 64, :], precision=HIGH,
            preferred_element_type=jnp.float32,
        )


def step_kernel(*refs, forward, cb, with_old, last):
    refs = list(refs)
    tables = []
    if not last:
        tables, refs = refs[:2], refs[2:]
    got_ref, scale_ref, factor_ref = refs[:3]
    refs = refs[3:]
    if with_old:
        part_ref, refs = refs[0], refs[1:]
    panel_ref, sent_ref = refs[:2]
    inverse = split_three(factor_ref[:, BLOCK:])
    gram = no_gram()
    for b in range(panel_ref.shape[0] // BLOCK):
        where = slice(64 * b, 64 * b + 64)
        value = exact_dot(
            inverse, split_three(got_ref[where, :] * scale_ref[b : b + 1, :])
        )
        if with_old:
            value += part_ref[where, :]
        panel_ref[where, :] = value
        if last:
            gram = add_gram(gram, value)
    if last:
        packed = pack_gram(whole_gram(gram))
        for k in range(sent_ref.shape[0]):
            sent_ref[k] = packed
    else:
        send_panel(
            *tables, panel_ref, scale_ref, sent_ref, refs[2], refs[3],
            forward=forward, cb=cb,
        )


def end_kernel(
    table_ref, got_ref, panel_ref, first_ref, second_ref, out_ref, lower_ref, factor_ref, *, right_size
):
    lower_ref[0] = first_ref[...]
    lower_ref[1] = second_ref[...]
    factor_rows(sum_gram(got_ref), factor_ref)
    lower_ref[2] = lower_factor(factor_ref)
    width = out_ref.shape[1]
    unit = (width // UNIT) * table_ref[table_ref.shape[0] - 1]
    block = unit // (TILE // UNIT)
    after = jnp.minimum(block + 1, panel_ref.shape[0] // BLOCK - 1)
    wide = jnp.concatenate(
        [
            panel_ref[pl.ds(pl.multiple_of(BLOCK * b, BLOCK), BLOCK), :]
            for b in (block, after)
        ],
        axis=1,
    )
    own = wide[:, :width]
    for k in range(1, TILE // UNIT):
        own = jnp.where(
            unit % (TILE // UNIT) == k, wide[:, UNIT * k : UNIT * k + width], own
        )
    out_ref[...] = math.sqrt(right_size) * jnp.dot(
        factor_ref[:, BLOCK:], own, precision=HIGH, preferred_element_type=jnp.float32
    )


SMEM = pl.BlockSpec(memory_space=pltpu.SMEM)
VMEM = pl.BlockSpec(memory_space=pltpu.VMEM)
PARAMS = pltpu.CompilerParams(vmem_limit_bytes=8 * 1024 * 1024)


def f32(*shape):
    return jax.ShapeDtypeStruct(shape, jnp.float32)


def fold(got, copies, rows, rest=False):
    shapes = [f32(copies, rows, TILE)]
    if rest:
        shapes.append(f32(got.shape[1] - rows, TILE))
    return pl.pallas_call(
        fold_kernel,
        out_shape=shapes,
        in_specs=[VMEM],
        out_specs=[VMEM] * len(shapes),
        compiler_params=PARAMS,
        name="fold",
    )(got)


def exchange(messages, axes):
    return lax.all_to_all(messages, axes, 0, 0, tiled=True)


def sum_col(sent):
    near = lax.axis_size(NEAR)
    own = fold(exchange(sent, NEAR), 1, sent.shape[1])[0][0]
    got = lax.all_gather(own, "zh", axis=0, tiled=False)
    rows = sent.shape[1] - GRAM_ROWS
    line = lax.axis_size("x")
    half = exchange(fold(got, line, rows)[0], "x").reshape(line * rows, TILE)
    return [got], lax.all_gather(half, "core", axis=0, tiled=True)


def sum_row(sent, table):
    count = lax.axis_size(ROW)
    rows = sent.shape[1] - HALF_ROWS
    copies, own = fold(exchange(sent, ROW), count, rows, rest=True)
    whole = exchange(copies, ROW).reshape(count * rows, TILE)
    other = lax.ppermute(own, "core", [(0, 1), (1, 0)])
    return [table, own, other], whole


def left_chunk(panel, blocks):
    group = blocks * TILE // lax.axis_size(COL)
    flat = jnp.transpose(panel.reshape(blocks, BLOCK, TILE), (1, 0, 2))
    flat = flat.reshape(BLOCK, blocks * TILE)
    return lax.dynamic_slice_in_dim(flat, lax.axis_index(COL) * group, group, 1)


def per_device(tiles, tile_slots, tile_counts, user_degree, item_degree, start_panel):
    tile_stack = tiles[0, 0]
    rb = user_degree.shape[0] // TILE
    cb = item_degree.shape[0] // TILE
    rows = lax.axis_size(ROW)
    near = lax.axis_size(NEAR)
    core = lax.axis_index("core").astype(jnp.int32).reshape(1)
    row = lax.axis_index(ROW).astype(jnp.int32).reshape(1)
    table = jnp.concatenate([tile_slots[0, 0], tile_counts[0], core, row])
    user_scale = lax.rsqrt(user_degree.astype(jnp.float32)).reshape(rb, TILE)
    item_scale = lax.rsqrt(item_degree.astype(jnp.float32)).reshape(cb, TILE)

    units = start_panel.shape[1] // UNIT
    start = pl.pallas_call(
        pack_kernel,
        out_shape=f32(rows, BLOCK * units * UNIT // TILE, TILE),
        in_specs=[VMEM],
        out_specs=VMEM,
        compiler_params=PARAMS,
        name="pack",
    )(start_panel)
    start = exchange(start, ROW)

    user_messages = f32(near, rb * BLOCK // near + GRAM_ROWS, TILE)
    item_messages = f32(rows, cb * BLOCK // rows + HALF_ROWS, TILE)
    user_sums = pltpu.VMEM((rb * BLOCK + BLOCK, TILE), jnp.float32)
    item_sums = pltpu.VMEM((cb * BLOCK + BLOCK, TILE), jnp.float32)
    user_parts = pltpu.VMEM((rb * 192, TILE), jnp.bfloat16)
    item_parts = pltpu.VMEM((cb * 192, TILE), jnp.bfloat16)
    start, sent = pl.pallas_call(
        functools.partial(start_kernel, cb=cb, units=units),
        out_shape=[f32(cb * BLOCK, TILE), user_messages],
        in_specs=[SMEM, pl.BlockSpec(memory_space=pltpu.HBM), VMEM, VMEM],
        out_specs=[VMEM, VMEM],
        scratch_shapes=[
            item_parts,
            user_sums,
            pltpu.VMEM(tile_stack.shape, tile_stack.dtype),
            pltpu.SemaphoreType.DMA,
        ],
        compiler_params=PARAMS,
        name="start",
    )(table, tile_stack, start, item_scale)

    panels = [start]
    factors = []
    lower = []
    for half in range(1, 2 * STEPS + 1):
        users = half % 2 == 1
        last = half == 2 * STEPS
        with_old = half > 1
        gram, whole = sum_col(sent) if users else sum_row(sent, table)
        panel_shape = f32((rb if users else cb) * BLOCK, TILE)
        old = [panels[half - 2], factors[half - 2]] if with_old else []
        finished = [left_chunk(panels[-1], rb), lower[0], lower[2]] if last else []
        shapes = [f32(BLOCK, 2 * BLOCK)]
        if with_old:
            shapes += [panel_shape, f32(*([STEPS] if last else []), BLOCK, BLOCK)]
        if last:
            shapes.append(f32(BLOCK, finished[0].shape[1]))
        factored = pl.pallas_call(
            functools.partial(
                factor_kernel, with_old=with_old, halves=not users,
                left_size=rb * TILE * rows if last else None,
            ),
            out_shape=shapes,
            in_specs=([VMEM] if users else [SMEM, VMEM, VMEM])
            + [VMEM] * len(old + finished),
            out_specs=[VMEM] * len(shapes),
            compiler_params=PARAMS,
            name=f"factor{half}",
        )(*gram, *old, *finished)
        factors.append(factored[0])
        if last:
            left_factors, left_panel = factored[2:]
        else:
            lower += factored[2:]
        tables = [] if last else [table, tile_stack]
        table_specs = [] if last else [SMEM, VMEM]
        operands = [whole, user_scale if users else item_scale, *factored[:2]]
        panel, sent = pl.pallas_call(
            functools.partial(
                step_kernel, forward=not users, cb=cb, with_old=with_old, last=last
            ),
            out_shape=[
                panel_shape,
                f32(near, GRAM_ROWS, TILE)
                if last
                else (item_messages if users else user_messages),
            ],
            in_specs=table_specs + [VMEM] * len(operands),
            out_specs=[VMEM, VMEM],
            scratch_shapes=[]
            if last
            else ([user_parts, item_sums] if users else [item_parts, user_sums]),
            compiler_params=PARAMS,
            name=f"half{half}",
        )(*tables, *operands)
        panels.append(panel)

    gram = fold(exchange(sent, NEAR), 1, GRAM_ROWS)[0][0]
    gram = lax.all_gather(gram, "zh", axis=0, tiled=False)

    right_panel, right_factors = pl.pallas_call(
        functools.partial(end_kernel, right_size=cb * TILE * lax.axis_size(COL)),
        out_shape=[f32(BLOCK, cb * TILE // rows), f32(STEPS, BLOCK, BLOCK)],
        in_specs=[SMEM] + [VMEM] * 4,
        out_specs=[VMEM] * 2,
        scratch_shapes=[pltpu.VMEM((BLOCK, 2 * BLOCK), jnp.float32)],
        compiler_params=PARAMS,
        name="end",
    )(table, gram, panels[-1], lower[1], lower[3])
    return left_panel, right_panel, left_factors, right_factors


def solution(mesh):
    split = Mesh(mesh.devices.reshape(4, 4, 4, 4, 2), ROW + COL)
    in_specs = (
        P(ROW, COL, None, None, None),
        P(ROW, COL, None),
        P(ROW, COL),
        P(ROW),
        P(COL),
        P(None, COL + ROW),
    )
    out_specs = (P(None, ROW + COL), P(None, COL + ROW), P(), P())
    return jax.shard_map(
        per_device, mesh=split, in_specs=in_specs, out_specs=out_specs, check_vma=False
    )
```

```python
import functools
import math

import jax
import jax.numpy as jnp
from jax import lax
from jax.experimental import pallas as pl
from jax.experimental.pallas import tpu as pltpu
from jax.sharding import Mesh
from jax.sharding import PartitionSpec as P

STEPS = 3
TILE = 128
BLOCK = 64
GRAM_ROWS = 24
HALF_ROWS = 16
UNIT = 32
HIGH = lax.Precision.HIGHEST

ROW = ("zl", "y")
COL = ("x", "zh", "core")
NEAR = ("core", "x")
FLAT = ("core", "y", "x")
LINE = ("zh", "zl")


def pack_gram(gram):
    half = BLOCK // 2

    def rows(block):
        return jnp.concatenate([block[8 * i : 8 * i + 8] for i in range(4)], axis=1)

    return jnp.concatenate(
        [
            rows(gram[:half, :half]),
            rows(gram[half:, half:]),
            rows(gram[half:, :half]),
        ],
        axis=0,
    )


def unpack_gram(packed):
    half = BLOCK // 2

    def block(rows):
        return jnp.concatenate(
            [rows[:, half * i : half * i + half] for i in range(4)], axis=0
        )

    upper, lower, cross = (block(packed[8 * i : 8 * i + 8]) for i in range(3))
    return jnp.concatenate(
        [
            jnp.concatenate([upper, jnp.transpose(cross)], axis=1),
            jnp.concatenate([cross, lower], axis=1),
        ],
        axis=0,
    )


def factor_rows(gram, out_ref):
    eye = (
        lax.broadcasted_iota(jnp.int32, (BLOCK, BLOCK), 0)
        == lax.broadcasted_iota(jnp.int32, (BLOCK, BLOCK), 1)
    ).astype(jnp.float32)
    whole = jnp.concatenate([gram, eye], axis=1)
    groups = [whole[8 * i : 8 * i + 8] for i in range(BLOCK // 8)]
    for first in range(BLOCK // 8):
        base = 8 * first
        below = range(first, BLOCK // 8)
        spread = {
            i: [
                jnp.broadcast_to(groups[i][:, base + m : base + m + 1], groups[i].shape)
                for m in range(8)
            ]
            for i in below
        }
        for k in range(8):
            root = lax.rsqrt(spread[first][k][k : k + 1])
            scaled = groups[first][k : k + 1] * root
            out_ref[base + k : base + k + 1, :] = scaled
            across = {m: spread[first][m][k : k + 1] * root for m in range(k + 1, 8)}
            for i in below:
                times = spread[i][k] * root
                groups[i] = groups[i] - times * scaled
                for m in across:
                    spread[i][m] = spread[i][m] - times * across[m]


def split_three(value):
    high = value.astype(jnp.bfloat16)
    rest = value - high.astype(jnp.float32)
    middle = rest.astype(jnp.bfloat16)
    low = (rest - middle.astype(jnp.float32)).astype(jnp.bfloat16)
    return high, middle, low


def exact_dot(left, right):
    high, middle, low = left
    first = jnp.concatenate([high, high, middle, high, middle, low], axis=1)
    high, middle, low = right
    second = jnp.concatenate([high, middle, high, low, middle, high], axis=0)
    return jnp.dot(first, second, preferred_element_type=jnp.float32)


def product(table_ref, tiles_ref, parts_ref, sums_ref, forward, cb):
    slot_count = tiles_ref.shape[0]
    count = table_ref[slot_count]
    spare = sums_ref.shape[0] // BLOCK - 1
    group = 16

    def visit(step, carry):
        added = []
        for g in range(group):
            t = step * group + g
            slot = table_ref[t]
            local_row = slot // cb
            local_col = slot - local_row * cb
            source, target = (
                (local_col, local_row) if forward else (local_row, local_col)
            )
            tile = tiles_ref[t]
            target = jnp.where(t < count, target, spare)
            parts = parts_ref[pl.ds(pl.multiple_of(source * 192, 64), 192), :]
            dims = (((1,), (1 if forward else 0,)), ((), ()))
            value = lax.dot_general(
                parts, tile, dims, preferred_element_type=jnp.float32
            )
            added.append((target, value[:64] + value[64:128] + value[128:]))
        for target, value in added:
            where = pl.ds(pl.multiple_of(target * 64, 64), 64)
            sums_ref[where, :] += value
        return carry

    lax.fori_loop(0, (count + group - 1) // group, visit, 0)


def add_gram(gram, value):
    same, cross = gram
    high, middle, low = split_three(value)
    dims = (((1,), (1,)), ((), ()))
    same += lax.dot_general(
        jnp.concatenate([high, middle], axis=1), jnp.concatenate([high, middle], axis=1), dims,
        preferred_element_type=jnp.float32,
    )
    cross += lax.dot_general(
        jnp.concatenate([high, high], axis=1), jnp.concatenate([middle, low], axis=1), dims,
        preferred_element_type=jnp.float32,
    )
    return same, cross


def no_gram():
    return (jnp.zeros((BLOCK, BLOCK), jnp.float32),) * 2


def whole_gram(gram):
    same, cross = gram
    return same + cross + jnp.transpose(cross)


def send_panel(
    table_ref, tiles_ref, panel_ref, scale_ref, sent_ref, parts_ref, sums_ref, *, forward, cb, ready=None,
    owned=False,
):
    sums_ref[...] = jnp.zeros_like(sums_ref)
    gram = no_gram()
    for b in range(panel_ref.shape[0] // BLOCK):
        value = panel_ref[64 * b : 64 * b + 64, :]
        gram = add_gram(gram, value)
        parts_ref[192 * b : 192 * b + 192, :] = jnp.concatenate(
            split_three(value * scale_ref[b : b + 1, :]), axis=0
        )
    if ready is not None:
        ready.wait()
    product(table_ref, tiles_ref, parts_ref, sums_ref, forward, cb)
    packed = pack_gram(whole_gram(gram))
    if not (forward or owned):
        cross = packed[HALF_ROWS:]
        packed = jnp.where(
            table_ref[tiles_ref.shape[0] + 1] == 0, packed[:HALF_ROWS], jnp.concatenate([cross, cross], axis=0)
        )
    count = sent_ref.shape[0]
    rows = (sums_ref.shape[0] - BLOCK) // count
    for k in range(count):
        if owned:
            per_block = TILE // UNIT
            units = rows * per_block // BLOCK
            sent_ref[k, :rows, :] = pack_units(
                [
                    sums_ref[
                        BLOCK * (u // per_block) : BLOCK * (u // per_block) + BLOCK,
                        UNIT * (u % per_block) : UNIT * (u % per_block) + UNIT,
                    ]
                    for u in range(units * k, units * k + units)
                ]
            )
        else:
            sent_ref[k, :rows, :] = sums_ref[rows * k : rows * k + rows, :]
        sent_ref[k, rows:, :] = packed


def unit_rows(unit, rows):
    for piece in range(BLOCK // 16):
        at = BLOCK * unit + 16 * piece
        yield at % rows, UNIT * (at // rows)


def pack_units(units):
    rows = len(units) * BLOCK * UNIT // TILE
    columns = [[] for _ in range(TILE // UNIT)]
    for unit, value in enumerate(units):
        for piece, (_, lane) in enumerate(unit_rows(unit, rows)):
            columns[lane // UNIT].append(value[16 * piece : 16 * piece + 16])
    return jnp.concatenate(
        [jnp.concatenate(pieces, axis=0) for pieces in columns], axis=1
    )


def unpack_units(packed):
    rows = packed.shape[0]
    units = []
    for unit in range(rows * TILE // (BLOCK * UNIT)):
        pieces = [
            packed[row : row + 16, lane : lane + UNIT]
            for row, lane in unit_rows(unit, rows)
        ]
        units.append(jnp.concatenate(pieces, axis=0))
    return jnp.concatenate(units, axis=1)


def pack_kernel(panel_ref, out_ref):
    packed = pack_units(
        [
            panel_ref[:, UNIT * unit : UNIT * unit + UNIT]
            for unit in range(panel_ref.shape[1] // UNIT)
        ]
    )
    for k in range(out_ref.shape[0]):
        out_ref[k] = packed


def start_kernel(
    table_ref, tiles_ref, got_ref, scale_ref, panel_ref, sent_ref,
    parts_ref, sums_ref, near_tiles_ref, sem, *, cb, units,
):
    copy = pltpu.make_async_copy(tiles_ref, near_tiles_ref, sem)
    copy.start()
    rows = got_ref.shape[1]
    for b in range(cb):
        found = []
        for c in range(TILE // UNIT):
            device, unit = divmod(TILE // UNIT * b + c, units)
            found.append(
                [
                    got_ref[device, row : row + 16, lane : lane + UNIT]
                    for row, lane in unit_rows(unit, rows)
                ]
            )
        for piece in range(BLOCK // 16):
            panel_ref[64 * b + 16 * piece : 64 * b + 16 * piece + 16, :] = (
                jnp.concatenate([pieces[piece] for pieces in found], axis=1)
            )
    send_panel(
        table_ref, near_tiles_ref, panel_ref, scale_ref, sent_ref, parts_ref, sums_ref,
        forward=True, cb=cb, ready=copy,
    )


def fold_kernel(got_ref, out_ref, *rest):
    rows = out_ref.shape[-2]
    total = got_ref[0, :rows, :]
    for k in range(1, got_ref.shape[0]):
        total += got_ref[k, :rows, :]
    for k in range(out_ref.shape[0]):
        out_ref[k] = total
    if rest:
        other = got_ref[0, rows:, :]
        for k in range(1, got_ref.shape[0]):
            other += got_ref[k, rows:, :]
        rest[0][...] = other


def sum_gram(got_ref):
    packed = got_ref[0, -GRAM_ROWS:, :]
    for k in range(1, got_ref.shape[0]):
        packed += got_ref[k, -GRAM_ROWS:, :]
    return unpack_gram(packed)


def join_gram(table_ref, own_ref, other_ref):
    first = table_ref[table_ref.shape[0] - 2] == 0
    own, other = own_ref[...], other_ref[...]
    return unpack_gram(
        jnp.concatenate(
            [
                jnp.where(first, own, other),
                jnp.where(first, other, own)[: GRAM_ROWS - HALF_ROWS],
            ],
            axis=0,
        )
    )


def lower_factor(factor_ref):
    lower = jnp.transpose(factor_ref[:, :BLOCK])
    mask = lax.broadcasted_iota(
        jnp.int32, (BLOCK, BLOCK), 0
    ) >= lax.broadcasted_iota(jnp.int32, (BLOCK, BLOCK), 1)
    return jnp.where(mask, lower, 0.0)


def factor_kernel(*refs, with_old, halves):
    refs = list(refs)
    if halves:
        gram, refs = join_gram(*refs[:3]), refs[3:]
    else:
        gram, refs = sum_gram(refs[0]), refs[1:]
    if not with_old:
        factor_rows(gram, refs[0])
        return
    old_ref, old_factor_ref, factor_ref, part_ref, lower_ref = refs
    factor_rows(gram, factor_ref)
    lower_ref[...] = lower_factor(factor_ref)
    back = backward_weights(factor_ref, old_factor_ref)
    for b in range(old_ref.shape[0] // BLOCK):
        part_ref[64 * b : 64 * b + 64, :] = jnp.dot(
            back, old_ref[64 * b : 64 * b + 64, :], precision=HIGH,
            preferred_element_type=jnp.float32,
        )


def backward_weights(factor_ref, old_factor_ref):
    upper_mask = lax.broadcasted_iota(
        jnp.int32, (BLOCK, BLOCK), 0
    ) <= lax.broadcasted_iota(jnp.int32, (BLOCK, BLOCK), 1)
    upper = jnp.where(upper_mask, factor_ref[:, :BLOCK], 0.0)
    return jnp.dot(
        upper, -old_factor_ref[:, BLOCK:], precision=HIGH,
        preferred_element_type=jnp.float32,
    )


def step_kernel(*refs, forward, cb, with_old, owned):
    refs = list(refs)
    table_ref, tiles_ref, got_ref, scale_ref, factor_ref = refs[:5]
    refs = refs[5:]
    if with_old:
        part_ref, refs = refs[0], refs[1:]
    panel_ref, sent_ref, parts_ref, sums_ref = refs
    inverse = split_three(factor_ref[:, BLOCK:])
    for b in range(panel_ref.shape[0] // BLOCK):
        where = slice(64 * b, 64 * b + 64)
        value = exact_dot(
            inverse, split_three(got_ref[where, :] * scale_ref[b : b + 1, :])
        )
        if with_old:
            value += part_ref[where, :]
        panel_ref[where, :] = value
    send_panel(
        table_ref, tiles_ref, panel_ref, scale_ref, sent_ref, parts_ref, sums_ref,
        forward=forward, cb=cb, owned=owned,
    )


def last_kernel(got_ref, old_ref, old_factor_ref, scale_ref, factor_ref, panel_ref, sent_ref):
    rows = got_ref.shape[1] - GRAM_ROWS
    total = got_ref[0, :rows, :]
    for k in range(1, got_ref.shape[0]):
        total += got_ref[k, :rows, :]
    value = unpack_units(total) * scale_ref[...]
    factor_rows(sum_gram(got_ref), factor_ref)
    weights = jnp.concatenate(
        [factor_ref[:, BLOCK:], backward_weights(factor_ref, old_factor_ref)], axis=1
    )
    value = jnp.dot(
        weights, jnp.concatenate([value, old_ref[...]], axis=0), precision=HIGH,
        preferred_element_type=jnp.float32,
    )
    panel_ref[...] = value
    gram = lax.dot_general(
        value, value, (((1,), (1,)), ((), ())), precision=HIGH,
        preferred_element_type=jnp.float32,
    )
    packed = pack_gram(gram)
    for k in range(sent_ref.shape[0]):
        sent_ref[k] = packed


def end_kernel(
    table_ref, got_ref, right_ref, left_ref, left_factor_ref, *refs, left_size, right_size
):
    lower_refs, refs = refs[:4], refs[4:]
    out_left_ref, out_right_ref, left_lower_ref, right_lower_ref, factor_ref = refs
    width = out_left_ref.shape[1]
    at = table_ref[table_ref.shape[0] - 1]
    block = at // (TILE // width)
    left = left_ref[pl.ds(pl.multiple_of(BLOCK * block, BLOCK), BLOCK), :]
    own = left[:, :width]
    for k in range(1, TILE // width):
        part = left[:, width * k : width * k + width]
        own = jnp.where(at - block * (TILE // width) == k, part, own)
    out_left_ref[...] = math.sqrt(left_size) * jnp.dot(
        left_factor_ref[:, BLOCK:], own, precision=HIGH,
        preferred_element_type=jnp.float32,
    )
    left_lower_ref[0] = lower_refs[0][...]
    right_lower_ref[0] = lower_refs[1][...]
    left_lower_ref[1] = lower_refs[2][...]
    right_lower_ref[1] = lower_refs[3][...]
    left_lower_ref[2] = lower_factor(left_factor_ref)
    factor_rows(sum_gram(got_ref), factor_ref)
    right_lower_ref[2] = lower_factor(factor_ref)
    out_right_ref[...] = math.sqrt(right_size) * jnp.dot(
        factor_ref[:, BLOCK:], right_ref[...], precision=HIGH,
        preferred_element_type=jnp.float32,
    )


SMEM = pl.BlockSpec(memory_space=pltpu.SMEM)
VMEM = pl.BlockSpec(memory_space=pltpu.VMEM)
PARAMS = pltpu.CompilerParams(vmem_limit_bytes=8 * 1024 * 1024)


def f32(*shape):
    return jax.ShapeDtypeStruct(shape, jnp.float32)


def fold(got, copies, rows, rest=False):
    shapes = [f32(copies, rows, TILE)]
    if rest:
        shapes.append(f32(got.shape[1] - rows, TILE))
    return pl.pallas_call(
        fold_kernel,
        out_shape=shapes,
        in_specs=[VMEM],
        out_specs=[VMEM] * len(shapes),
        compiler_params=PARAMS,
        name="fold",
    )(got)


def exchange(messages, axes):
    return lax.all_to_all(messages, axes, 0, 0, tiled=True)


def sum_col(sent):
    near = lax.axis_size(NEAR)
    own = fold(exchange(sent, NEAR), 1, sent.shape[1])[0][0]
    got = lax.all_gather(own, "zh", axis=0, tiled=False)
    rows = sent.shape[1] - GRAM_ROWS
    line = lax.axis_size("x")
    half = exchange(fold(got, line, rows)[0], "x").reshape(line * rows, TILE)
    return [got], lax.all_gather(half, "core", axis=0, tiled=True)


def sum_row(sent, table):
    count = lax.axis_size(ROW)
    rows = sent.shape[1] - HALF_ROWS
    copies, own = fold(exchange(sent, ROW), count, rows, rest=True)
    whole = exchange(copies, ROW).reshape(count * rows, TILE)
    other = lax.ppermute(own, "core", [(0, 1), (1, 0)])
    return [table, own, other], whole


def own_columns(panel, axes):
    blocks = panel.shape[0] // BLOCK
    group = blocks * TILE // lax.axis_size(axes)
    flat = jnp.transpose(panel.reshape(blocks, BLOCK, TILE), (1, 0, 2))
    flat = flat.reshape(BLOCK, blocks * TILE)
    return lax.dynamic_slice_in_dim(flat, lax.axis_index(axes) * group, group, 1)


def per_device(tiles, tile_slots, tile_counts, user_degree, item_degree, start_panel):
    tile_stack = tiles[0, 0]
    rb = user_degree.shape[0] // TILE
    cb = item_degree.shape[0] // TILE
    rows = lax.axis_size(ROW)
    near = lax.axis_size(NEAR)
    core = lax.axis_index("core").astype(jnp.int32).reshape(1)
    col = lax.axis_index(COL).astype(jnp.int32).reshape(1)
    table = jnp.concatenate([tile_slots[0, 0], tile_counts[0], core, col])
    user_scale = lax.rsqrt(user_degree.astype(jnp.float32)).reshape(rb, TILE)
    item_scale = lax.rsqrt(item_degree.astype(jnp.float32)).reshape(cb, TILE)

    units = start_panel.shape[1] // UNIT
    start = pl.pallas_call(
        pack_kernel,
        out_shape=f32(rows, BLOCK * units * UNIT // TILE, TILE),
        in_specs=[VMEM],
        out_specs=VMEM,
        compiler_params=PARAMS,
        name="pack",
    )(start_panel)
    start = exchange(start, ROW)

    user_messages = f32(near, rb * BLOCK // near + GRAM_ROWS, TILE)
    item_messages = f32(rows, cb * BLOCK // rows + HALF_ROWS, TILE)
    owned_messages = f32(rows, cb * BLOCK // rows + GRAM_ROWS, TILE)
    user_sums = pltpu.VMEM((rb * BLOCK + BLOCK, TILE), jnp.float32)
    item_sums = pltpu.VMEM((cb * BLOCK + BLOCK, TILE), jnp.float32)
    user_parts = pltpu.VMEM((rb * 192, TILE), jnp.bfloat16)
    item_parts = pltpu.VMEM((cb * 192, TILE), jnp.bfloat16)
    start, sent = pl.pallas_call(
        functools.partial(start_kernel, cb=cb, units=units),
        out_shape=[f32(cb * BLOCK, TILE), user_messages],
        in_specs=[SMEM, pl.BlockSpec(memory_space=pltpu.HBM), VMEM, VMEM],
        out_specs=[VMEM, VMEM],
        scratch_shapes=[
            item_parts,
            user_sums,
            pltpu.VMEM(tile_stack.shape, tile_stack.dtype),
            pltpu.SemaphoreType.DMA,
        ],
        compiler_params=PARAMS,
        name="start",
    )(table, tile_stack, start, item_scale)

    item_group = cb * TILE // rows
    own_scale = lax.dynamic_slice_in_dim(
        item_scale.reshape(1, cb * TILE), lax.axis_index(ROW) * item_group, item_group, 1
    )
    panels = [start]
    factors = []
    lower = []
    for half in range(1, 2 * STEPS):
        users = half % 2 == 1
        owned = half == 2 * STEPS - 1
        with_old = half > 1
        gram, whole = sum_col(sent) if users else sum_row(sent, table)
        panel_shape = f32((rb if users else cb) * BLOCK, TILE)
        if owned:
            old_items, gram[0] = lax.optimization_barrier((panels[-1], gram[0]))
            own_old = own_columns(old_items, ROW)
        old = [panels[half - 2], factors[half - 2]] if with_old else []
        shapes = [f32(BLOCK, 2 * BLOCK)]
        if with_old:
            shapes += [panel_shape, f32(BLOCK, BLOCK)]
        factored = pl.pallas_call(
            functools.partial(factor_kernel, with_old=with_old, halves=not users),
            out_shape=shapes,
            in_specs=([VMEM] if users else [SMEM, VMEM, VMEM]) + [VMEM] * len(old),
            out_specs=[VMEM] * len(shapes),
            compiler_params=PARAMS,
            name=f"factor{half}",
        )(*gram, *old)
        factors.append(factored[0])
        lower += factored[2:]
        messages = user_messages
        if users:
            messages = owned_messages if owned else item_messages
        operands = [whole, user_scale if users else item_scale, *factored[:2]]
        if owned:
            operands[2:], own_old, own_scale = lax.optimization_barrier(
                (operands[2:], own_old, own_scale)
            )
        panel, sent = pl.pallas_call(
            functools.partial(
                step_kernel, forward=not users, cb=cb, with_old=with_old, owned=owned
            ),
            out_shape=[panel_shape, messages],
            in_specs=[SMEM, VMEM] + [VMEM] * len(operands),
            out_specs=[VMEM, VMEM],
            scratch_shapes=[user_parts, item_sums] if users else [item_parts, user_sums],
            compiler_params=PARAMS,
            name=f"half{half}",
        )(table, tile_stack, *operands)
        panels.append(panel)

    factor, right, sent = pl.pallas_call(
        last_kernel,
        out_shape=[
            f32(BLOCK, 2 * BLOCK),
            f32(BLOCK, item_group),
            f32(lax.axis_size(FLAT), GRAM_ROWS, TILE),
        ],
        in_specs=[VMEM] * 4,
        out_specs=[VMEM] * 3,
        compiler_params=PARAMS,
        name="last",
    )(exchange(sent, ROW), own_old, factors[-1], own_scale)
    gram = exchange(
        fold(exchange(sent, FLAT), lax.axis_size(LINE), GRAM_ROWS)[0], LINE
    )
    return tuple(
        pl.pallas_call(
            functools.partial(
                end_kernel,
                left_size=rb * TILE * rows,
                right_size=cb * TILE * lax.axis_size(COL),
            ),
            out_shape=[
                f32(BLOCK, rb * TILE // lax.axis_size(COL)),
                f32(BLOCK, item_group),
                f32(STEPS, BLOCK, BLOCK),
                f32(STEPS, BLOCK, BLOCK),
            ],
            in_specs=[SMEM] + [VMEM] * 8,
            out_specs=[VMEM] * 4,
            scratch_shapes=[pltpu.VMEM((BLOCK, 2 * BLOCK), jnp.float32)],
            compiler_params=PARAMS,
            name="end",
        )(table, gram, right, panels[-1], factor, *lower)
    )


def solution(mesh):
    split = Mesh(mesh.devices.reshape(4, 4, 4, 4, 2), ROW + COL)
    in_specs = (
        P(ROW, COL, None, None, None),
        P(ROW, COL, None),
        P(ROW, COL),
        P(ROW),
        P(COL),
        P(None, COL + ROW),
    )
    out_specs = (P(None, ROW + COL), P(None, COL + ROW), P(), P())
    return jax.shard_map(
        per_device, mesh=split, in_specs=in_specs, out_specs=out_specs, check_vma=False
    )
```

```python
import functools
import math

import jax
import jax.numpy as jnp
from jax import lax
from jax.experimental import pallas as pl
from jax.experimental.pallas import tpu as pltpu
from jax.sharding import Mesh
from jax.sharding import PartitionSpec as P

STEPS = 3
TILE = 128
BLOCK = 64
GRAM_ROWS = 24
HALF_ROWS = 16
UNIT = 32
HIGH = lax.Precision.HIGHEST

ROW = ("zl", "y")
COL = ("x", "zh", "core")
NEAR = ("core", "x")
FLAT = ("core", "y", "x")
LINE = ("zh", "zl")


def pack_gram(gram):
    half = BLOCK // 2

    def rows(block):
        return jnp.concatenate([block[8 * i : 8 * i + 8] for i in range(4)], axis=1)

    return jnp.concatenate(
        [
            rows(gram[:half, :half]),
            rows(gram[half:, half:]),
            rows(gram[half:, :half]),
        ],
        axis=0,
    )


def unpack_gram(packed):
    half = BLOCK // 2

    def block(rows):
        return jnp.concatenate(
            [rows[:, half * i : half * i + half] for i in range(4)], axis=0
        )

    upper, lower, cross = (block(packed[8 * i : 8 * i + 8]) for i in range(3))
    return jnp.concatenate(
        [
            jnp.concatenate([upper, jnp.transpose(cross)], axis=1),
            jnp.concatenate([cross, lower], axis=1),
        ],
        axis=0,
    )


def factor_rows(gram, out_ref):
    eye = (
        lax.broadcasted_iota(jnp.int32, (BLOCK, BLOCK), 0)
        == lax.broadcasted_iota(jnp.int32, (BLOCK, BLOCK), 1)
    ).astype(jnp.float32)
    whole = jnp.concatenate([gram, eye], axis=1)
    groups = [whole[8 * i : 8 * i + 8] for i in range(BLOCK // 8)]
    for first in range(BLOCK // 8):
        base = 8 * first
        below = range(first, BLOCK // 8)
        spread = {
            i: [
                jnp.broadcast_to(groups[i][:, base + m : base + m + 1], groups[i].shape)
                for m in range(8)
            ]
            for i in below
        }
        for k in range(8):
            root = lax.rsqrt(spread[first][k][k : k + 1])
            scaled = groups[first][k : k + 1] * root
            out_ref[base + k : base + k + 1, :] = scaled
            across = {m: spread[first][m][k : k + 1] * root for m in range(k + 1, 8)}
            for i in below:
                times = spread[i][k] * root
                groups[i] = groups[i] - times * scaled
                for m in across:
                    spread[i][m] = spread[i][m] - times * across[m]


def split_three(value):
    high = value.astype(jnp.bfloat16)
    rest = value - high.astype(jnp.float32)
    middle = rest.astype(jnp.bfloat16)
    low = (rest - middle.astype(jnp.float32)).astype(jnp.bfloat16)
    return high, middle, low


def exact_dot(left, right):
    high, middle, low = left
    first = jnp.concatenate([high, high, middle, high, middle, low], axis=1)
    high, middle, low = right
    second = jnp.concatenate([high, middle, high, low, middle, high], axis=0)
    return jnp.dot(first, second, preferred_element_type=jnp.float32)


def product(table_ref, tiles_ref, parts_ref, sums_ref, forward, cb):
    slot_count = tiles_ref.shape[0]
    count = table_ref[slot_count]
    spare = sums_ref.shape[0] // BLOCK - 1
    group = 16

    def visit(step, carry):
        added = []
        for g in range(group):
            t = step * group + g
            slot = table_ref[t]
            local_row = slot // cb
            local_col = slot - local_row * cb
            source, target = (
                (local_col, local_row) if forward else (local_row, local_col)
            )
            tile = tiles_ref[t]
            target = jnp.where(t < count, target, spare)
            parts = parts_ref[pl.ds(pl.multiple_of(source * 192, 64), 192), :]
            dims = (((1,), (1 if forward else 0,)), ((), ()))
            value = lax.dot_general(
                parts, tile, dims, preferred_element_type=jnp.float32
            )
            added.append((target, value[:64] + value[64:128] + value[128:]))
        for target, value in added:
            where = pl.ds(pl.multiple_of(target * 64, 64), 64)
            sums_ref[where, :] += value
        return carry

    lax.fori_loop(0, (count + group - 1) // group, visit, 0)


def add_gram(gram, value):
    same, cross = gram
    high, middle, low = split_three(value)
    dims = (((1,), (1,)), ((), ()))
    same += lax.dot_general(
        jnp.concatenate([high, middle], axis=1), jnp.concatenate([high, middle], axis=1), dims,
        preferred_element_type=jnp.float32,
    )
    cross += lax.dot_general(
        jnp.concatenate([high, high], axis=1), jnp.concatenate([middle, low], axis=1), dims,
        preferred_element_type=jnp.float32,
    )
    return same, cross


def no_gram():
    return (jnp.zeros((BLOCK, BLOCK), jnp.float32),) * 2


def whole_gram(gram):
    same, cross = gram
    return same + cross + jnp.transpose(cross)


def send_panel(
    table_ref, tiles_ref, panel_ref, scale_ref, sent_ref, parts_ref, sums_ref, *, forward, cb, ready=None,
    owned=False,
):
    sums_ref[...] = jnp.zeros_like(sums_ref)
    gram = no_gram()
    for b in range(panel_ref.shape[0] // BLOCK):
        value = panel_ref[64 * b : 64 * b + 64, :]
        gram = add_gram(gram, value)
        parts_ref[192 * b : 192 * b + 192, :] = jnp.concatenate(
            split_three(value * scale_ref[b : b + 1, :]), axis=0
        )
    if ready is not None:
        ready.wait()
    product(table_ref, tiles_ref, parts_ref, sums_ref, forward, cb)
    packed = pack_gram(whole_gram(gram))
    if not (forward or owned):
        cross = packed[HALF_ROWS:]
        packed = jnp.where(
            table_ref[tiles_ref.shape[0] + 1] == 0, packed[:HALF_ROWS], jnp.concatenate([cross, cross], axis=0)
        )
    count = sent_ref.shape[0]
    rows = (sums_ref.shape[0] - BLOCK) // count
    for k in range(count):
        if owned:
            per_block = TILE // UNIT
            units = rows * per_block // BLOCK
            sent_ref[k, :rows, :] = pack_units(
                [
                    sums_ref[
                        BLOCK * (u // per_block) : BLOCK * (u // per_block) + BLOCK,
                        UNIT * (u % per_block) : UNIT * (u % per_block) + UNIT,
                    ]
                    for u in range(units * k, units * k + units)
                ]
            )
        else:
            sent_ref[k, :rows, :] = sums_ref[rows * k : rows * k + rows, :]
        sent_ref[k, rows:, :] = packed


def unit_rows(unit, rows):
    for piece in range(BLOCK // 16):
        at = BLOCK * unit + 16 * piece
        yield at % rows, UNIT * (at // rows)


def pack_units(units):
    rows = len(units) * BLOCK * UNIT // TILE
    columns = [[] for _ in range(TILE // UNIT)]
    for unit, value in enumerate(units):
        for piece, (_, lane) in enumerate(unit_rows(unit, rows)):
            columns[lane // UNIT].append(value[16 * piece : 16 * piece + 16])
    return jnp.concatenate(
        [jnp.concatenate(pieces, axis=0) for pieces in columns], axis=1
    )


def unpack_units(packed):
    rows = packed.shape[0]
    units = []
    for unit in range(rows * TILE // (BLOCK * UNIT)):
        pieces = [
            packed[row : row + 16, lane : lane + UNIT]
            for row, lane in unit_rows(unit, rows)
        ]
        units.append(jnp.concatenate(pieces, axis=0))
    return jnp.concatenate(units, axis=1)


def pack_kernel(panel_ref, out_ref):
    packed = pack_units(
        [
            panel_ref[:, UNIT * unit : UNIT * unit + UNIT]
            for unit in range(panel_ref.shape[1] // UNIT)
        ]
    )
    for k in range(out_ref.shape[0]):
        out_ref[k] = packed


def start_kernel(
    table_ref, tiles_ref, got_ref, scale_ref, panel_ref, sent_ref,
    parts_ref, sums_ref, near_tiles_ref, sem, *, cb, units,
):
    copy = pltpu.make_async_copy(tiles_ref, near_tiles_ref, sem)
    copy.start()
    rows = got_ref.shape[1]
    for b in range(cb):
        found = []
        for c in range(TILE // UNIT):
            device, unit = divmod(TILE // UNIT * b + c, units)
            found.append(
                [
                    got_ref[device, row : row + 16, lane : lane + UNIT]
                    for row, lane in unit_rows(unit, rows)
                ]
            )
        for piece in range(BLOCK // 16):
            panel_ref[64 * b + 16 * piece : 64 * b + 16 * piece + 16, :] = (
                jnp.concatenate([pieces[piece] for pieces in found], axis=1)
            )
    send_panel(
        table_ref, near_tiles_ref, panel_ref, scale_ref, sent_ref, parts_ref, sums_ref,
        forward=True, cb=cb, ready=copy,
    )


def fold_kernel(got_ref, out_ref, *rest):
    rows = out_ref.shape[-2]
    total = got_ref[0, :rows, :]
    for k in range(1, got_ref.shape[0]):
        total += got_ref[k, :rows, :]
    for k in range(out_ref.shape[0]):
        out_ref[k] = total
    if rest:
        other = got_ref[0, rows:, :]
        for k in range(1, got_ref.shape[0]):
            other += got_ref[k, rows:, :]
        rest[0][...] = other


def sum_gram(got_ref):
    packed = got_ref[0, -GRAM_ROWS:, :]
    for k in range(1, got_ref.shape[0]):
        packed += got_ref[k, -GRAM_ROWS:, :]
    return unpack_gram(packed)


def join_gram(table_ref, own_ref, other_ref):
    first = table_ref[table_ref.shape[0] - 3] == 0
    own, other = own_ref[...], other_ref[...]
    return unpack_gram(
        jnp.concatenate(
            [
                jnp.where(first, own, other),
                jnp.where(first, other, own)[: GRAM_ROWS - HALF_ROWS],
            ],
            axis=0,
        )
    )


def lower_factor(factor_ref):
    lower = jnp.transpose(factor_ref[:, :BLOCK])
    mask = lax.broadcasted_iota(
        jnp.int32, (BLOCK, BLOCK), 0
    ) >= lax.broadcasted_iota(jnp.int32, (BLOCK, BLOCK), 1)
    return jnp.where(mask, lower, 0.0)


def cut(ref, height, start, width):
    per_block = TILE // UNIT
    block = start // per_block
    after = jnp.minimum(block + 1, ref.shape[0] // height - 1)
    wide = jnp.concatenate(
        [
            ref[pl.ds(pl.multiple_of(height * b, height), height), :]
            for b in (block, after)
        ],
        axis=1,
    )
    own = wide[:, :width]
    for k in range(1, per_block):
        own = jnp.where(
            start - block * per_block == k, wide[:, UNIT * k : UNIT * k + width], own
        )
    return own


def factor_kernel(*refs, with_old, halves, owned=False):
    refs = list(refs)
    if owned:
        table_ref, items_ref, scale_ref = refs[3:6]
        own_items_ref, own_scale_ref = refs[-2:]
        width = own_items_ref.shape[1]
        start = (width // UNIT) * table_ref[table_ref.shape[0] - 1]
        own_items_ref[...] = cut(items_ref, BLOCK, start, width)
        own_scale_ref[...] = cut(scale_ref, 1, start, width)
        refs = refs[:3] + refs[6:-2]
    if halves:
        gram, refs = join_gram(*refs[:3]), refs[3:]
    else:
        gram, refs = sum_gram(refs[0]), refs[1:]
    if not with_old:
        factor_rows(gram, refs[0])
        return
    old_ref, old_factor_ref, factor_ref, part_ref, lower_ref = refs
    factor_rows(gram, factor_ref)
    lower_ref[...] = lower_factor(factor_ref)
    back = backward_weights(factor_ref, old_factor_ref)
    for b in range(old_ref.shape[0] // BLOCK):
        part_ref[64 * b : 64 * b + 64, :] = jnp.dot(
            back, old_ref[64 * b : 64 * b + 64, :], precision=HIGH,
            preferred_element_type=jnp.float32,
        )


def backward_weights(factor_ref, old_factor_ref):
    upper_mask = lax.broadcasted_iota(
        jnp.int32, (BLOCK, BLOCK), 0
    ) <= lax.broadcasted_iota(jnp.int32, (BLOCK, BLOCK), 1)
    upper = jnp.where(upper_mask, factor_ref[:, :BLOCK], 0.0)
    return jnp.dot(
        upper, -old_factor_ref[:, BLOCK:], precision=HIGH,
        preferred_element_type=jnp.float32,
    )


def step_kernel(*refs, forward, cb, with_old, owned):
    refs = list(refs)
    table_ref, tiles_ref, got_ref, scale_ref, factor_ref = refs[:5]
    refs = refs[5:]
    if with_old:
        part_ref, refs = refs[0], refs[1:]
    if owned:
        sent_ref, own_ref, panel_ref = refs[:3]
    else:
        panel_ref, sent_ref = refs[:2]
    parts_ref, sums_ref = refs[-2:]
    inverse = split_three(factor_ref[:, BLOCK:])
    for b in range(panel_ref.shape[0] // BLOCK):
        where = slice(64 * b, 64 * b + 64)
        value = exact_dot(
            inverse, split_three(got_ref[where, :] * scale_ref[b : b + 1, :])
        )
        if with_old:
            value += part_ref[where, :]
        panel_ref[where, :] = value
    send_panel(
        table_ref, tiles_ref, panel_ref, scale_ref, sent_ref, parts_ref, sums_ref,
        forward=forward, cb=cb, owned=owned,
    )
    if owned:
        width = own_ref.shape[1]
        start = (width // UNIT) * table_ref[table_ref.shape[0] - 2]
        own_ref[...] = cut(panel_ref, BLOCK, start, width)


def last_kernel(got_ref, old_ref, old_factor_ref, scale_ref, factor_ref, panel_ref, sent_ref):
    rows = got_ref.shape[1] - GRAM_ROWS
    total = got_ref[0, :rows, :]
    for k in range(1, got_ref.shape[0]):
        total += got_ref[k, :rows, :]
    value = unpack_units(total) * scale_ref[...]
    factor_rows(sum_gram(got_ref), factor_ref)
    weights = jnp.concatenate(
        [factor_ref[:, BLOCK:], backward_weights(factor_ref, old_factor_ref)], axis=1
    )
    value = jnp.dot(
        weights, jnp.concatenate([value, old_ref[...]], axis=0), precision=HIGH,
        preferred_element_type=jnp.float32,
    )
    panel_ref[...] = value
    gram = lax.dot_general(
        value, value, (((1,), (1,)), ((), ())), precision=HIGH,
        preferred_element_type=jnp.float32,
    )
    packed = pack_gram(gram)
    for k in range(sent_ref.shape[0]):
        sent_ref[k] = packed


def end_kernel(
    got_ref, right_ref, left_ref, left_factor_ref, *refs, left_size, right_size
):
    lower_refs, refs = refs[:4], refs[4:]
    out_left_ref, out_right_ref, left_lower_ref, right_lower_ref, factor_ref = refs
    out_left_ref[...] = math.sqrt(left_size) * jnp.dot(
        left_factor_ref[:, BLOCK:], left_ref[...], precision=HIGH,
        preferred_element_type=jnp.float32,
    )
    left_lower_ref[0] = lower_refs[0][...]
    right_lower_ref[0] = lower_refs[1][...]
    left_lower_ref[1] = lower_refs[2][...]
    right_lower_ref[1] = lower_refs[3][...]
    left_lower_ref[2] = lower_factor(left_factor_ref)
    factor_rows(sum_gram(got_ref), factor_ref)
    right_lower_ref[2] = lower_factor(factor_ref)
    out_right_ref[...] = math.sqrt(right_size) * jnp.dot(
        factor_ref[:, BLOCK:], right_ref[...], precision=HIGH,
        preferred_element_type=jnp.float32,
    )


SMEM = pl.BlockSpec(memory_space=pltpu.SMEM)
VMEM = pl.BlockSpec(memory_space=pltpu.VMEM)
PARAMS = pltpu.CompilerParams(vmem_limit_bytes=8 * 1024 * 1024)


def f32(*shape):
    return jax.ShapeDtypeStruct(shape, jnp.float32)


def fold(got, copies, rows, rest=False):
    shapes = [f32(copies, rows, TILE)]
    if rest:
        shapes.append(f32(got.shape[1] - rows, TILE))
    return pl.pallas_call(
        fold_kernel,
        out_shape=shapes,
        in_specs=[VMEM],
        out_specs=[VMEM] * len(shapes),
        compiler_params=PARAMS,
        name="fold",
    )(got)


def exchange(messages, axes):
    return lax.all_to_all(messages, axes, 0, 0, tiled=True)


def sum_col(sent):
    near = lax.axis_size(NEAR)
    own = fold(exchange(sent, NEAR), 1, sent.shape[1])[0][0]
    got = lax.all_gather(own, "zh", axis=0, tiled=False)
    rows = sent.shape[1] - GRAM_ROWS
    line = lax.axis_size("x")
    half = exchange(fold(got, line, rows)[0], "x").reshape(line * rows, TILE)
    return [got], lax.all_gather(half, "core", axis=0, tiled=True)


def sum_row(sent, table):
    count = lax.axis_size(ROW)
    rows = sent.shape[1] - HALF_ROWS
    copies, own = fold(exchange(sent, ROW), count, rows, rest=True)
    whole = exchange(copies, ROW).reshape(count * rows, TILE)
    other = lax.ppermute(own, "core", [(0, 1), (1, 0)])
    return [table, own, other], whole


def per_device(tiles, tile_slots, tile_counts, user_degree, item_degree, start_panel):
    tile_stack = tiles[0, 0]
    rb = user_degree.shape[0] // TILE
    cb = item_degree.shape[0] // TILE
    rows = lax.axis_size(ROW)
    near = lax.axis_size(NEAR)
    core = lax.axis_index("core").astype(jnp.int32).reshape(1)
    col = lax.axis_index(COL).astype(jnp.int32).reshape(1)
    row = lax.axis_index(ROW).astype(jnp.int32).reshape(1)
    table = jnp.concatenate([tile_slots[0, 0], tile_counts[0], core, col, row])
    user_scale = lax.rsqrt(user_degree.astype(jnp.float32)).reshape(rb, TILE)
    item_scale = lax.rsqrt(item_degree.astype(jnp.float32)).reshape(cb, TILE)

    units = start_panel.shape[1] // UNIT
    start = pl.pallas_call(
        pack_kernel,
        out_shape=f32(rows, BLOCK * units * UNIT // TILE, TILE),
        in_specs=[VMEM],
        out_specs=VMEM,
        compiler_params=PARAMS,
        name="pack",
    )(start_panel)
    start = exchange(start, ROW)

    user_messages = f32(near, rb * BLOCK // near + GRAM_ROWS, TILE)
    item_messages = f32(rows, cb * BLOCK // rows + HALF_ROWS, TILE)
    owned_messages = f32(rows, cb * BLOCK // rows + GRAM_ROWS, TILE)
    user_sums = pltpu.VMEM((rb * BLOCK + BLOCK, TILE), jnp.float32)
    item_sums = pltpu.VMEM((cb * BLOCK + BLOCK, TILE), jnp.float32)
    user_parts = pltpu.VMEM((rb * 192, TILE), jnp.bfloat16)
    item_parts = pltpu.VMEM((cb * 192, TILE), jnp.bfloat16)
    start, sent = pl.pallas_call(
        functools.partial(start_kernel, cb=cb, units=units),
        out_shape=[f32(cb * BLOCK, TILE), user_messages],
        in_specs=[SMEM, pl.BlockSpec(memory_space=pltpu.HBM), VMEM, VMEM],
        out_specs=[VMEM, VMEM],
        scratch_shapes=[
            item_parts,
            user_sums,
            pltpu.VMEM(tile_stack.shape, tile_stack.dtype),
            pltpu.SemaphoreType.DMA,
        ],
        compiler_params=PARAMS,
        name="start",
    )(table, tile_stack, start, item_scale)

    item_group = cb * TILE // rows
    panels = [start]
    factors = []
    lower = []
    for half in range(1, 2 * STEPS):
        users = half % 2 == 1
        owned = half == 2 * STEPS - 1
        with_old = half > 1
        gram, whole = sum_col(sent) if users else sum_row(sent, table)
        panel_shape = f32((rb if users else cb) * BLOCK, TILE)
        old = [panels[half - 2], factors[half - 2]] if with_old else []
        shapes = [f32(BLOCK, 2 * BLOCK)]
        if with_old:
            shapes += [panel_shape, f32(BLOCK, BLOCK)]
        wanted = []
        if owned:
            wanted = [table, panels[-1], item_scale]
            shapes += [f32(BLOCK, item_group), f32(1, item_group)]
        factored = pl.pallas_call(
            functools.partial(
                factor_kernel, with_old=with_old, halves=not users, owned=owned
            ),
            out_shape=shapes,
            in_specs=([VMEM] if users else [SMEM, VMEM, VMEM])
            + [VMEM] * len(old)
            + ([SMEM, VMEM, VMEM] if owned else []),
            out_specs=[VMEM] * len(shapes),
            compiler_params=PARAMS,
            name=f"factor{half}",
        )(*gram, *old, *wanted)
        factors.append(factored[0])
        lower += factored[2:3]
        messages = user_messages
        if users:
            messages = owned_messages if owned else item_messages
        operands = [whole, user_scale if users else item_scale, *factored[:2]]
        scratch = [user_parts, item_sums] if users else [item_parts, user_sums]
        shapes = [panel_shape, messages]
        if owned:
            shapes = [messages, f32(BLOCK, rb * TILE // lax.axis_size(COL))]
            scratch = [pltpu.VMEM(panel_shape.shape, jnp.float32), *scratch]
        results = pl.pallas_call(
            functools.partial(
                step_kernel, forward=not users, cb=cb, with_old=with_old, owned=owned
            ),
            out_shape=shapes,
            in_specs=[SMEM, VMEM] + [VMEM] * len(operands),
            out_specs=[VMEM, VMEM],
            scratch_shapes=scratch,
            compiler_params=PARAMS,
            name=f"half{half}",
        )(table, tile_stack, *operands)
        if owned:
            sent, left = results
        else:
            panel, sent = results
            panels.append(panel)

    factor, right, sent = pl.pallas_call(
        last_kernel,
        out_shape=[
            f32(BLOCK, 2 * BLOCK),
            f32(BLOCK, item_group),
            f32(lax.axis_size(FLAT), GRAM_ROWS, TILE),
        ],
        in_specs=[VMEM] * 4,
        out_specs=[VMEM] * 3,
        compiler_params=PARAMS,
        name="last",
    )(exchange(sent, ROW), factored[3], factors[-1], factored[4])
    gram = exchange(
        fold(exchange(sent, FLAT), lax.axis_size(LINE), GRAM_ROWS)[0], LINE
    )
    return tuple(
        pl.pallas_call(
            functools.partial(
                end_kernel,
                left_size=rb * TILE * rows,
                right_size=cb * TILE * lax.axis_size(COL),
            ),
            out_shape=[
                f32(BLOCK, rb * TILE // lax.axis_size(COL)),
                f32(BLOCK, item_group),
                f32(STEPS, BLOCK, BLOCK),
                f32(STEPS, BLOCK, BLOCK),
            ],
            in_specs=[VMEM] * 8,
            out_specs=[VMEM] * 4,
            scratch_shapes=[pltpu.VMEM((BLOCK, 2 * BLOCK), jnp.float32)],
            compiler_params=PARAMS,
            name="end",
        )(gram, right, left, factor, *lower)
    )


def solution(mesh):
    split = Mesh(mesh.devices.reshape(4, 4, 4, 4, 2), ROW + COL)
    in_specs = (
        P(ROW, COL, None, None, None),
        P(ROW, COL, None),
        P(ROW, COL),
        P(ROW),
        P(COL),
        P(None, COL + ROW),
    )
    out_specs = (P(None, ROW + COL), P(None, COL + ROW), P(), P())
    return jax.shard_map(
        per_device, mesh=split, in_specs=in_specs, out_specs=out_specs, check_vma=False
    )
```

```python
import functools
import math

import jax
import jax.numpy as jnp
from jax import lax
from jax.experimental import pallas as pl
from jax.experimental.pallas import tpu as pltpu
from jax.sharding import Mesh
from jax.sharding import PartitionSpec as P

STEPS = 3
TILE = 128
BLOCK = 64
GRAM_ROWS = 24
HALF_ROWS = 16
UNIT = 32
COUNT_AT, CORE_AT, COL_AT, ROW_AT, SLOTS_AT = range(5)
TABLE = 128
HIGH = lax.Precision.HIGHEST

ROW = ("zl", "y")
COL = ("x", "zh", "core")
NEAR = ("core", "x")
FLAT = ("core", "y", "x")
LINE = ("zh", "zl")


def pack_gram(gram):
    half = BLOCK // 2

    def rows(block):
        return jnp.concatenate([block[8 * i : 8 * i + 8] for i in range(4)], axis=1)

    return jnp.concatenate(
        [
            rows(gram[:half, :half]),
            rows(gram[half:, half:]),
            rows(gram[half:, :half]),
        ],
        axis=0,
    )


def unpack_gram(packed):
    half = BLOCK // 2

    def block(rows):
        return jnp.concatenate(
            [rows[:, half * i : half * i + half] for i in range(4)], axis=0
        )

    upper, lower, cross = (block(packed[8 * i : 8 * i + 8]) for i in range(3))
    return jnp.concatenate(
        [
            jnp.concatenate([upper, jnp.transpose(cross)], axis=1),
            jnp.concatenate([cross, lower], axis=1),
        ],
        axis=0,
    )


def factor_rows(gram, out_ref):
    eye = (
        lax.broadcasted_iota(jnp.int32, (BLOCK, BLOCK), 0)
        == lax.broadcasted_iota(jnp.int32, (BLOCK, BLOCK), 1)
    ).astype(jnp.float32)
    whole = jnp.concatenate([gram, eye], axis=1)
    groups = [whole[8 * i : 8 * i + 8] for i in range(BLOCK // 8)]
    for first in range(BLOCK // 8):
        base = 8 * first
        below = range(first, BLOCK // 8)
        spread = {
            i: [
                jnp.broadcast_to(groups[i][:, base + m : base + m + 1], groups[i].shape)
                for m in range(8)
            ]
            for i in below
        }
        for k in range(8):
            root = lax.rsqrt(spread[first][k][k : k + 1])
            scaled = groups[first][k : k + 1] * root
            out_ref[base + k : base + k + 1, :] = scaled
            across = {m: spread[first][m][k : k + 1] * root for m in range(k + 1, 8)}
            for i in below:
                times = spread[i][k] * root
                groups[i] = groups[i] - times * scaled
                for m in across:
                    spread[i][m] = spread[i][m] - times * across[m]


def split_three(value):
    high = value.astype(jnp.bfloat16)
    rest = value - high.astype(jnp.float32)
    middle = rest.astype(jnp.bfloat16)
    low = (rest - middle.astype(jnp.float32)).astype(jnp.bfloat16)
    return high, middle, low


def exact_dot(left, right):
    high, middle, low = left
    first = jnp.concatenate([high, high, middle, high, middle, low], axis=1)
    high, middle, low = right
    second = jnp.concatenate([high, middle, high, low, middle, high], axis=0)
    return jnp.dot(first, second, preferred_element_type=jnp.float32)


def product(table_ref, tiles_ref, parts_ref, sums_ref, forward, cb):
    count = table_ref[COUNT_AT]
    spare = sums_ref.shape[0] // BLOCK - 1
    group = 16

    def visit(step, carry):
        added = []
        for g in range(group):
            t = step * group + g
            slot = table_ref[SLOTS_AT + t]
            local_row = slot // cb
            local_col = slot - local_row * cb
            source, target = (
                (local_col, local_row) if forward else (local_row, local_col)
            )
            tile = tiles_ref[t]
            target = jnp.where(t < count, target, spare)
            parts = parts_ref[pl.ds(pl.multiple_of(source * 192, 64), 192), :]
            dims = (((1,), (1 if forward else 0,)), ((), ()))
            value = lax.dot_general(
                parts, tile, dims, preferred_element_type=jnp.float32
            )
            added.append((target, value[:64] + value[64:128] + value[128:]))
        for target, value in added:
            where = pl.ds(pl.multiple_of(target * 64, 64), 64)
            sums_ref[where, :] += value
        return carry

    lax.fori_loop(0, (count + group - 1) // group, visit, 0)


def add_gram(gram, value):
    same, cross = gram
    high, middle, low = split_three(value)
    dims = (((1,), (1,)), ((), ()))
    same += lax.dot_general(
        jnp.concatenate([high, middle], axis=1), jnp.concatenate([high, middle], axis=1), dims,
        preferred_element_type=jnp.float32,
    )
    cross += lax.dot_general(
        jnp.concatenate([high, high], axis=1), jnp.concatenate([middle, low], axis=1), dims,
        preferred_element_type=jnp.float32,
    )
    return same, cross


def no_gram():
    return (jnp.zeros((BLOCK, BLOCK), jnp.float32),) * 2


def whole_gram(gram):
    same, cross = gram
    return same + cross + jnp.transpose(cross)


def send_panel(
    table_ref, tiles_ref, panel_ref, scale_ref, sent_ref, parts_ref, sums_ref, *, forward, cb, ready=(),
    owned=False,
):
    sums_ref[...] = jnp.zeros_like(sums_ref)
    gram = no_gram()
    for b in range(panel_ref.shape[0] // BLOCK):
        value = panel_ref[64 * b : 64 * b + 64, :]
        gram = add_gram(gram, value)
        parts_ref[192 * b : 192 * b + 192, :] = jnp.concatenate(
            split_three(value * scale_ref[b : b + 1, :]), axis=0
        )
    for copy in ready:
        copy.wait()
    product(table_ref, tiles_ref, parts_ref, sums_ref, forward, cb)
    packed = pack_gram(whole_gram(gram))
    if not (forward or owned):
        cross = packed[HALF_ROWS:]
        packed = jnp.where(
            table_ref[CORE_AT] == 0, packed[:HALF_ROWS], jnp.concatenate([cross, cross], axis=0)
        )
    count = sent_ref.shape[0]
    rows = (sums_ref.shape[0] - BLOCK) // count
    for k in range(count):
        if owned:
            per_block = TILE // UNIT
            units = rows * per_block // BLOCK
            sent_ref[k, :rows, :] = pack_units(
                [
                    sums_ref[
                        BLOCK * (u // per_block) : BLOCK * (u // per_block) + BLOCK,
                        UNIT * (u % per_block) : UNIT * (u % per_block) + UNIT,
                    ]
                    for u in range(units * k, units * k + units)
                ]
            )
        else:
            sent_ref[k, :rows, :] = sums_ref[rows * k : rows * k + rows, :]
        sent_ref[k, rows:, :] = packed


def unit_rows(unit, rows):
    for piece in range(BLOCK // 16):
        at = BLOCK * unit + 16 * piece
        yield at % rows, UNIT * (at // rows)


def pack_units(units):
    rows = len(units) * BLOCK * UNIT // TILE
    columns = [[] for _ in range(TILE // UNIT)]
    for unit, value in enumerate(units):
        for piece, (_, lane) in enumerate(unit_rows(unit, rows)):
            columns[lane // UNIT].append(value[16 * piece : 16 * piece + 16])
    return jnp.concatenate(
        [jnp.concatenate(pieces, axis=0) for pieces in columns], axis=1
    )


def unpack_units(packed):
    rows = packed.shape[0]
    units = []
    for unit in range(rows * TILE // (BLOCK * UNIT)):
        pieces = [
            packed[row : row + 16, lane : lane + UNIT]
            for row, lane in unit_rows(unit, rows)
        ]
        units.append(jnp.concatenate(pieces, axis=0))
    return jnp.concatenate(units, axis=1)


def pack_kernel(panel_ref, out_ref):
    packed = pack_units(
        [
            panel_ref[:, UNIT * unit : UNIT * unit + UNIT]
            for unit in range(panel_ref.shape[1] // UNIT)
        ]
    )
    for k in range(out_ref.shape[0]):
        out_ref[k] = packed


def start_kernel(
    far_table_ref, tiles_ref, got_ref, scale_ref, panel_ref, sent_ref,
    parts_ref, sums_ref, near_tiles_ref, sem, table_ref, table_sem, *, cb, units,
):
    copy = pltpu.make_async_copy(tiles_ref, near_tiles_ref, sem)
    copy.start()
    table_copy = pltpu.make_async_copy(far_table_ref, table_ref, table_sem)
    table_copy.start()
    rows = got_ref.shape[1]
    for b in range(cb):
        found = []
        for c in range(TILE // UNIT):
            device, unit = divmod(TILE // UNIT * b + c, units)
            found.append(
                [
                    got_ref[device, row : row + 16, lane : lane + UNIT]
                    for row, lane in unit_rows(unit, rows)
                ]
            )
        for piece in range(BLOCK // 16):
            panel_ref[64 * b + 16 * piece : 64 * b + 16 * piece + 16, :] = (
                jnp.concatenate([pieces[piece] for pieces in found], axis=1)
            )
    send_panel(
        table_ref, near_tiles_ref, panel_ref, scale_ref, sent_ref, parts_ref, sums_ref,
        forward=True, cb=cb, ready=(copy, table_copy),
    )


def fold_kernel(got_ref, out_ref, *rest):
    rows = out_ref.shape[-2]
    total = got_ref[0, :rows, :]
    for k in range(1, got_ref.shape[0]):
        total += got_ref[k, :rows, :]
    for k in range(out_ref.shape[0]):
        out_ref[k] = total
    if rest:
        other = got_ref[0, rows:, :]
        for k in range(1, got_ref.shape[0]):
            other += got_ref[k, rows:, :]
        rest[0][...] = other


def sum_gram(got_ref):
    packed = got_ref[0, -GRAM_ROWS:, :]
    for k in range(1, got_ref.shape[0]):
        packed += got_ref[k, -GRAM_ROWS:, :]
    return unpack_gram(packed)


def join_gram(table_ref, own_ref, other_ref):
    first = table_ref[CORE_AT] == 0
    own, other = own_ref[...], other_ref[...]
    return unpack_gram(
        jnp.concatenate(
            [
                jnp.where(first, own, other),
                jnp.where(first, other, own)[: GRAM_ROWS - HALF_ROWS],
            ],
            axis=0,
        )
    )


def lower_factor(factor_ref):
    lower = jnp.transpose(factor_ref[:, :BLOCK])
    mask = lax.broadcasted_iota(
        jnp.int32, (BLOCK, BLOCK), 0
    ) >= lax.broadcasted_iota(jnp.int32, (BLOCK, BLOCK), 1)
    return jnp.where(mask, lower, 0.0)


def cut(ref, height, start, width):
    per_block = TILE // UNIT
    block = start // per_block
    after = jnp.minimum(block + 1, ref.shape[0] // height - 1)
    wide = jnp.concatenate(
        [
            ref[pl.ds(pl.multiple_of(height * b, height), height), :]
            for b in (block, after)
        ],
        axis=1,
    )
    own = wide[:, :width]
    for k in range(1, per_block):
        own = jnp.where(
            start - block * per_block == k, wide[:, UNIT * k : UNIT * k + width], own
        )
    return own


def factor_kernel(*refs, with_old, halves, owned=False):
    refs = list(refs)
    if owned:
        table_ref, items_ref, scale_ref = refs[3:6]
        own_items_ref, own_scale_ref = refs[-2:]
        width = own_items_ref.shape[1]
        start = (width // UNIT) * table_ref[ROW_AT]
        own_items_ref[...] = cut(items_ref, BLOCK, start, width)
        own_scale_ref[...] = cut(scale_ref, 1, start, width)
        refs = refs[:3] + refs[6:-2]
    if halves:
        gram, refs = join_gram(*refs[:3]), refs[3:]
    else:
        gram, refs = sum_gram(refs[0]), refs[1:]
    if not with_old:
        factor_rows(gram, refs[0])
        return
    old_ref, old_factor_ref, factor_ref, part_ref, lower_ref = refs
    factor_rows(gram, factor_ref)
    lower_ref[...] = lower_factor(factor_ref)
    back = backward_weights(factor_ref, old_factor_ref)
    for b in range(old_ref.shape[0] // BLOCK):
        part_ref[64 * b : 64 * b + 64, :] = jnp.dot(
            back, old_ref[64 * b : 64 * b + 64, :], precision=HIGH,
            preferred_element_type=jnp.float32,
        )


def backward_weights(factor_ref, old_factor_ref):
    upper_mask = lax.broadcasted_iota(
        jnp.int32, (BLOCK, BLOCK), 0
    ) <= lax.broadcasted_iota(jnp.int32, (BLOCK, BLOCK), 1)
    upper = jnp.where(upper_mask, factor_ref[:, :BLOCK], 0.0)
    return jnp.dot(
        upper, -old_factor_ref[:, BLOCK:], precision=HIGH,
        preferred_element_type=jnp.float32,
    )


def step_kernel(*refs, forward, cb, with_old, owned):
    refs = list(refs)
    far_table_ref, tiles_ref, got_ref, scale_ref, factor_ref = refs[:5]
    table_ref, table_sem = refs[-2:]
    refs = refs[5:-2]
    table_copy = pltpu.make_async_copy(far_table_ref, table_ref, table_sem)
    table_copy.start()
    if with_old:
        part_ref, refs = refs[0], refs[1:]
    if owned:
        sent_ref, own_ref, panel_ref = refs[:3]
    else:
        panel_ref, sent_ref = refs[:2]
    parts_ref, sums_ref = refs[-2:]
    inverse = split_three(factor_ref[:, BLOCK:])
    for b in range(panel_ref.shape[0] // BLOCK):
        where = slice(64 * b, 64 * b + 64)
        value = exact_dot(
            inverse, split_three(got_ref[where, :] * scale_ref[b : b + 1, :])
        )
        if with_old:
            value += part_ref[where, :]
        panel_ref[where, :] = value
    send_panel(
        table_ref, tiles_ref, panel_ref, scale_ref, sent_ref, parts_ref, sums_ref,
        forward=forward, cb=cb, owned=owned, ready=(table_copy,),
    )
    if owned:
        width = own_ref.shape[1]
        start = (width // UNIT) * table_ref[COL_AT]
        own_ref[...] = cut(panel_ref, BLOCK, start, width)


def last_kernel(got_ref, old_ref, old_factor_ref, scale_ref, factor_ref, panel_ref, sent_ref):
    rows = got_ref.shape[1] - GRAM_ROWS
    total = got_ref[0, :rows, :]
    for k in range(1, got_ref.shape[0]):
        total += got_ref[k, :rows, :]
    value = unpack_units(total) * scale_ref[...]
    factor_rows(sum_gram(got_ref), factor_ref)
    weights = jnp.concatenate(
        [factor_ref[:, BLOCK:], backward_weights(factor_ref, old_factor_ref)], axis=1
    )
    value = jnp.dot(
        weights, jnp.concatenate([value, old_ref[...]], axis=0), precision=HIGH,
        preferred_element_type=jnp.float32,
    )
    panel_ref[...] = value
    gram = lax.dot_general(
        value, value, (((1,), (1,)), ((), ())), precision=HIGH,
        preferred_element_type=jnp.float32,
    )
    packed = pack_gram(gram)
    for k in range(sent_ref.shape[0]):
        sent_ref[k] = packed


def end_kernel(
    got_ref, right_ref, left_ref, left_factor_ref, *refs, left_size, right_size
):
    lower_refs, refs = refs[:4], refs[4:]
    out_left_ref, out_right_ref, left_lower_ref, right_lower_ref, factor_ref = refs
    out_left_ref[...] = math.sqrt(left_size) * jnp.dot(
        left_factor_ref[:, BLOCK:], left_ref[...], precision=HIGH,
        preferred_element_type=jnp.float32,
    )
    left_lower_ref[0] = lower_refs[0][...]
    right_lower_ref[0] = lower_refs[1][...]
    left_lower_ref[1] = lower_refs[2][...]
    right_lower_ref[1] = lower_refs[3][...]
    left_lower_ref[2] = lower_factor(left_factor_ref)
    factor_rows(sum_gram(got_ref), factor_ref)
    right_lower_ref[2] = lower_factor(factor_ref)
    out_right_ref[...] = math.sqrt(right_size) * jnp.dot(
        factor_ref[:, BLOCK:], right_ref[...], precision=HIGH,
        preferred_element_type=jnp.float32,
    )


SMEM = pl.BlockSpec(memory_space=pltpu.SMEM)
VMEM = pl.BlockSpec(memory_space=pltpu.VMEM)
FAR = pl.BlockSpec(memory_space=pltpu.HBM)
PARAMS = pltpu.CompilerParams(vmem_limit_bytes=8 * 1024 * 1024)


def f32(*shape):
    return jax.ShapeDtypeStruct(shape, jnp.float32)


def fold(got, copies, rows, rest=False):
    shapes = [f32(copies, rows, TILE)]
    if rest:
        shapes.append(f32(got.shape[1] - rows, TILE))
    return pl.pallas_call(
        fold_kernel,
        out_shape=shapes,
        in_specs=[VMEM],
        out_specs=[VMEM] * len(shapes),
        compiler_params=PARAMS,
        name="fold",
    )(got)


def exchange(messages, axes):
    return lax.all_to_all(messages, axes, 0, 0, tiled=True)


def sum_col(sent):
    near = lax.axis_size(NEAR)
    own = fold(exchange(sent, NEAR), 1, sent.shape[1])[0][0]
    got = lax.all_gather(own, "zh", axis=0, tiled=False)
    rows = sent.shape[1] - GRAM_ROWS
    line = lax.axis_size("x")
    half = exchange(fold(got, line, rows)[0], "x").reshape(line * rows, TILE)
    return [got], lax.all_gather(half, "core", axis=0, tiled=True)


def sum_row(sent, table):
    count = lax.axis_size(ROW)
    rows = sent.shape[1] - HALF_ROWS
    copies, own = fold(exchange(sent, ROW), count, rows, rest=True)
    whole = exchange(copies, ROW).reshape(count * rows, TILE)
    other = lax.ppermute(own, "core", [(0, 1), (1, 0)])
    return [table, own, other], whole


def per_device(tiles, tile_slots, tile_counts, user_degree, item_degree, start_panel):
    tile_stack = tiles[0, 0]
    rb = user_degree.shape[0] // TILE
    cb = item_degree.shape[0] // TILE
    rows = lax.axis_size(ROW)
    near = lax.axis_size(NEAR)
    core = lax.axis_index("core").astype(jnp.int32).reshape(1)
    col = lax.axis_index(COL).astype(jnp.int32).reshape(1)
    row = lax.axis_index(ROW).astype(jnp.int32).reshape(1)
    table = jnp.concatenate([tile_counts[0], core, col, row, tile_slots[0, 0]])
    table = jnp.pad(table, (0, TABLE - table.shape[0]))
    user_scale = lax.rsqrt(user_degree.astype(jnp.float32)).reshape(rb, TILE)
    item_scale = lax.rsqrt(item_degree.astype(jnp.float32)).reshape(cb, TILE)

    units = start_panel.shape[1] // UNIT
    start = pl.pallas_call(
        pack_kernel,
        out_shape=f32(rows, BLOCK * units * UNIT // TILE, TILE),
        in_specs=[VMEM],
        out_specs=VMEM,
        compiler_params=PARAMS,
        name="pack",
    )(start_panel)
    start = exchange(start, ROW)

    user_messages = f32(near, rb * BLOCK // near + GRAM_ROWS, TILE)
    item_messages = f32(rows, cb * BLOCK // rows + HALF_ROWS, TILE)
    owned_messages = f32(rows, cb * BLOCK // rows + GRAM_ROWS, TILE)
    user_sums = pltpu.VMEM((rb * BLOCK + BLOCK, TILE), jnp.float32)
    item_sums = pltpu.VMEM((cb * BLOCK + BLOCK, TILE), jnp.float32)
    user_parts = pltpu.VMEM((rb * 192, TILE), jnp.bfloat16)
    item_parts = pltpu.VMEM((cb * 192, TILE), jnp.bfloat16)
    near_table = [pltpu.SMEM((TABLE,), jnp.int32), pltpu.SemaphoreType.DMA]
    start, sent = pl.pallas_call(
        functools.partial(start_kernel, cb=cb, units=units),
        out_shape=[f32(cb * BLOCK, TILE), user_messages],
        in_specs=[FAR, FAR, VMEM, VMEM],
        out_specs=[VMEM, VMEM],
        scratch_shapes=[
            item_parts,
            user_sums,
            pltpu.VMEM(tile_stack.shape, tile_stack.dtype),
            pltpu.SemaphoreType.DMA,
            *near_table,
        ],
        compiler_params=PARAMS,
        name="start",
    )(table, tile_stack, start, item_scale)

    item_group = cb * TILE // rows
    panels = [start]
    factors = []
    lower = []
    for half in range(1, 2 * STEPS):
        users = half % 2 == 1
        owned = half == 2 * STEPS - 1
        with_old = half > 1
        gram, whole = sum_col(sent) if users else sum_row(sent, table)
        panel_shape = f32((rb if users else cb) * BLOCK, TILE)
        old = [panels[half - 2], factors[half - 2]] if with_old else []
        shapes = [f32(BLOCK, 2 * BLOCK)]
        if with_old:
            shapes += [panel_shape, f32(BLOCK, BLOCK)]
        wanted = []
        if owned:
            wanted = [table, panels[-1], item_scale]
            shapes += [f32(BLOCK, item_group), f32(1, item_group)]
        factored = pl.pallas_call(
            functools.partial(
                factor_kernel, with_old=with_old, halves=not users, owned=owned
            ),
            out_shape=shapes,
            in_specs=([VMEM] if users else [SMEM, VMEM, VMEM])
            + [VMEM] * len(old)
            + ([SMEM, VMEM, VMEM] if owned else []),
            out_specs=[VMEM] * len(shapes),
            compiler_params=PARAMS,
            name=f"factor{half}",
        )(*gram, *old, *wanted)
        factors.append(factored[0])
        lower += factored[2:3]
        messages = user_messages
        if users:
            messages = owned_messages if owned else item_messages
        operands = [whole, user_scale if users else item_scale, *factored[:2]]
        scratch = [user_parts, item_sums] if users else [item_parts, user_sums]
        shapes = [panel_shape, messages]
        if owned:
            shapes = [messages, f32(BLOCK, rb * TILE // lax.axis_size(COL))]
            scratch = [pltpu.VMEM(panel_shape.shape, jnp.float32), *scratch]
        results = pl.pallas_call(
            functools.partial(
                step_kernel, forward=not users, cb=cb, with_old=with_old, owned=owned
            ),
            out_shape=shapes,
            in_specs=[FAR, VMEM] + [VMEM] * len(operands),
            out_specs=[VMEM, VMEM],
            scratch_shapes=[*scratch, *near_table],
            compiler_params=PARAMS,
            name=f"half{half}",
        )(table, tile_stack, *operands)
        if owned:
            sent, left = results
        else:
            panel, sent = results
            panels.append(panel)

    factor, right, sent = pl.pallas_call(
        last_kernel,
        out_shape=[
            f32(BLOCK, 2 * BLOCK),
            f32(BLOCK, item_group),
            f32(lax.axis_size(FLAT), GRAM_ROWS, TILE),
        ],
        in_specs=[VMEM] * 4,
        out_specs=[VMEM] * 3,
        compiler_params=PARAMS,
        name="last",
    )(exchange(sent, ROW), factored[3], factors[-1], factored[4])
    gram = exchange(
        fold(exchange(sent, FLAT), lax.axis_size(LINE), GRAM_ROWS)[0], LINE
    )
    return tuple(
        pl.pallas_call(
            functools.partial(
                end_kernel,
                left_size=rb * TILE * rows,
                right_size=cb * TILE * lax.axis_size(COL),
            ),
            out_shape=[
                f32(BLOCK, rb * TILE // lax.axis_size(COL)),
                f32(BLOCK, item_group),
                f32(STEPS, BLOCK, BLOCK),
                f32(STEPS, BLOCK, BLOCK),
            ],
            in_specs=[VMEM] * 8,
            out_specs=[VMEM] * 4,
            scratch_shapes=[pltpu.VMEM((BLOCK, 2 * BLOCK), jnp.float32)],
            compiler_params=PARAMS,
            name="end",
        )(gram, right, left, factor, *lower)
    )


def solution(mesh):
    split = Mesh(mesh.devices.reshape(4, 4, 4, 4, 2), ROW + COL)
    in_specs = (
        P(ROW, COL, None, None, None),
        P(ROW, COL, None),
        P(ROW, COL),
        P(ROW),
        P(COL),
        P(None, COL + ROW),
    )
    out_specs = (P(None, ROW + COL), P(None, COL + ROW), P(), P())
    return jax.shard_map(
        per_device, mesh=split, in_specs=in_specs, out_specs=out_specs, check_vma=False
    )
```

```python
import functools
import math

import jax
import jax.numpy as jnp
from jax import lax
from jax.experimental import pallas as pl
from jax.experimental.pallas import tpu as pltpu
from jax.sharding import Mesh
from jax.sharding import PartitionSpec as P

STEPS = 3
TILE = 128
BLOCK = 64
GRAM_ROWS = 24
HALF_ROWS = 16
UNIT = 32
COUNT_AT, CORE_AT, COL_AT, ROW_AT, SLOTS_AT = range(5)
TABLE = 128
HIGH = lax.Precision.HIGHEST

ROW = ("zl", "y")
COL = ("x", "zh", "core")
NEAR = ("core", "x")
FLAT = ("core", "y", "x")
LINE = ("zh", "zl")


def flat_rows(block):
    return jnp.concatenate([block[8 * i : 8 * i + 8] for i in range(4)], axis=1)


def square_block(rows):
    half = BLOCK // 2
    return jnp.concatenate(
        [rows[:, half * i : half * i + half] for i in range(4)], axis=0
    )


def symmetric(upper, lower, cross):
    return jnp.concatenate(
        [
            jnp.concatenate([upper, jnp.transpose(cross)], axis=1),
            jnp.concatenate([cross, lower], axis=1),
        ],
        axis=0,
    )


def pack_gram(gram):
    half = BLOCK // 2
    blocks = gram[:half, :half], gram[half:, half:], gram[half:, :half]
    return jnp.concatenate([flat_rows(block) for block in blocks], axis=0)


def unpack_gram(packed):
    return symmetric(*(square_block(packed[8 * i : 8 * i + 8]) for i in range(3)))


def factor_rows(gram, out_ref):
    eye = (
        lax.broadcasted_iota(jnp.int32, (BLOCK, BLOCK), 0)
        == lax.broadcasted_iota(jnp.int32, (BLOCK, BLOCK), 1)
    ).astype(jnp.float32)
    whole = jnp.concatenate([gram, eye], axis=1)
    groups = [whole[8 * i : 8 * i + 8] for i in range(BLOCK // 8)]
    for first in range(BLOCK // 8):
        base = 8 * first
        below = range(first, BLOCK // 8)
        spread = {
            i: [
                jnp.broadcast_to(groups[i][:, base + m : base + m + 1], groups[i].shape)
                for m in range(8)
            ]
            for i in below
        }
        for k in range(8):
            root = lax.rsqrt(spread[first][k][k : k + 1])
            scaled = groups[first][k : k + 1] * root
            out_ref[base + k : base + k + 1, :] = scaled
            across = {m: spread[first][m][k : k + 1] * root for m in range(k + 1, 8)}
            for i in below:
                times = spread[i][k] * root
                groups[i] = groups[i] - times * scaled
                for m in across:
                    spread[i][m] = spread[i][m] - times * across[m]


def split_three(value):
    high = value.astype(jnp.bfloat16)
    rest = value - high.astype(jnp.float32)
    middle = rest.astype(jnp.bfloat16)
    low = (rest - middle.astype(jnp.float32)).astype(jnp.bfloat16)
    return high, middle, low


def exact_dot(left, right):
    high, middle, low = left
    first = jnp.concatenate([high, high, middle, high, middle, low], axis=1)
    high, middle, low = right
    second = jnp.concatenate([high, middle, high, low, middle, high], axis=0)
    return jnp.dot(first, second, preferred_element_type=jnp.float32)


def product(table_ref, tiles_ref, parts_ref, sums_ref, forward, cb):
    count = table_ref[COUNT_AT]
    spare = sums_ref.shape[0] // BLOCK - 1
    group = 16

    def visit(step, carry):
        added = []
        for g in range(group):
            t = step * group + g
            slot = table_ref[SLOTS_AT + t]
            local_row = slot // cb
            local_col = slot - local_row * cb
            source, target = (
                (local_col, local_row) if forward else (local_row, local_col)
            )
            tile = tiles_ref[t]
            target = jnp.where(t < count, target, spare)
            parts = parts_ref[pl.ds(pl.multiple_of(source * 192, 64), 192), :]
            dims = (((1,), (1 if forward else 0,)), ((), ()))
            value = lax.dot_general(
                parts, tile, dims, preferred_element_type=jnp.float32
            )
            added.append((target, value[:64] + value[64:128] + value[128:]))
        for target, value in added:
            where = pl.ds(pl.multiple_of(target * 64, 64), 64)
            sums_ref[where, :] += value
        return carry

    lax.fori_loop(0, (count + group - 1) // group, visit, 0)


def add_gram(gram, value):
    same, cross = gram
    high, middle, low = split_three(value)
    dims = (((1,), (1,)), ((), ()))
    same += lax.dot_general(
        jnp.concatenate([high, middle], axis=1), jnp.concatenate([high, middle], axis=1), dims,
        preferred_element_type=jnp.float32,
    )
    cross += lax.dot_general(
        jnp.concatenate([high, high], axis=1), jnp.concatenate([middle, low], axis=1), dims,
        preferred_element_type=jnp.float32,
    )
    return same, cross


def no_gram():
    return (jnp.zeros((BLOCK, BLOCK), jnp.float32),) * 2


def whole_gram(gram):
    same, cross = gram
    return same + cross + jnp.transpose(cross)


def send_panel(
    table_ref, tiles_ref, panel_ref, scale_ref, sent_ref, parts_ref, sums_ref, *, forward, cb, ready=(),
    owned=False,
):
    sums_ref[...] = jnp.zeros_like(sums_ref)
    gram = no_gram()
    for b in range(panel_ref.shape[0] // BLOCK):
        value = panel_ref[64 * b : 64 * b + 64, :]
        gram = add_gram(gram, value)
        parts_ref[192 * b : 192 * b + 192, :] = jnp.concatenate(
            split_three(value * scale_ref[b : b + 1, :]), axis=0
        )
    for copy in ready:
        copy.wait()
    product(table_ref, tiles_ref, parts_ref, sums_ref, forward, cb)
    gram = whole_gram(gram)
    if owned:
        send_owned(sums_ref, gram, sent_ref)
        return
    packed = pack_gram(gram)
    if not forward:
        cross = packed[HALF_ROWS:]
        packed = jnp.where(
            table_ref[CORE_AT] == 0, packed[:HALF_ROWS], jnp.concatenate([cross, cross], axis=0)
        )
    count = sent_ref.shape[0]
    rows = (sums_ref.shape[0] - BLOCK) // count
    for k in range(count):
        sent_ref[k, :rows, :] = sums_ref[rows * k : rows * k + rows, :]
        sent_ref[k, rows:, :] = packed


def send_owned(sums_ref, gram, sent_ref):
    half = BLOCK // 2
    side = jnp.concatenate([gram[:half, :half], gram[half:, half:]], axis=0)
    cross = flat_rows(gram[half:, :half])
    width = TILE - half
    for k in range(sent_ref.shape[0]):
        pieces, at = [], width * k
        while at < width * k + width:
            block, lane = divmod(at, TILE)
            lanes = min(TILE - lane, width * k + width - at)
            pieces.append(
                sums_ref[BLOCK * block : BLOCK * block + BLOCK, lane : lane + lanes]
            )
            at += lanes
        sent_ref[k, :BLOCK, :] = jnp.concatenate([*pieces, side], axis=1)
        sent_ref[k, BLOCK:, :] = cross


def unit_rows(unit, rows):
    for piece in range(BLOCK // 16):
        at = BLOCK * unit + 16 * piece
        yield at % rows, UNIT * (at // rows)


def pack_units(units):
    rows = len(units) * BLOCK * UNIT // TILE
    columns = [[] for _ in range(TILE // UNIT)]
    for unit, value in enumerate(units):
        for piece, (_, lane) in enumerate(unit_rows(unit, rows)):
            columns[lane // UNIT].append(value[16 * piece : 16 * piece + 16])
    return jnp.concatenate(
        [jnp.concatenate(pieces, axis=0) for pieces in columns], axis=1
    )


def pack_kernel(panel_ref, out_ref):
    packed = pack_units(
        [
            panel_ref[:, UNIT * unit : UNIT * unit + UNIT]
            for unit in range(panel_ref.shape[1] // UNIT)
        ]
    )
    for k in range(out_ref.shape[0]):
        out_ref[k] = packed


def start_kernel(
    far_table_ref, tiles_ref, got_ref, scale_ref, panel_ref, sent_ref,
    parts_ref, sums_ref, near_tiles_ref, sem, table_ref, table_sem, *, cb, units,
):
    copy = pltpu.make_async_copy(tiles_ref, near_tiles_ref, sem)
    copy.start()
    table_copy = pltpu.make_async_copy(far_table_ref, table_ref, table_sem)
    table_copy.start()
    rows = got_ref.shape[1]
    for b in range(cb):
        found = []
        for c in range(TILE // UNIT):
            device, unit = divmod(TILE // UNIT * b + c, units)
            found.append(
                [
                    got_ref[device, row : row + 16, lane : lane + UNIT]
                    for row, lane in unit_rows(unit, rows)
                ]
            )
        for piece in range(BLOCK // 16):
            panel_ref[64 * b + 16 * piece : 64 * b + 16 * piece + 16, :] = (
                jnp.concatenate([pieces[piece] for pieces in found], axis=1)
            )
    send_panel(
        table_ref, near_tiles_ref, panel_ref, scale_ref, sent_ref, parts_ref, sums_ref,
        forward=True, cb=cb, ready=(copy, table_copy),
    )


def fold_kernel(got_ref, out_ref, *rest):
    rows = out_ref.shape[-2]
    total = got_ref[0, :rows, :]
    for k in range(1, got_ref.shape[0]):
        total += got_ref[k, :rows, :]
    for k in range(out_ref.shape[0]):
        out_ref[k] = total
    if rest:
        other = got_ref[0, rows:, :]
        for k in range(1, got_ref.shape[0]):
            other += got_ref[k, rows:, :]
        rest[0][...] = other


def sum_gram(got_ref):
    packed = got_ref[0, -GRAM_ROWS:, :]
    for k in range(1, got_ref.shape[0]):
        packed += got_ref[k, -GRAM_ROWS:, :]
    return unpack_gram(packed)


def join_gram(table_ref, own_ref, other_ref):
    first = table_ref[CORE_AT] == 0
    own, other = own_ref[...], other_ref[...]
    return unpack_gram(
        jnp.concatenate(
            [
                jnp.where(first, own, other),
                jnp.where(first, other, own)[: GRAM_ROWS - HALF_ROWS],
            ],
            axis=0,
        )
    )


def lower_factor(factor_ref):
    lower = jnp.transpose(factor_ref[:, :BLOCK])
    mask = lax.broadcasted_iota(
        jnp.int32, (BLOCK, BLOCK), 0
    ) >= lax.broadcasted_iota(jnp.int32, (BLOCK, BLOCK), 1)
    return jnp.where(mask, lower, 0.0)


def cut(ref, height, start, width):
    per_block = TILE // UNIT
    block = start // per_block
    after = jnp.minimum(block + 1, ref.shape[0] // height - 1)
    wide = jnp.concatenate(
        [
            ref[pl.ds(pl.multiple_of(height * b, height), height), :]
            for b in (block, after)
        ],
        axis=1,
    )
    own = wide[:, :width]
    for k in range(1, per_block):
        own = jnp.where(
            start - block * per_block == k, wide[:, UNIT * k : UNIT * k + width], own
        )
    return own


def factor_kernel(*refs, with_old, halves, owned=False):
    refs = list(refs)
    if owned:
        table_ref, items_ref, scale_ref = refs[3:6]
        own_items_ref, own_scale_ref = refs[-2:]
        width = own_items_ref.shape[1]
        start = (width // UNIT) * table_ref[ROW_AT]
        own_items_ref[...] = cut(items_ref, BLOCK, start, width)
        own_scale_ref[...] = cut(scale_ref, 1, start, width)
        refs = refs[:3] + refs[6:-2]
    if halves:
        gram, refs = join_gram(*refs[:3]), refs[3:]
    else:
        gram, refs = sum_gram(refs[0]), refs[1:]
    if not with_old:
        factor_rows(gram, refs[0])
        return
    old_ref, old_factor_ref, factor_ref, part_ref, lower_ref = refs
    factor_rows(gram, factor_ref)
    lower_ref[...] = lower_factor(factor_ref)
    back = backward_weights(factor_ref, old_factor_ref)
    for b in range(old_ref.shape[0] // BLOCK):
        part_ref[64 * b : 64 * b + 64, :] = jnp.dot(
            back, old_ref[64 * b : 64 * b + 64, :], precision=HIGH,
            preferred_element_type=jnp.float32,
        )


def backward_weights(factor_ref, old_factor_ref):
    upper_mask = lax.broadcasted_iota(
        jnp.int32, (BLOCK, BLOCK), 0
    ) <= lax.broadcasted_iota(jnp.int32, (BLOCK, BLOCK), 1)
    upper = jnp.where(upper_mask, factor_ref[:, :BLOCK], 0.0)
    return jnp.dot(
        upper, -old_factor_ref[:, BLOCK:], precision=HIGH,
        preferred_element_type=jnp.float32,
    )


def step_kernel(*refs, forward, cb, with_old, owned):
    refs = list(refs)
    far_table_ref, tiles_ref, got_ref, scale_ref, factor_ref = refs[:5]
    table_ref, table_sem = refs[-2:]
    refs = refs[5:-2]
    table_copy = pltpu.make_async_copy(far_table_ref, table_ref, table_sem)
    table_copy.start()
    if with_old:
        part_ref, refs = refs[0], refs[1:]
    if owned:
        sent_ref, own_ref, panel_ref = refs[:3]
    else:
        panel_ref, sent_ref = refs[:2]
    parts_ref, sums_ref = refs[-2:]
    inverse = split_three(factor_ref[:, BLOCK:])
    for b in range(panel_ref.shape[0] // BLOCK):
        where = slice(64 * b, 64 * b + 64)
        value = exact_dot(
            inverse, split_three(got_ref[where, :] * scale_ref[b : b + 1, :])
        )
        if with_old:
            value += part_ref[where, :]
        panel_ref[where, :] = value
    send_panel(
        table_ref, tiles_ref, panel_ref, scale_ref, sent_ref, parts_ref, sums_ref,
        forward=forward, cb=cb, owned=owned, ready=(table_copy,),
    )
    if owned:
        width = own_ref.shape[1]
        start = (width // UNIT) * table_ref[COL_AT]
        own_ref[...] = cut(panel_ref, BLOCK, start, width)


def last_kernel(got_ref, old_ref, old_factor_ref, scale_ref, factor_ref, panel_ref, sent_ref):
    total = got_ref[0]
    for k in range(1, got_ref.shape[0]):
        total += got_ref[k]
    half = BLOCK // 2
    width = TILE - half
    value = total[:BLOCK, :width] * scale_ref[...]
    gram = symmetric(
        total[:half, width:], total[half:BLOCK, width:], square_block(total[BLOCK:])
    )
    factor_rows(gram, factor_ref)
    weights = jnp.concatenate(
        [factor_ref[:, BLOCK:], backward_weights(factor_ref, old_factor_ref)], axis=1
    )
    value = jnp.dot(
        weights, jnp.concatenate([value, old_ref[...]], axis=0), precision=HIGH,
        preferred_element_type=jnp.float32,
    )
    panel_ref[...] = value
    gram = lax.dot_general(
        value, value, (((1,), (1,)), ((), ())), precision=HIGH,
        preferred_element_type=jnp.float32,
    )
    packed = pack_gram(gram)
    for k in range(sent_ref.shape[0]):
        sent_ref[k] = packed


def end_kernel(
    got_ref, right_ref, left_ref, left_factor_ref, *refs, left_size, right_size
):
    lower_refs, refs = refs[:4], refs[4:]
    out_left_ref, out_right_ref, left_lower_ref, right_lower_ref, factor_ref = refs
    out_left_ref[...] = math.sqrt(left_size) * jnp.dot(
        left_factor_ref[:, BLOCK:], left_ref[...], precision=HIGH,
        preferred_element_type=jnp.float32,
    )
    left_lower_ref[0] = lower_refs[0][...]
    right_lower_ref[0] = lower_refs[1][...]
    left_lower_ref[1] = lower_refs[2][...]
    right_lower_ref[1] = lower_refs[3][...]
    left_lower_ref[2] = lower_factor(left_factor_ref)
    factor_rows(sum_gram(got_ref), factor_ref)
    right_lower_ref[2] = lower_factor(factor_ref)
    out_right_ref[...] = math.sqrt(right_size) * jnp.dot(
        factor_ref[:, BLOCK:], right_ref[...], precision=HIGH,
        preferred_element_type=jnp.float32,
    )


SMEM = pl.BlockSpec(memory_space=pltpu.SMEM)
VMEM = pl.BlockSpec(memory_space=pltpu.VMEM)
FAR = pl.BlockSpec(memory_space=pltpu.HBM)
PARAMS = pltpu.CompilerParams(vmem_limit_bytes=8 * 1024 * 1024)


def f32(*shape):
    return jax.ShapeDtypeStruct(shape, jnp.float32)


def fold(got, copies, rows, rest=False):
    shapes = [f32(copies, rows, TILE)]
    if rest:
        shapes.append(f32(got.shape[1] - rows, TILE))
    return pl.pallas_call(
        fold_kernel,
        out_shape=shapes,
        in_specs=[VMEM],
        out_specs=[VMEM] * len(shapes),
        compiler_params=PARAMS,
        name="fold",
    )(got)


def exchange(messages, axes):
    return lax.all_to_all(messages, axes, 0, 0, tiled=True)


def sum_col(sent):
    near = lax.axis_size(NEAR)
    own = fold(exchange(sent, NEAR), 1, sent.shape[1])[0][0]
    got = lax.all_gather(own, "zh", axis=0, tiled=False)
    rows = sent.shape[1] - GRAM_ROWS
    line = lax.axis_size("x")
    half = exchange(fold(got, line, rows)[0], "x").reshape(line * rows, TILE)
    return [got], lax.all_gather(half, "core", axis=0, tiled=True)


def sum_row(sent, table):
    count = lax.axis_size(ROW)
    rows = sent.shape[1] - HALF_ROWS
    copies, own = fold(exchange(sent, ROW), count, rows, rest=True)
    whole = exchange(copies, ROW).reshape(count * rows, TILE)
    other = lax.ppermute(own, "core", [(0, 1), (1, 0)])
    return [table, own, other], whole


def per_device(tiles, tile_slots, tile_counts, user_degree, item_degree, start_panel):
    tile_stack = tiles[0, 0]
    rb = user_degree.shape[0] // TILE
    cb = item_degree.shape[0] // TILE
    rows = lax.axis_size(ROW)
    near = lax.axis_size(NEAR)
    core = lax.axis_index("core").astype(jnp.int32).reshape(1)
    col = lax.axis_index(COL).astype(jnp.int32).reshape(1)
    row = lax.axis_index(ROW).astype(jnp.int32).reshape(1)
    table = jnp.concatenate([tile_counts[0], core, col, row, tile_slots[0, 0]])
    table = jnp.pad(table, (0, TABLE - table.shape[0]))
    user_scale = lax.rsqrt(user_degree.astype(jnp.float32)).reshape(rb, TILE)
    item_scale = lax.rsqrt(item_degree.astype(jnp.float32)).reshape(cb, TILE)

    units = start_panel.shape[1] // UNIT
    start = pl.pallas_call(
        pack_kernel,
        out_shape=f32(rows, BLOCK * units * UNIT // TILE, TILE),
        in_specs=[VMEM],
        out_specs=VMEM,
        compiler_params=PARAMS,
        name="pack",
    )(start_panel)
    start = exchange(start, ROW)

    user_messages = f32(near, rb * BLOCK // near + GRAM_ROWS, TILE)
    item_messages = f32(rows, cb * BLOCK // rows + HALF_ROWS, TILE)
    owned_messages = f32(rows, BLOCK + GRAM_ROWS - HALF_ROWS, TILE)
    user_sums = pltpu.VMEM((rb * BLOCK + BLOCK, TILE), jnp.float32)
    item_sums = pltpu.VMEM((cb * BLOCK + BLOCK, TILE), jnp.float32)
    user_parts = pltpu.VMEM((rb * 192, TILE), jnp.bfloat16)
    item_parts = pltpu.VMEM((cb * 192, TILE), jnp.bfloat16)
    near_table = [pltpu.SMEM((TABLE,), jnp.int32), pltpu.SemaphoreType.DMA]
    start, sent = pl.pallas_call(
        functools.partial(start_kernel, cb=cb, units=units),
        out_shape=[f32(cb * BLOCK, TILE), user_messages],
        in_specs=[FAR, FAR, VMEM, VMEM],
        out_specs=[VMEM, VMEM],
        scratch_shapes=[
            item_parts,
            user_sums,
            pltpu.VMEM(tile_stack.shape, tile_stack.dtype),
            pltpu.SemaphoreType.DMA,
            *near_table,
        ],
        compiler_params=PARAMS,
        name="start",
    )(table, tile_stack, start, item_scale)

    item_group = cb * TILE // rows
    panels = [start]
    factors = []
    lower = []
    for half in range(1, 2 * STEPS):
        users = half % 2 == 1
        owned = half == 2 * STEPS - 1
        with_old = half > 1
        gram, whole = sum_col(sent) if users else sum_row(sent, table)
        panel_shape = f32((rb if users else cb) * BLOCK, TILE)
        old = [panels[half - 2], factors[half - 2]] if with_old else []
        shapes = [f32(BLOCK, 2 * BLOCK)]
        if with_old:
            shapes += [panel_shape, f32(BLOCK, BLOCK)]
        wanted = []
        if owned:
            wanted = [table, panels[-1], item_scale]
            shapes += [f32(BLOCK, item_group), f32(1, item_group)]
        factored = pl.pallas_call(
            functools.partial(
                factor_kernel, with_old=with_old, halves=not users, owned=owned
            ),
            out_shape=shapes,
            in_specs=([VMEM] if users else [SMEM, VMEM, VMEM])
            + [VMEM] * len(old)
            + ([SMEM, VMEM, VMEM] if owned else []),
            out_specs=[VMEM] * len(shapes),
            compiler_params=PARAMS,
            name=f"factor{half}",
        )(*gram, *old, *wanted)
        factors.append(factored[0])
        lower += factored[2:3]
        messages = user_messages
        if users:
            messages = owned_messages if owned else item_messages
        operands = [whole, user_scale if users else item_scale, *factored[:2]]
        scratch = [user_parts, item_sums] if users else [item_parts, user_sums]
        shapes = [panel_shape, messages]
        if owned:
            shapes = [messages, f32(BLOCK, rb * TILE // lax.axis_size(COL))]
            scratch = [pltpu.VMEM(panel_shape.shape, jnp.float32), *scratch]
        results = pl.pallas_call(
            functools.partial(
                step_kernel, forward=not users, cb=cb, with_old=with_old, owned=owned
            ),
            out_shape=shapes,
            in_specs=[FAR, VMEM] + [VMEM] * len(operands),
            out_specs=[VMEM, VMEM],
            scratch_shapes=[*scratch, *near_table],
            compiler_params=PARAMS,
            name=f"half{half}",
        )(table, tile_stack, *operands)
        if owned:
            sent, left = results
        else:
            panel, sent = results
            panels.append(panel)

    factor, right, sent = pl.pallas_call(
        last_kernel,
        out_shape=[
            f32(BLOCK, 2 * BLOCK),
            f32(BLOCK, item_group),
            f32(lax.axis_size(FLAT), GRAM_ROWS, TILE),
        ],
        in_specs=[VMEM] * 4,
        out_specs=[VMEM] * 3,
        compiler_params=PARAMS,
        name="last",
    )(exchange(sent, ROW), factored[3], factors[-1], factored[4])
    gram = exchange(
        fold(exchange(sent, FLAT), lax.axis_size(LINE), GRAM_ROWS)[0], LINE
    )
    return tuple(
        pl.pallas_call(
            functools.partial(
                end_kernel,
                left_size=rb * TILE * rows,
                right_size=cb * TILE * lax.axis_size(COL),
            ),
            out_shape=[
                f32(BLOCK, rb * TILE // lax.axis_size(COL)),
                f32(BLOCK, item_group),
                f32(STEPS, BLOCK, BLOCK),
                f32(STEPS, BLOCK, BLOCK),
            ],
            in_specs=[VMEM] * 8,
            out_specs=[VMEM] * 4,
            scratch_shapes=[pltpu.VMEM((BLOCK, 2 * BLOCK), jnp.float32)],
            compiler_params=PARAMS,
            name="end",
        )(gram, right, left, factor, *lower)
    )


def solution(mesh):
    split = Mesh(mesh.devices.reshape(4, 4, 4, 4, 2), ROW + COL)
    in_specs = (
        P(ROW, COL, None, None, None),
        P(ROW, COL, None),
        P(ROW, COL),
        P(ROW),
        P(COL),
        P(None, COL + ROW),
    )
    out_specs = (P(None, ROW + COL), P(None, COL + ROW), P(), P())
    return jax.shard_map(
        per_device, mesh=split, in_specs=in_specs, out_specs=out_specs, check_vma=False
    )
```

```python
import functools
import math

import jax
import jax.numpy as jnp
from jax import lax
from jax.experimental import pallas as pl
from jax.experimental.pallas import tpu as pltpu
from jax.sharding import Mesh
from jax.sharding import PartitionSpec as P

STEPS = 3
TILE = 128
BLOCK = 64
GRAM_ROWS = 24
HALF_ROWS = 16
UNIT = 32
COUNT_AT, CORE_AT, COL_AT, ROW_AT, SLOTS_AT = range(5)
TABLE = 128
HIGH = lax.Precision.HIGHEST

ROW = ("zl", "y")
COL = ("x", "zh", "core")
NEAR = ("core", "x")
FLAT = ("core", "y", "x")
LINE = ("zh", "zl")


def flat_rows(block):
    return jnp.concatenate([block[8 * i : 8 * i + 8] for i in range(4)], axis=1)


def square_block(rows):
    half = BLOCK // 2
    return jnp.concatenate(
        [rows[:, half * i : half * i + half] for i in range(4)], axis=0
    )


def symmetric(upper, lower, cross):
    return jnp.concatenate(
        [
            jnp.concatenate([upper, jnp.transpose(cross)], axis=1),
            jnp.concatenate([cross, lower], axis=1),
        ],
        axis=0,
    )


def pack_gram(gram):
    half = BLOCK // 2
    blocks = gram[:half, :half], gram[half:, half:], gram[half:, :half]
    return jnp.concatenate([flat_rows(block) for block in blocks], axis=0)


def unpack_gram(packed):
    return symmetric(*(square_block(packed[8 * i : 8 * i + 8]) for i in range(3)))


def factor_rows(gram, out_ref):
    eye = (
        lax.broadcasted_iota(jnp.int32, (BLOCK, BLOCK), 0)
        == lax.broadcasted_iota(jnp.int32, (BLOCK, BLOCK), 1)
    ).astype(jnp.float32)
    whole = jnp.concatenate([gram, eye], axis=1)
    groups = [whole[8 * i : 8 * i + 8] for i in range(BLOCK // 8)]
    for first in range(BLOCK // 8):
        base = 8 * first
        below = range(first, BLOCK // 8)
        spread = {
            i: [
                jnp.broadcast_to(groups[i][:, base + m : base + m + 1], groups[i].shape)
                for m in range(8)
            ]
            for i in below
        }
        for k in range(8):
            root = lax.rsqrt(spread[first][k][k : k + 1])
            scaled = groups[first][k : k + 1] * root
            out_ref[base + k : base + k + 1, :] = scaled
            across = {m: spread[first][m][k : k + 1] * root for m in range(k + 1, 8)}
            for i in below:
                times = spread[i][k] * root
                groups[i] = groups[i] - times * scaled
                for m in across:
                    spread[i][m] = spread[i][m] - times * across[m]


def split_three(value):
    high = value.astype(jnp.bfloat16)
    rest = value - high.astype(jnp.float32)
    middle = rest.astype(jnp.bfloat16)
    low = (rest - middle.astype(jnp.float32)).astype(jnp.bfloat16)
    return high, middle, low


def exact_dot(left, right):
    high, middle, low = left
    first = jnp.concatenate([high, high, middle, high, middle, low], axis=1)
    high, middle, low = right
    second = jnp.concatenate([high, middle, high, low, middle, high], axis=0)
    return jnp.dot(first, second, preferred_element_type=jnp.float32)


def product(table_ref, tiles_ref, parts_ref, sums_ref, forward, cb):
    count = table_ref[COUNT_AT]
    spare = sums_ref.shape[0] // BLOCK - 1
    group = 16

    def visit(step, carry):
        added = []
        for g in range(group):
            t = step * group + g
            slot = table_ref[SLOTS_AT + t]
            local_row = slot // cb
            local_col = slot - local_row * cb
            source, target = (
                (local_col, local_row) if forward else (local_row, local_col)
            )
            tile = tiles_ref[t]
            target = jnp.where(t < count, target, spare)
            parts = parts_ref[pl.ds(pl.multiple_of(source * 192, 64), 192), :]
            dims = (((1,), (1 if forward else 0,)), ((), ()))
            value = lax.dot_general(
                parts, tile, dims, preferred_element_type=jnp.float32
            )
            added.append((target, value[:64] + value[64:128] + value[128:]))
        for target, value in added:
            where = pl.ds(pl.multiple_of(target * 64, 64), 64)
            sums_ref[where, :] += value
        return carry

    lax.fori_loop(0, (count + group - 1) // group, visit, 0)


def add_gram(gram, value):
    same, cross = gram
    high, middle, low = split_three(value)
    dims = (((1,), (1,)), ((), ()))
    same += lax.dot_general(
        jnp.concatenate([high, middle], axis=1), jnp.concatenate([high, middle], axis=1), dims,
        preferred_element_type=jnp.float32,
    )
    cross += lax.dot_general(
        jnp.concatenate([high, high], axis=1), jnp.concatenate([middle, low], axis=1), dims,
        preferred_element_type=jnp.float32,
    )
    return same, cross


def no_gram():
    return (jnp.zeros((BLOCK, BLOCK), jnp.float32),) * 2


def whole_gram(gram):
    same, cross = gram
    return same + cross + jnp.transpose(cross)


def send_panel(
    table_ref, tiles_ref, panel_ref, scale_ref, sent_ref, parts_ref, sums_ref, *, forward, cb, ready=(),
    owned=False,
):
    sums_ref[...] = jnp.zeros_like(sums_ref)
    gram = no_gram()
    for b in range(panel_ref.shape[0] // BLOCK):
        value = panel_ref[64 * b : 64 * b + 64, :]
        gram = add_gram(gram, value)
        parts_ref[192 * b : 192 * b + 192, :] = jnp.concatenate(
            split_three(value * scale_ref[b : b + 1, :]), axis=0
        )
    for copy in ready:
        copy.wait()
    product(table_ref, tiles_ref, parts_ref, sums_ref, forward, cb)
    gram = whole_gram(gram)
    if owned:
        send_owned(sums_ref, gram, sent_ref)
        return
    packed = pack_gram(gram)
    if not forward:
        cross = packed[HALF_ROWS:]
        packed = jnp.where(
            table_ref[CORE_AT] == 0, packed[:HALF_ROWS], jnp.concatenate([cross, cross], axis=0)
        )
    count = sent_ref.shape[0]
    rows = (sums_ref.shape[0] - BLOCK) // count
    for k in range(count):
        sent_ref[k, :rows, :] = sums_ref[rows * k : rows * k + rows, :]
        sent_ref[k, rows:, :] = packed


def send_owned(sums_ref, gram, sent_ref):
    half = BLOCK // 2
    side = jnp.concatenate([gram[:half, :half], gram[half:, half:]], axis=0)
    cross = flat_rows(gram[half:, :half])
    width = TILE - half
    for k in range(sent_ref.shape[0]):
        pieces, at = [], width * k
        while at < width * k + width:
            block, lane = divmod(at, TILE)
            lanes = min(TILE - lane, width * k + width - at)
            pieces.append(
                sums_ref[BLOCK * block : BLOCK * block + BLOCK, lane : lane + lanes]
            )
            at += lanes
        sent_ref[k, :BLOCK, :] = jnp.concatenate([*pieces, side], axis=1)
        sent_ref[k, BLOCK:, :] = cross


def unit_rows(unit, rows):
    for piece in range(BLOCK // 16):
        at = BLOCK * unit + 16 * piece
        yield at % rows, UNIT * (at // rows)


def pack_units(units):
    rows = len(units) * BLOCK * UNIT // TILE
    columns = [[] for _ in range(TILE // UNIT)]
    for unit, value in enumerate(units):
        for piece, (_, lane) in enumerate(unit_rows(unit, rows)):
            columns[lane // UNIT].append(value[16 * piece : 16 * piece + 16])
    return jnp.concatenate(
        [jnp.concatenate(pieces, axis=0) for pieces in columns], axis=1
    )


def pack_kernel(panel_ref, out_ref):
    packed = pack_units(
        [
            panel_ref[:, UNIT * unit : UNIT * unit + UNIT]
            for unit in range(panel_ref.shape[1] // UNIT)
        ]
    )
    for k in range(out_ref.shape[0]):
        out_ref[k] = packed


def start_kernel(
    far_table_ref, tiles_ref, got_ref, scale_ref, panel_ref, sent_ref,
    parts_ref, sums_ref, near_tiles_ref, sem, table_ref, table_sem, *, cb, units,
):
    copy = pltpu.make_async_copy(tiles_ref, near_tiles_ref, sem)
    copy.start()
    table_copy = pltpu.make_async_copy(far_table_ref, table_ref, table_sem)
    table_copy.start()
    rows = got_ref.shape[1]
    for b in range(cb):
        found = []
        for c in range(TILE // UNIT):
            device, unit = divmod(TILE // UNIT * b + c, units)
            found.append(
                [
                    got_ref[device, row : row + 16, lane : lane + UNIT]
                    for row, lane in unit_rows(unit, rows)
                ]
            )
        for piece in range(BLOCK // 16):
            panel_ref[64 * b + 16 * piece : 64 * b + 16 * piece + 16, :] = (
                jnp.concatenate([pieces[piece] for pieces in found], axis=1)
            )
    send_panel(
        table_ref, near_tiles_ref, panel_ref, scale_ref, sent_ref, parts_ref, sums_ref,
        forward=True, cb=cb, ready=(copy, table_copy),
    )


def fold_kernel(got_ref, out_ref, *rest):
    rows = out_ref.shape[-2]
    total = got_ref[0, :rows, :]
    for k in range(1, got_ref.shape[0]):
        total += got_ref[k, :rows, :]
    for k in range(out_ref.shape[0]):
        out_ref[k] = total
    if rest:
        other = got_ref[0, rows:, :]
        for k in range(1, got_ref.shape[0]):
            other += got_ref[k, rows:, :]
        rest[0][...] = other


def sum_gram(got_ref):
    packed = got_ref[0, -GRAM_ROWS:, :]
    for k in range(1, got_ref.shape[0]):
        packed += got_ref[k, -GRAM_ROWS:, :]
    return unpack_gram(packed)


def join_gram(table_ref, own_ref, other_ref):
    first = table_ref[CORE_AT] == 0
    own, other = own_ref[...], other_ref[...]
    return unpack_gram(
        jnp.concatenate(
            [
                jnp.where(first, own, other),
                jnp.where(first, other, own)[: GRAM_ROWS - HALF_ROWS],
            ],
            axis=0,
        )
    )


def lower_factor(factor_ref):
    lower = jnp.transpose(factor_ref[:, :BLOCK])
    mask = lax.broadcasted_iota(
        jnp.int32, (BLOCK, BLOCK), 0
    ) >= lax.broadcasted_iota(jnp.int32, (BLOCK, BLOCK), 1)
    return jnp.where(mask, lower, 0.0)


def cut(ref, height, start, width):
    per_block = TILE // UNIT
    block = start // per_block
    after = jnp.minimum(block + 1, ref.shape[0] // height - 1)
    wide = jnp.concatenate(
        [
            ref[pl.ds(pl.multiple_of(height * b, height), height), :]
            for b in (block, after)
        ],
        axis=1,
    )
    own = wide[:, :width]
    for k in range(1, per_block):
        own = jnp.where(
            start - block * per_block == k, wide[:, UNIT * k : UNIT * k + width], own
        )
    return own


def factor_kernel(*refs, with_old, halves, owned=False):
    refs = list(refs)
    if owned:
        table_ref, items_ref, scale_ref = refs[3:6]
        own_items_ref, own_scale_ref = refs[-2:]
        width = own_items_ref.shape[1]
        start = (width // UNIT) * table_ref[ROW_AT]
        own_items_ref[...] = cut(items_ref, BLOCK, start, width)
        own_scale_ref[...] = cut(scale_ref, 1, start, width)
        refs = refs[:3] + refs[6:-2]
    if halves:
        gram, refs = join_gram(*refs[:3]), refs[3:]
    else:
        gram, refs = sum_gram(refs[0]), refs[1:]
    if not with_old:
        factor_rows(gram, refs[0])
        return
    old_ref, old_factor_ref, factor_ref, part_ref, lower_ref = refs
    factor_rows(gram, factor_ref)
    lower_ref[...] = lower_factor(factor_ref)
    back = backward_weights(factor_ref, old_factor_ref)
    for b in range(old_ref.shape[0] // BLOCK):
        part_ref[64 * b : 64 * b + 64, :] = jnp.dot(
            back, old_ref[64 * b : 64 * b + 64, :], precision=HIGH,
            preferred_element_type=jnp.float32,
        )


def backward_weights(factor_ref, old_factor_ref):
    upper_mask = lax.broadcasted_iota(
        jnp.int32, (BLOCK, BLOCK), 0
    ) <= lax.broadcasted_iota(jnp.int32, (BLOCK, BLOCK), 1)
    upper = jnp.where(upper_mask, factor_ref[:, :BLOCK], 0.0)
    return jnp.dot(
        upper, -old_factor_ref[:, BLOCK:], precision=HIGH,
        preferred_element_type=jnp.float32,
    )


def step_kernel(*refs, forward, cb, with_old, owned):
    refs = list(refs)
    far_table_ref, tiles_ref, got_ref, scale_ref, factor_ref = refs[:5]
    table_ref, table_sem = refs[-2:]
    refs = refs[5:-2]
    table_copy = pltpu.make_async_copy(far_table_ref, table_ref, table_sem)
    table_copy.start()
    if with_old:
        part_ref, refs = refs[0], refs[1:]
    if owned:
        sent_ref, own_ref, panel_ref = refs[:3]
    else:
        panel_ref, sent_ref = refs[:2]
    parts_ref, sums_ref = refs[-2:]
    inverse = split_three(factor_ref[:, BLOCK:])
    for b in range(0, panel_ref.shape[0] // BLOCK, 2):
        wheres = [slice(64 * c, 64 * c + 64) for c in (b, b + 1)]
        pair = jnp.concatenate(
            [
                got_ref[where, :] * scale_ref[c : c + 1, :]
                for c, where in zip((b, b + 1), wheres)
            ],
            axis=1,
        )
        pair = exact_dot(inverse, split_three(pair))
        for i, where in enumerate(wheres):
            value = pair[:, TILE * i : TILE * i + TILE]
            if with_old:
                value += part_ref[where, :]
            panel_ref[where, :] = value
    send_panel(
        table_ref, tiles_ref, panel_ref, scale_ref, sent_ref, parts_ref, sums_ref,
        forward=forward, cb=cb, owned=owned, ready=(table_copy,),
    )
    if owned:
        width = own_ref.shape[1]
        start = (width // UNIT) * table_ref[COL_AT]
        own_ref[...] = cut(panel_ref, BLOCK, start, width)


def last_kernel(got_ref, old_ref, old_factor_ref, scale_ref, factor_ref, panel_ref, sent_ref):
    total = got_ref[0]
    for k in range(1, got_ref.shape[0]):
        total += got_ref[k]
    half = BLOCK // 2
    width = TILE - half
    value = total[:BLOCK, :width] * scale_ref[...]
    gram = symmetric(
        total[:half, width:], total[half:BLOCK, width:], square_block(total[BLOCK:])
    )
    factor_rows(gram, factor_ref)
    weights = jnp.concatenate(
        [factor_ref[:, BLOCK:], backward_weights(factor_ref, old_factor_ref)], axis=1
    )
    value = jnp.dot(
        weights, jnp.concatenate([value, old_ref[...]], axis=0), precision=HIGH,
        preferred_element_type=jnp.float32,
    )
    panel_ref[...] = value
    gram = lax.dot_general(
        value, value, (((1,), (1,)), ((), ())), precision=HIGH,
        preferred_element_type=jnp.float32,
    )
    packed = pack_gram(gram)
    for k in range(sent_ref.shape[0]):
        sent_ref[k] = packed


def end_kernel(
    got_ref, right_ref, left_ref, left_factor_ref, *refs, left_size, right_size
):
    lower_refs, refs = refs[:4], refs[4:]
    out_left_ref, out_right_ref, left_lower_ref, right_lower_ref, factor_ref = refs
    out_left_ref[...] = math.sqrt(left_size) * jnp.dot(
        left_factor_ref[:, BLOCK:], left_ref[...], precision=HIGH,
        preferred_element_type=jnp.float32,
    )
    left_lower_ref[0] = lower_refs[0][...]
    right_lower_ref[0] = lower_refs[1][...]
    left_lower_ref[1] = lower_refs[2][...]
    right_lower_ref[1] = lower_refs[3][...]
    left_lower_ref[2] = lower_factor(left_factor_ref)
    factor_rows(sum_gram(got_ref), factor_ref)
    right_lower_ref[2] = lower_factor(factor_ref)
    out_right_ref[...] = math.sqrt(right_size) * jnp.dot(
        factor_ref[:, BLOCK:], right_ref[...], precision=HIGH,
        preferred_element_type=jnp.float32,
    )


SMEM = pl.BlockSpec(memory_space=pltpu.SMEM)
VMEM = pl.BlockSpec(memory_space=pltpu.VMEM)
FAR = pl.BlockSpec(memory_space=pltpu.HBM)
PARAMS = pltpu.CompilerParams(vmem_limit_bytes=8 * 1024 * 1024)


def f32(*shape):
    return jax.ShapeDtypeStruct(shape, jnp.float32)


def fold(got, copies, rows, rest=False):
    shapes = [f32(copies, rows, TILE)]
    if rest:
        shapes.append(f32(got.shape[1] - rows, TILE))
    return pl.pallas_call(
        fold_kernel,
        out_shape=shapes,
        in_specs=[VMEM],
        out_specs=[VMEM] * len(shapes),
        compiler_params=PARAMS,
        name="fold",
    )(got)


def exchange(messages, axes):
    return lax.all_to_all(messages, axes, 0, 0, tiled=True)


def sum_col(sent):
    near = lax.axis_size(NEAR)
    own = fold(exchange(sent, NEAR), 1, sent.shape[1])[0][0]
    got = lax.all_gather(own, "zh", axis=0, tiled=False)
    rows = sent.shape[1] - GRAM_ROWS
    line = lax.axis_size("x")
    half = exchange(fold(got, line, rows)[0], "x").reshape(line * rows, TILE)
    return [got], lax.all_gather(half, "core", axis=0, tiled=True)


def sum_row(sent, table):
    count = lax.axis_size(ROW)
    rows = sent.shape[1] - HALF_ROWS
    copies, own = fold(exchange(sent, ROW), count, rows, rest=True)
    whole = exchange(copies, ROW).reshape(count * rows, TILE)
    other = lax.ppermute(own, "core", [(0, 1), (1, 0)])
    return [table, own, other], whole


def per_device(tiles, tile_slots, tile_counts, user_degree, item_degree, start_panel):
    tile_stack = tiles[0, 0]
    rb = user_degree.shape[0] // TILE
    cb = item_degree.shape[0] // TILE
    rows = lax.axis_size(ROW)
    near = lax.axis_size(NEAR)
    core = lax.axis_index("core").astype(jnp.int32).reshape(1)
    col = lax.axis_index(COL).astype(jnp.int32).reshape(1)
    row = lax.axis_index(ROW).astype(jnp.int32).reshape(1)
    table = jnp.concatenate([tile_counts[0], core, col, row, tile_slots[0, 0]])
    table = jnp.pad(table, (0, TABLE - table.shape[0]))
    user_scale = lax.rsqrt(user_degree.astype(jnp.float32)).reshape(rb, TILE)
    item_scale = lax.rsqrt(item_degree.astype(jnp.float32)).reshape(cb, TILE)

    units = start_panel.shape[1] // UNIT
    start = pl.pallas_call(
        pack_kernel,
        out_shape=f32(rows, BLOCK * units * UNIT // TILE, TILE),
        in_specs=[VMEM],
        out_specs=VMEM,
        compiler_params=PARAMS,
        name="pack",
    )(start_panel)
    start = exchange(start, ROW)

    user_messages = f32(near, rb * BLOCK // near + GRAM_ROWS, TILE)
    item_messages = f32(rows, cb * BLOCK // rows + HALF_ROWS, TILE)
    owned_messages = f32(rows, BLOCK + GRAM_ROWS - HALF_ROWS, TILE)
    user_sums = pltpu.VMEM((rb * BLOCK + BLOCK, TILE), jnp.float32)
    item_sums = pltpu.VMEM((cb * BLOCK + BLOCK, TILE), jnp.float32)
    user_parts = pltpu.VMEM((rb * 192, TILE), jnp.bfloat16)
    item_parts = pltpu.VMEM((cb * 192, TILE), jnp.bfloat16)
    near_table = [pltpu.SMEM((TABLE,), jnp.int32), pltpu.SemaphoreType.DMA]
    start, sent = pl.pallas_call(
        functools.partial(start_kernel, cb=cb, units=units),
        out_shape=[f32(cb * BLOCK, TILE), user_messages],
        in_specs=[FAR, FAR, VMEM, VMEM],
        out_specs=[VMEM, VMEM],
        scratch_shapes=[
            item_parts,
            user_sums,
            pltpu.VMEM(tile_stack.shape, tile_stack.dtype),
            pltpu.SemaphoreType.DMA,
            *near_table,
        ],
        compiler_params=PARAMS,
        name="start",
    )(table, tile_stack, start, item_scale)

    item_group = cb * TILE // rows
    panels = [start]
    factors = []
    lower = []
    for half in range(1, 2 * STEPS):
        users = half % 2 == 1
        owned = half == 2 * STEPS - 1
        with_old = half > 1
        gram, whole = sum_col(sent) if users else sum_row(sent, table)
        panel_shape = f32((rb if users else cb) * BLOCK, TILE)
        old = [panels[half - 2], factors[half - 2]] if with_old else []
        shapes = [f32(BLOCK, 2 * BLOCK)]
        if with_old:
            shapes += [panel_shape, f32(BLOCK, BLOCK)]
        wanted = []
        if owned:
            wanted = [table, panels[-1], item_scale]
            shapes += [f32(BLOCK, item_group), f32(1, item_group)]
        factored = pl.pallas_call(
            functools.partial(
                factor_kernel, with_old=with_old, halves=not users, owned=owned
            ),
            out_shape=shapes,
            in_specs=([VMEM] if users else [SMEM, VMEM, VMEM])
            + [VMEM] * len(old)
            + ([SMEM, VMEM, VMEM] if owned else []),
            out_specs=[VMEM] * len(shapes),
            compiler_params=PARAMS,
            name=f"factor{half}",
        )(*gram, *old, *wanted)
        factors.append(factored[0])
        lower += factored[2:3]
        messages = user_messages
        if users:
            messages = owned_messages if owned else item_messages
        operands = [whole, user_scale if users else item_scale, *factored[:2]]
        scratch = [user_parts, item_sums] if users else [item_parts, user_sums]
        shapes = [panel_shape, messages]
        if owned:
            shapes = [messages, f32(BLOCK, rb * TILE // lax.axis_size(COL))]
            scratch = [pltpu.VMEM(panel_shape.shape, jnp.float32), *scratch]
        results = pl.pallas_call(
            functools.partial(
                step_kernel, forward=not users, cb=cb, with_old=with_old, owned=owned
            ),
            out_shape=shapes,
            in_specs=[FAR, VMEM] + [VMEM] * len(operands),
            out_specs=[VMEM, VMEM],
            scratch_shapes=[*scratch, *near_table],
            compiler_params=PARAMS,
            name=f"half{half}",
        )(table, tile_stack, *operands)
        if owned:
            sent, left = results
        else:
            panel, sent = results
            panels.append(panel)

    factor, right, sent = pl.pallas_call(
        last_kernel,
        out_shape=[
            f32(BLOCK, 2 * BLOCK),
            f32(BLOCK, item_group),
            f32(lax.axis_size(FLAT), GRAM_ROWS, TILE),
        ],
        in_specs=[VMEM] * 4,
        out_specs=[VMEM] * 3,
        compiler_params=PARAMS,
        name="last",
    )(exchange(sent, ROW), factored[3], factors[-1], factored[4])
    gram = exchange(
        fold(exchange(sent, FLAT), lax.axis_size(LINE), GRAM_ROWS)[0], LINE
    )
    return tuple(
        pl.pallas_call(
            functools.partial(
                end_kernel,
                left_size=rb * TILE * rows,
                right_size=cb * TILE * lax.axis_size(COL),
            ),
            out_shape=[
                f32(BLOCK, rb * TILE // lax.axis_size(COL)),
                f32(BLOCK, item_group),
                f32(STEPS, BLOCK, BLOCK),
                f32(STEPS, BLOCK, BLOCK),
            ],
            in_specs=[VMEM] * 8,
            out_specs=[VMEM] * 4,
            scratch_shapes=[pltpu.VMEM((BLOCK, 2 * BLOCK), jnp.float32)],
            compiler_params=PARAMS,
            name="end",
        )(gram, right, left, factor, *lower)
    )


def solution(mesh):
    split = Mesh(mesh.devices.reshape(4, 4, 4, 4, 2), ROW + COL)
    in_specs = (
        P(ROW, COL, None, None, None),
        P(ROW, COL, None),
        P(ROW, COL),
        P(ROW),
        P(COL),
        P(None, COL + ROW),
    )
    out_specs = (P(None, ROW + COL), P(None, COL + ROW), P(), P())
    return jax.shard_map(
        per_device, mesh=split, in_specs=in_specs, out_specs=out_specs, check_vma=False
    )
```
